32 devices in a mesh: mesh: 16 (over z, y, core), band: 2 (over x).
Axes of the slice: x: 2, y: 2, z: 4, core: 2. Of those that a mesh axis runs over, the one named last changes fastest.
Arguments:
- psi: bfloat16 [16, 286720], P('band', 'mesh'), may hold values from -9 to 9
- cell_nodes: int32 [216, 128], replicated, may hold values from 0 to 19711, as said below
- cell_scale: float32 [2048], P('mesh'), may hold values from 0.5 to 2
- cell_matrix: bfloat16 [216, 216], replicated, may hold values from -1 to 2
- node_potential: bfloat16 [286720], P('mesh'), may hold values from -1.5 to 0.5
- proj_values: bfloat16 [216, 8, 2048], P(None, None, 'mesh'), may hold values from -1 to 1
- entry_cell: int32 [2048], P('mesh'), may hold values from 0 to 127
- entry_atom: int32 [2048], P('mesh'), may hold values from -1 to 191, as said below
- coupling: float32 [1024, 8, 8], P('mesh'), may hold values from -3 to 3
Outputs:
- filtered: bfloat16 [16, 286720], P('band', 'mesh')
- correlation: float32 [16, 16], replicated
The draws below stay inside these ranges and needn't reach their ends.
Inputs may be any that keep to these rules, and one draw needn't show every extreme that they name: `cell_nodes`: node j = 36 a + 6 b + c of a cell is its local node (a, b, c) in the order the cell_matrix uses; cells that share a node give it the same number; values 17920 + i name node i of the next partition, and only nodes below 1792 of a partition are named so by the previous one. `entry_atom`: live entries of a partition come first, then -1 padding; the number of live entries differs between partitions.
All inputs are finite; a program needn't handle non-finite values.
Results may differ from the reference program's by a relative error of at most 0.0022.
Values may be sent and summed in bfloat16 or wider, within the bound.
A program may use at most 128 MiB of HBM per device.

```python
import math
import jax
import jax.numpy as jnp
from jax import lax

STATES = 16
NPROJ = 8
CROSS = 8
ATOMS = 64
ENTRIES = 128
FACEP = 1792
NODES = 17920
CELLS = 128
NODES_ALL = 286720
CELLS_ALL = 2048
ENTRIES_ALL = 2048
ATOMS_ALL = 1024
N_MESH = 16


def draw_psi(key, part):
    ramp = 0.5 * (1.0 + 2.0 * jnp.arange(NODES_ALL, dtype=jnp.float32) / NODES_ALL)
    values = jnp.clip(jax.random.normal(jax.random.fold_in(key, 13), (STATES, NODES_ALL), jnp.float32), -6.0, 6.0)
    return (values * ramp[None, :]).astype(jnp.bfloat16)


def draw_cell_matrix(key, part):
    noise_vals = jnp.clip(jax.random.normal(jax.random.fold_in(key, 22), (216, 216), jnp.float32) * 0.048, -0.2, 0.2)
    matrix = jnp.eye(216, dtype=jnp.float32) + noise_vals + noise_vals.T
    return matrix.astype(jnp.bfloat16)


def draw_cell_nodes(key, part):
    side = 5 * CROSS + 1
    cell_ids = jnp.arange(CELLS, dtype=jnp.int32)
    cell_x = cell_ids // (CROSS * CROSS)
    cell_y = cell_ids // CROSS % CROSS
    cell_z = cell_ids % CROSS
    local_ids = jnp.arange(216, dtype=jnp.int32)
    local_a = local_ids // 36
    local_b = local_ids // 6 % 6
    local_c = local_ids % 6
    layer = 5 * cell_x[None, :] + local_a[:, None]
    across = (5 * cell_y[None, :] + local_b[:, None]) * side + 5 * cell_z[None, :] + local_c[:, None]
    shuffled = 1 + jax.random.permutation(jax.random.fold_in(key, 31), FACEP - 2).astype(jnp.int32)
    position = jnp.concatenate([jnp.array([FACEP - 1, 0], jnp.int32), shuffled])
    base_table = layer * FACEP + position[across]
    order = jax.random.permutation(jax.random.fold_in(key, 32), CELLS).astype(jnp.int32)
    table = base_table[:, order]
    return table.astype(jnp.int32)


def draw_entry_atom(key, part):
    partitions = ENTRIES_ALL // ENTRIES
    live_count = jax.random.randint(jax.random.fold_in(key, 41), (partitions,), ENTRIES // 4, ENTRIES + 1)
    live_count = live_count.at[0].set(ENTRIES).at[partitions - 1].set(ENTRIES // 2)
    slot_vals = jax.random.randint(jax.random.fold_in(key, 42), (partitions, ENTRIES), 0, 3 * ATOMS)
    slot_vals = slot_vals.at[0, 0].set(3 * ATOMS - 1)
    places = jnp.arange(ENTRIES, dtype=jnp.int32)
    result = jnp.where(places[None, :] < live_count[:, None], slot_vals, -1)
    return result.reshape(ENTRIES_ALL).astype(jnp.int32)


def with_ends(entries, stream_key, low, top_value):
    spot = [jax.random.randint(jax.random.fold_in(stream_key, axis), (), 0, length) for axis, length in enumerate(entries.shape)]
    main_axis = entries.shape.index(max(entries.shape))
    beside = spot[:main_axis] + [(spot[main_axis] + 1) % entries.shape[main_axis]] + spot[main_axis + 1:]
    return entries.at[tuple(spot)].set(low).at[tuple(beside)].set(top_value)


def steps_of(stream_key, shape, pieces, least, largest):
    level = 1.0
    for axis_at, shards_of in pieces:
        draws = jax.random.uniform(jax.random.fold_in(jax.random.fold_in(stream_key, 6), axis_at), (shards_of,), jnp.float32, least / len(pieces), largest / len(pieces))
        level = level * jnp.repeat(jnp.exp(draws), shape[axis_at] // shards_of).reshape((-1,) + (1,) * (len(shape) - 1 - axis_at))
    return level


def bell_draw(key, dims, deviation, bound, split=(), held_as=jnp.bfloat16):
    entries = deviation * jax.random.normal(key, dims, jnp.float32)
    if split:
        entries = entries * steps_of(key, dims, split, -0.22, 0.18)
    return jnp.clip(entries, -bound, bound).astype(held_as)


def setup_inputs(seed: int = 0) -> dict:
    streams_of = jax.random.split(jax.random.key(seed), 10)
    return {
        "psi": draw_psi(jax.random.fold_in(streams_of[9], 71), 0),
        "cell_nodes": draw_cell_nodes(jax.random.fold_in(streams_of[9], 71), 0),
        "cell_scale": jnp.clip(jnp.exp(math.log(2.0) - 1.3862944 * jax.random.uniform(streams_of[2], (CELLS_ALL,), jnp.float32) ** steps_of(streams_of[2], (CELLS_ALL,), ((0, 16),), -0.2, 0.2)), 0.5, 2.0),
        "cell_matrix": draw_cell_matrix(jax.random.fold_in(streams_of[9], 71), 0),
        "node_potential": jnp.clip(-1.5 + 2.0 * jax.random.uniform(streams_of[4], (NODES_ALL,), jnp.float32) ** steps_of(streams_of[4], (NODES_ALL,), ((0, 16),), -0.2, 0.2), -1.5, 0.5).astype(jnp.bfloat16),
        "proj_values": bell_draw(streams_of[5], (216, NPROJ, ENTRIES_ALL), 0.15, 1.0, ((2, 16),)),
        "entry_cell": with_ends(jax.random.randint(streams_of[6], (ENTRIES_ALL,), 0, CELLS), jax.random.fold_in(streams_of[6], 1), 0, CELLS - 1).astype(jnp.int32),
        "entry_atom": draw_entry_atom(jax.random.fold_in(streams_of[9], 71), 0),
        "coupling": bell_draw(streams_of[8], (ATOMS_ALL, NPROJ, NPROJ), 0.5, 3.0, ((0, 16),), jnp.float32),
    }


CENTER = 0.5
HALFWIDTH = 2.5
HIGH = lax.Precision.HIGHEST


def one_hot(entry_slots):
    slot_ids = jnp.arange(3 * ATOMS, dtype=jnp.int32)
    return (entry_slots[:, None] == slot_ids[None, :]).astype(jnp.float32)


def finish(summed, field, potential, base_field, second):
    scaled = (summed + (potential.astype(jnp.float32) - CENTER) * field.astype(jnp.float32)) / HALFWIDTH
    if second:
        return (2.0 * scaled - base_field.astype(jnp.float32)).astype(jnp.bfloat16)
    return scaled.astype(jnp.bfloat16)


def reference(psi, cell_nodes, cell_scale, cell_matrix, node_potential, proj_values, entry_cell, entry_atom, coupling):
    partitions = N_MESH
    states = psi.shape[0]
    local_width = cell_nodes.shape[0]
    fields = psi.reshape(states, partitions, NODES).transpose(1, 0, 2)
    cell_list = cell_nodes
    scale_rows = cell_scale.reshape(partitions, CELLS)
    potentials = node_potential.reshape(partitions, NODES)
    projectors = proj_values.reshape(local_width, NPROJ, partitions, ENTRIES).transpose(2, 0, 1, 3)
    entry_cells = entry_cell.reshape(partitions, ENTRIES)
    entry_slots = entry_atom.reshape(partitions, ENTRIES)
    couplings = coupling.reshape(partitions, ATOMS, NPROJ, NPROJ)
    kernel = cell_matrix.astype(jnp.float32)

    def partial_terms(items):
        field, ghost, project, ecells, eslots = items
        extended = jnp.concatenate([field, ghost], axis=1)
        values = extended[:, cell_list[:, ecells]].astype(jnp.float32)
        partial_sum = jnp.einsum("jke,sje->esk", project.astype(jnp.float32), values, precision=HIGH)
        partial_sum = partial_sum.reshape(ENTRIES, states * NPROJ)
        grouped = jnp.dot(one_hot(eslots).T, partial_sum, precision=HIGH)
        return grouped.reshape(3, ATOMS, states * NPROJ)

    def make_assemble(second):
        def assemble(items):
            field, ghost, scales, project, ecells, eslots, beside_all, potential, base_field = items
            extended = jnp.concatenate([field, ghost], axis=1)
            cell_vals = extended[:, cell_list].astype(jnp.float32)
            cell_terms = jnp.einsum("ij,sjc->sic", kernel, cell_vals, precision=HIGH) * scales
            entry_terms = jnp.dot(one_hot(eslots), beside_all, precision=HIGH).reshape(ENTRIES, states, NPROJ)
            node_terms = jnp.einsum("jke,esk->sje", project.astype(jnp.float32), entry_terms, precision=HIGH)
            summed = jnp.zeros((states, NODES + FACEP), jnp.float32)
            summed = summed.at[:, cell_list].add(cell_terms)
            summed = summed.at[:, cell_list[:, ecells]].add(node_terms)
            tail = finish(summed[:, FACEP:NODES], field[:, FACEP:], potential[None, FACEP:], base_field[:, FACEP:], second)
            return tail, summed[:, :FACEP], summed[:, NODES:]
        return assemble

    def apply_filter(field_all, base_all, second):
        ghosts = jnp.roll(field_all[:, :, :FACEP], -1, axis=0)
        grouped = lax.map(partial_terms, (field_all, ghosts, projectors, entry_cells, entry_slots))
        coefficient = grouped[:, 1] + jnp.roll(grouped[:, 2], 1, axis=0) + jnp.roll(grouped[:, 0], -1, axis=0)
        coefficient = coefficient.reshape(partitions, ATOMS, states, NPROJ)
        atom_vals = jnp.einsum("pakl,pasl->pask", couplings, coefficient, precision=HIGH)
        atom_vals = atom_vals.reshape(partitions, ATOMS, states * NPROJ)
        beside_all = jnp.concatenate([jnp.roll(atom_vals, 1, axis=0), atom_vals, jnp.roll(atom_vals, -1, axis=0)], axis=1)
        tails, heads, backs = lax.map(make_assemble(second), (field_all, ghosts, scale_rows, projectors, entry_cells, entry_slots, beside_all, potentials, base_all))
        heads = heads + jnp.roll(backs, 1, axis=0)
        head_out = finish(heads, field_all[:, :, :FACEP], potentials[:, None, :FACEP], base_all[:, :, :FACEP], second)
        return jnp.concatenate([head_out, tails], axis=2)

    first_step = apply_filter(fields, fields, False)
    filtered = apply_filter(first_step, fields, True)

    def accumulate(running, block):
        return running + jnp.dot(block, block.T, preferred_element_type=jnp.float32), None

    correlation, unused = lax.scan(accumulate, jnp.zeros((states, states), jnp.float32), filtered)
    correlation = correlation / NODES_ALL
    filtered_out = filtered.transpose(1, 0, 2).reshape(states, partitions * NODES)
    return filtered_out, correlation
```

```python
import jax
import jax.numpy as jnp
from jax import lax
from jax.experimental import pallas as pl
from jax.experimental.pallas import tpu as pltpu
from jax.sharding import PartitionSpec as P

FACEP = 1792
CENTER = 0.5
HALFWIDTH = 2.5
HIGH = lax.Precision.HIGHEST
WIDE = 256
GROUP = 36
F32 = jnp.float32
BF16 = jnp.bfloat16


def fill_onehot(cn_ref, group, oh_ref):
    rows = cn_ref[group]
    hi = jnp.bitwise_and(rows, WIDE - 1)
    lanes = rows.shape[1]
    iota = lax.broadcasted_iota(jnp.int32, (WIDE, lanes), 0)
    for jj in range(GROUP):
        oh_ref[:, jj * lanes:(jj + 1) * lanes] = jnp.where(
            iota == hi[jj:jj + 1, :], 1.0, 0.0
        ).astype(BF16)
    return lax.shift_right_logical(rows, 8)


def gather_kernel(sched_ref, cn_ref, ext_ref, xs_ref, lhs_ref, oh_ref):
    states = ext_ref.shape[0]
    chunks = lhs_ref.shape[0] - 1
    layers = ext_ref.shape[1] // (chunks * WIDE)
    groups = cn_ref.shape[0]
    cells = cn_ref.shape[2]
    padded = lhs_ref.shape[1]
    slots = sched_ref.shape[0] // groups
    lhs_ref[...] = jnp.zeros_like(lhs_ref)
    for c in range(chunks):
        base = c * layers * WIDE
        parts = [
            ext_ref[:, base + l * WIDE:base + (l + 1) * WIDE].astype(F32) for l in range(layers)
        ]
        parts.append(jnp.zeros((padded - layers * states, WIDE), F32))
        lhs_ref[c] = jnp.concatenate(parts, axis=0).astype(BF16)
    xs_ref[...] = jnp.zeros_like(xs_ref)

    def group_body(g, carry):
        lo = fill_onehot(cn_ref, g, oh_ref)

        def pair_body(r, inner):
            first = sched_ref[g * slots + 2 * r]
            second = sched_ref[g * slots + 2 * r + 1]
            lhs = jnp.concatenate([lhs_ref[first], lhs_ref[second]], axis=0)
            out = jnp.dot(lhs, oh_ref[...], preferred_element_type=F32)
            for jj in range(GROUP):
                where = pl.ds(pl.multiple_of((g * GROUP + jj) * states, states), states)
                value = xs_ref[where, :]
                lanes = slice(jj * cells, (jj + 1) * cells)
                for half, chunk in enumerate((first, second)):
                    row = lo[jj:jj + 1, :] - chunk * layers
                    for l in range(layers):
                        at = half * padded + l * states
                        value = jnp.where(row == l, out[at:at + states, lanes], value)
                xs_ref[where, :] = value
            return inner

        pairs = lax.shift_right_logical(sched_ref[g * slots + slots - 1] + 1, 1)
        return lax.fori_loop(0, pairs, pair_body, carry)

    lax.fori_loop(0, groups, group_body, 0)


def scatter_kernel(sched_ref, cn_ref, ct_ref, coef_ref, coup_ref, proj_ref, ecell_ref,
                   eatom_ref, y_ref, oh_ref, ns_ref, v_ref, lhs_ref, acc_ref):
    chunks, rows_in_chunk, _ = acc_ref.shape
    chunks = chunks - 1
    groups = cn_ref.shape[0]
    cells = cn_ref.shape[2]
    width = groups * GROUP
    states = ct_ref.shape[0] // width
    layers = rows_in_chunk // (2 * states)
    nproj = proj_ref.shape[1]
    entries = ecell_ref.shape[1]
    atoms = coef_ref.shape[2]
    slot_ids = lax.broadcasted_iota(jnp.int32, (atoms, entries), 0)
    entry_terms = jnp.zeros((nproj * states, entries), F32)
    for g in range(3):
        rows = []
        for k in range(nproj):
            acc = jnp.zeros((states, atoms), F32)
            for l in range(nproj):
                acc = acc + (
                    coup_ref[g, k * nproj + l:k * nproj + l + 1, :]
                    * coef_ref[g, l * states:(l + 1) * states, :]
                )
            rows.append(acc)
        chosen = jnp.where(eatom_ref[...] == slot_ids + g * atoms, 1.0, 0.0)
        entry_terms = entry_terms + jnp.dot(
            jnp.concatenate(rows, axis=0), chosen, precision=HIGH, preferred_element_type=F32
        )
    terms = [entry_terms[k * states:(k + 1) * states, :] for k in range(nproj)]

    def node_body(j, carry):
        proj = proj_ref[j].astype(F32)
        total = proj[0:1, :] * terms[0]
        for k in range(1, nproj):
            total = total + proj[k:k + 1, :] * terms[k]
        ns_ref[pl.ds(pl.multiple_of(j * states, states), states), :] = total
        return carry

    lax.fori_loop(0, width, node_body, 0, unroll=8)
    cell_ids = lax.broadcasted_iota(jnp.int32, (cells, entries), 0)
    spread = jnp.where(cell_ids == ecell_ref[...], 1.0, 0.0).astype(BF16)
    back = (((1,), (1,)), ((), ()))
    node_vals = ns_ref[...]
    node_top = node_vals.astype(BF16)
    node_rest = (node_vals - node_top.astype(F32)).astype(BF16)
    v_ref[...] = (
        ct_ref[...]
        + lax.dot_general(node_top, spread, back, preferred_element_type=F32)
        + lax.dot_general(node_rest, spread, back, preferred_element_type=F32)
    )
    acc_ref[...] = jnp.zeros_like(acc_ref)
    slots = sched_ref.shape[0] // groups

    def group_body(g, carry):
        lo = fill_onehot(cn_ref, g, oh_ref)

        def pair_body(r, inner):
            first = sched_ref[g * slots + 2 * r]
            second = sched_ref[g * slots + 2 * r + 1]
            for jj in range(GROUP):
                start = pl.multiple_of((g * GROUP + jj) * states, states)
                value = v_ref[pl.ds(start, states), :]
                top = value.astype(BF16).astype(F32)
                both = jnp.concatenate([top, value - top], axis=0)
                lanes = slice(jj * cells, (jj + 1) * cells)
                for half, chunk in enumerate((first, second)):
                    row = lo[jj:jj + 1, :] - chunk * layers
                    for l in range(layers):
                        at = half * rows_in_chunk + l * 2 * states
                        lhs_ref[at:at + 2 * states, lanes] = (
                            jnp.where(row == l, both, 0.0).astype(BF16)
                        )
            out = lax.dot_general(lhs_ref[...], oh_ref[...], back, preferred_element_type=F32)
            acc_ref[first] += out[:rows_in_chunk]
            acc_ref[second] += out[rows_in_chunk:]
            return inner

        pairs = lax.shift_right_logical(sched_ref[g * slots + slots - 1] + 1, 1)
        return lax.fori_loop(0, pairs, pair_body, carry)

    lax.fori_loop(0, groups, group_body, 0)
    for c in range(chunks):
        for l in range(layers):
            base = (c * layers + l) * WIDE
            at = l * 2 * states
            y_ref[:, base:base + WIDE] = (
                acc_ref[c, at:at + states, :] + acc_ref[c, at + states:at + 2 * states, :]
            )


MESH_ID = pl.DeviceIdType.MESH


def ring_peer(steps):
    count = lax.axis_size("mesh")
    return lax.rem(lax.axis_index("mesh") + steps + count, count)


def send(src, dst, sems, at, peer):
    copy = pltpu.make_async_remote_copy(
        src_ref=src, dst_ref=dst, send_sem=sems.at[0, at], recv_sem=sems.at[1, at],
        device_id=peer, device_id_type=MESH_ID,
    )
    copy.start()
    return copy


def greet(peers):
    barrier = pltpu.get_barrier_semaphore()
    for peer in peers:
        pl.semaphore_signal(barrier, inc=1, device_id=peer, device_id_type=MESH_ID)
    return barrier


def start_kernel(psi_ref, pot_ref, coup_ref, ext_ref, potx_ref, coups_ref, sems):
    count = psi_ref.shape[1]
    face = ext_ref.shape[1] - count
    ahead, behind = {"mesh": ring_peer(1)}, {"mesh": ring_peer(-1)}
    pl.semaphore_wait(greet((ahead, behind)), 2)
    copies = [
        send(psi_ref.at[:, :face], ext_ref.at[:, count:], sems, 0, behind),
        send(coup_ref, coups_ref.at[0], sems, 1, ahead),
        send(coup_ref, coups_ref.at[2], sems, 2, behind),
        send(pot_ref.at[:, :face], potx_ref.at[:, count:], sems, 3, behind),
    ]
    ext_ref[:, :count] = psi_ref[...]
    potx_ref[:, :count] = pot_ref[...]
    coups_ref[1] = coup_ref[...]
    for copy in copies:
        copy.wait()


def atoms_kernel(xs_ref, kmat_ref, scale_ref, proj_ref, ecell_ref, eatom_ref, ct_ref, coef_ref,
                 es_ref, grouped_ref, left_ref, right_ref, far_ref, sems):
    peers = [{"mesh": ring_peer(steps)} for steps in (1, -1, 2, -2)]
    barrier = greet(peers)
    width, nproj, entries = proj_ref.shape
    cells = xs_ref.shape[1]
    states = xs_ref.shape[0] // width
    cell_ids = lax.broadcasted_iota(jnp.int32, (cells, entries), 0)
    spread = jnp.where(cell_ids == ecell_ref[...], 1.0, 0.0).astype(BF16)
    es_ref[...] = jnp.dot(xs_ref[...].astype(BF16), spread, preferred_element_type=F32)

    def partial_body(j, accs):
        values = es_ref[pl.ds(pl.multiple_of(j * states, states), states), :]
        proj = proj_ref[j].astype(F32)
        return tuple(acc + proj[k:k + 1, :] * values for k, acc in enumerate(accs))

    zero = jnp.zeros((states, entries), F32)
    accs = lax.fori_loop(0, width, partial_body, (zero,) * nproj, unroll=8)
    partial_sum = jnp.concatenate(accs, axis=0)
    atoms = grouped_ref.shape[2]
    slot_ids = lax.broadcasted_iota(jnp.int32, (atoms, entries), 0)
    for g in range(3):
        chosen = jnp.where(eatom_ref[...] == slot_ids + g * atoms, 1.0, 0.0)
        grouped_ref[g] = lax.dot_general(
            partial_sum, chosen, (((1,), (1,)), ((), ())), precision=HIGH,
            preferred_element_type=F32,
        )
    pl.semaphore_wait(barrier, 4)
    copies = [
        send(grouped_ref.at[1:3], left_ref, sems, 0, peers[0]),
        send(grouped_ref.at[0:2], right_ref, sems, 1, peers[1]),
        send(grouped_ref.at[2], far_ref.at[0], sems, 2, peers[2]),
        send(grouped_ref.at[0], far_ref.at[1], sems, 3, peers[3]),
    ]
    kmat = kmat_ref[...]
    scale = scale_ref[...]
    for s in range(0, states, 2):
        pair = jnp.concatenate(
            [xs_ref[pl.ds(s, width, stride=states), :], xs_ref[pl.ds(s + 1, width, stride=states), :]],
            axis=1,
        ).astype(BF16)
        out = jnp.dot(kmat, pair, preferred_element_type=F32)
        ct_ref[pl.ds(s, width, stride=states), :] = out[:, :cells] * scale
        ct_ref[pl.ds(s + 1, width, stride=states), :] = out[:, cells:] * scale
    for copy in copies:
        copy.wait()
    coef_ref[0] = left_ref[0] + far_ref[0] + grouped_ref[0]
    coef_ref[1] = grouped_ref[1] + left_ref[1] + right_ref[0]
    coef_ref[2] = right_ref[1] + grouped_ref[2] + far_ref[1]


def first_kernel(y_ref, ext_ref, pot_ref, first_ref, low_ref, high_ref, sems):
    full = y_ref.shape[1]
    face = low_ref.shape[1]
    count = full - face
    ahead, behind = {"mesh": ring_peer(1)}, {"mesh": ring_peer(-1)}
    barrier = greet((ahead, behind))

    def finish(total, at):
        scaled = (total + pot_ref[:, at] * ext_ref[:, at].astype(F32)) / HALFWIDTH
        first_ref[:, at] = scaled.astype(BF16)

    middle = face * (1 + (count // face - 1) // 2)
    for base in range(face, middle, face):
        at = slice(base, base + face)
        finish(y_ref[:, at], at)
    pl.semaphore_wait(barrier, 2)
    copies = [
        send(y_ref.at[:, count:], low_ref, sems, 0, ahead),
        send(y_ref.at[:, :face], high_ref, sems, 1, behind),
    ]
    for base in range(middle, count, face):
        at = slice(base, base + face)
        finish(y_ref[:, at], at)
    for copy in copies:
        copy.wait()
    finish(y_ref[:, :face] + low_ref[...], slice(0, face))
    finish(y_ref[:, count:] + high_ref[...], slice(count, full))


def last_kernel(y_ref, first_ref, psi_ref, pot_ref, out_ref, corr_ref, low_ref, other_ref,
                slots_ref, sems):
    count = psi_ref.shape[1]
    face = low_ref.shape[1]
    devices = lax.axis_size("mesh")
    bands = lax.axis_size("band")
    me = lax.axis_index("mesh")
    band = lax.axis_index("band")
    partner = {"band": lax.rem(band + 1, bands)}
    barrier = greet((partner,))

    def greet_body(steps, carry):
        pl.semaphore_signal(
            barrier, inc=1, device_id={"mesh": lax.rem(me + steps, devices)}, device_id_type=MESH_ID
        )
        return carry

    lax.fori_loop(1, devices, greet_body, 0)

    def finish(total, at):
        scaled = (total + pot_ref[:, at] * first_ref[:, at].astype(F32)) / HALFWIDTH
        out_ref[:, at] = (2.0 * scaled - psi_ref[:, at].astype(F32)).astype(BF16)

    for base in range(face, count, face):
        at = slice(base, base + face)
        finish(y_ref[:, at], at)
    pl.semaphore_wait(barrier, devices)
    tail = send(y_ref.at[:, count:count + face], low_ref, sems, 0, {"mesh": ring_peer(1)})
    swap = send(out_ref.at[:, face:], other_ref.at[:, face:], sems, 1, partner)
    states = out_ref.shape[0]

    def gram(base):
        at = slice(base, base + face)
        own, other = out_ref[:, at].astype(F32), other_ref[:, at].astype(F32)
        block = jnp.concatenate(
            [jnp.where(band == 0, own, other), jnp.where(band == 0, other, own)], axis=0
        ).astype(BF16)
        return lax.dot_general(
            block, block, (((1,), (1,)), ((), ())), preferred_element_type=F32
        )

    swap.wait()
    total = gram(face)
    for base in range(2 * face, count, face):
        total = total + gram(base)
    tail.wait()
    finish(y_ref[:, :face] + low_ref[...], slice(0, face))
    edge = send(out_ref.at[:, :face], other_ref.at[:, :face], sems, 3, partner)
    edge.wait()
    total = total + gram(0)
    slots_ref[me] = total

    def push(steps, carry):
        send(slots_ref.at[me], slots_ref.at[me], sems, 2, {"mesh": lax.rem(me + steps, devices)})
        return carry

    lax.fori_loop(1, devices, push, 0)
    pltpu.make_async_remote_copy(
        src_ref=slots_ref.at[pl.ds(0, devices - 1)], dst_ref=slots_ref.at[pl.ds(0, devices - 1)],
        send_sem=sems.at[0, 2], recv_sem=sems.at[1, 2], device_id=partner, device_id_type=MESH_ID,
    ).wait()
    corr_ref[...] = jnp.sum(slots_ref[...], axis=0) * (1.0 / (devices * count))


def everyone(count):
    bands = lax.axis_size("band")
    flat = lax.axis_index("mesh") * bands + lax.axis_index("band")

    def peer(steps):
        other = lax.rem(flat + steps, count)
        return {"mesh": other // bands, "band": lax.rem(other, bands)}

    return flat, peer


def halves(value, axis):
    top = value.astype(BF16)
    return jnp.concatenate([top, (value - top.astype(F32)).astype(BF16)], axis=axis)


def fused_kernel(psi_ref, cn_ref, scale_ref, kmat_ref, pot_ref, proj_ref, ecell_ref, eatom_ref,
                 coup_ref, out_ref, corr_ref, flag_ref,
                 oh_ref, oht_ref, hi_ref, pd_ref, xs_ref, ct_ref, five_ref, ys_ref, lhs_ref,
                 masked_ref, mid_ref, first_ref, potf_ref, head_ref, tail_ref, low_ref, high_ref,
                 grouped_ref, left_ref, right_ref, far_ref, ghost_ref, potg_ref, coups_ref,
                 spread_ref, other_ref, slots_ref, sems):
    states, count = psi_ref.shape
    width, cells = cn_ref.shape
    face = ghost_ref.shape[1]
    slabs = count // face
    layers = slabs + 1
    _, nproj, entries = proj_ref.shape
    atoms = coup_ref.shape[1]
    edge = slabs // 2 + 1
    group = width // edge
    pairs = cells // 2
    tiles = face // WIDE
    block = (tiles + 1) * states
    wraps = group // 2
    devices, bands = lax.axis_size("mesh"), lax.axis_size("band")
    band = lax.axis_index("band")
    me, peer = everyone(devices * bands)
    ahead, behind = {"mesh": ring_peer(1)}, {"mesh": ring_peer(-1)}
    ahead2, behind2 = {"mesh": ring_peer(2)}, {"mesh": ring_peer(-2)}
    partner = {"band": lax.rem(band + 1, bands)}
    barrier = pltpu.get_barrier_semaphore()

    def greet_body(steps, carry):
        pl.semaphore_signal(barrier, inc=1, device_id=peer(steps), device_id_type=MESH_ID)
        return carry

    lax.fori_loop(1, devices * bands, greet_body, 0)

    down = lax.broadcasted_iota(jnp.int32, (cells, cells), 0)
    across = lax.broadcasted_iota(jnp.int32, (cells, cells), 1)
    eye = down == across
    key = jnp.broadcast_to(cn_ref[0:1, :].astype(F32), (cells, cells))
    key_col = jnp.sum(jnp.where(eye, key, 0.0), axis=1, keepdims=True)
    rank = jnp.sum(jnp.where(key < key_col, 1.0, 0.0), axis=1, keepdims=True)
    chosen_cell = rank == across.astype(F32)
    order = jnp.where(chosen_cell, 1.0, 0.0).astype(BF16)
    scale_col = jnp.sum(
        jnp.where(eye, jnp.broadcast_to(scale_ref[...], (cells, cells)), 0.0), axis=1, keepdims=True
    )
    scale = jnp.sum(jnp.where(chosen_cell, scale_col, 0.0), axis=0, keepdims=True)
    entry_rank = jnp.sum(
        jnp.where(lax.broadcasted_iota(jnp.int32, (cells, entries), 0) == ecell_ref[...], rank, 0.0),
        axis=0, keepdims=True,
    )
    spread = jnp.where(
        lax.broadcasted_iota(jnp.int32, (cells, entries), 0).astype(F32) == entry_rank, 1.0, 0.0
    )
    spread_ref[...] = spread.astype(BF16)
    table = cn_ref[...]
    upper = lax.shift_right_logical(table, 8).astype(F32)
    lower = jnp.bitwise_and(table, WIDE - 1).astype(F32)
    table = WIDE * jnp.dot(upper.astype(BF16), order, preferred_element_type=F32) + jnp.dot(
        lower.astype(BF16), order, preferred_element_type=F32
    )
    low_half = lax.broadcasted_iota(jnp.int32, (1, cells), 1) < pairs
    base = table[:group]
    base = jnp.where(low_half, base, pltpu.roll(base, pairs, 1))
    lift = jnp.where(low_half, 0.0, float((edge - 1) * face))
    wrong = jnp.where((base < 0.0) | (base >= float(face)), 1.0, 0.0)
    for a in range(edge):
        expected = base + (lift + float(a * face))
        wrong = jnp.maximum(
            wrong, jnp.where(table[a * group:(a + 1) * group] == expected, 0.0, 1.0)
        )
    flag_ref[0, 0] = jnp.max(wrong)
    pd_ref[:group, :] = base
    places = jnp.where(
        low_half, pd_ref[pl.ds(0, wraps, stride=2), :], pd_ref[pl.ds(1, wraps, stride=2), :]
    ).astype(jnp.int32)
    slot = jnp.bitwise_and(places, WIDE - 1)
    hi_ref[:wraps, :] = lax.shift_right_logical(places, 8)
    wide_ids = lax.broadcasted_iota(jnp.int16, (WIDE, cells), 0)
    one, zero = jnp.array(1.0, BF16), jnp.array(0.0, BF16)
    for w in range(wraps):
        hot = jnp.where(wide_ids == slot[w:w + 1, :].astype(jnp.int16), one, zero)
        oh_ref[:, w * cells:(w + 1) * cells] = hot
        oht_ref[w * cells:(w + 1) * cells, :] = hot.T

    pl.semaphore_wait(barrier, devices * bands - 1)
    coups_ref[1] = coup_ref[...]
    gaps = [
        send(psi_ref.at[:, :face], ghost_ref, sems, 0, behind),
        send(pot_ref.at[:potg_ref.shape[0], :], potg_ref, sems, 1, behind),
        send(coup_ref, coups_ref.at[0], sems, 2, ahead),
        send(coup_ref, coups_ref.at[2], sems, 3, behind),
    ]
    rows128 = face // 128
    potf_ref[:slabs * rows128, :] = pot_ref[...].astype(F32) - CENTER

    def place(layer):
        if isinstance(layer, int):
            return 0 if layer == 0 else 1 if layer == slabs else layer + 1
        return layer + 1

    def put(layer, blocks):
        both = jnp.concatenate(blocks + [blocks[-1]], axis=0).astype(BF16)
        start = place(layer) * block
        if not isinstance(layer, int):
            start = pl.multiple_of(start, block)
        lhs_ref[pl.ds(start, block), :] = both

    def put_psi(layer, source, at):
        put(layer, [
            source[:, pl.ds(pl.multiple_of(at + t * WIDE, WIDE), WIDE)].astype(F32)
            for t in range(tiles)
        ])

    def psi_body(layer, carry):
        put_psi(layer, psi_ref, layer * face)
        return carry

    put_psi(0, psi_ref, 0)
    lax.fori_loop(1, slabs, psi_body, 0)

    def gather(first_row, chosen, finish):
        rows = len(chosen) * block

        def body(n, carry):
            hot = oh_ref[:, pl.ds(pl.multiple_of(n * WIDE, WIDE), WIDE)]
            out = jnp.dot(lhs_ref[first_row:first_row + rows, :], hot, preferred_element_type=F32)
            for c in range(WIDE // cells):
                w = n * (WIDE // cells) + c
                hi = jnp.broadcast_to(hi_ref[pl.ds(w, 1), :], (states, cells))
                masks = [hi == t for t in range(1, tiles)]
                found = {}
                for k, layer in enumerate(chosen):
                    part = out[k * block:(k + 1) * block, c * cells:(c + 1) * cells]
                    value = part[:states]
                    for t in range(1, tiles):
                        value = jnp.where(
                            masks[t - 1], part[t * states:(t + 1) * states], value
                        )
                    found[layer] = value
                finish(w, found)
            return carry

        lax.fori_loop(0, wraps * cells // WIDE, body, 0)

    def store_pair(a, w, lower_cells, upper_cells):
        mixed = pltpu.roll(jnp.where(low_half, upper_cells, lower_cells), pairs, 1)
        at = pl.multiple_of((a * group + 2 * w) * states, 2 * states)
        xs_ref[pl.ds(at, states), :] = jnp.where(low_half, lower_cells, mixed)
        xs_ref[pl.ds(at + states, states), :] = jnp.where(low_half, mixed, upper_cells)

    def inner_found(w, found):
        for a in range(1, edge - 1):
            store_pair(a, w, found[a], found[edge - 1 + a])
        five_ref[pl.ds(pl.multiple_of(w * states, states), states), :] = found[edge - 1]

    def outer_found(w, found):
        middle = five_ref[pl.ds(pl.multiple_of(w * states, states), states), :]
        store_pair(0, w, found[0], middle)
        store_pair(edge - 1, w, middle, found[slabs])

    def gather_inner():
        gather(2 * block, tuple(range(1, slabs)), inner_found)

    def gather_outer():
        gather(0, (0, slabs), outer_found)

    def partial_body(a, accs):
        at = pl.multiple_of(a * group * states, group * states)
        values = jnp.dot(
            xs_ref[pl.ds(at, group * states), :].astype(BF16), spread_ref[...],
            preferred_element_type=F32,
        )
        accs = list(accs)
        for j in range(group):
            proj = proj_ref[a * group + j].astype(F32)
            value = values[j * states:(j + 1) * states]
            for k in range(nproj):
                accs[k] = accs[k] + proj[k:k + 1, :] * value
        return tuple(accs)

    slot_ids = lax.broadcasted_iota(jnp.int32, (3 * atoms, entries), 0)
    chosen_atom = jnp.where(slot_ids == eatom_ref[...], 1.0, 0.0).astype(BF16)
    back = (((1,), (1,)), ((), ()))
    empty = tuple(jnp.zeros((states, entries), F32) for _ in range(nproj))

    def send_atoms(step, accs):
        grouped = lax.dot_general(
            halves(jnp.concatenate(accs, axis=0), 1),
            jnp.concatenate([chosen_atom, chosen_atom], axis=1),
            back, preferred_element_type=F32,
        )
        for g in range(3):
            grouped_ref[step, g] = grouped[:, g * atoms:(g + 1) * atoms]
        at = 4 + 6 * step
        return [
            send(grouped_ref.at[step, 1:3], left_ref.at[step], sems, at, ahead),
            send(grouped_ref.at[step, 0:2], right_ref.at[step], sems, at + 1, behind),
            send(grouped_ref.at[step, 2], far_ref.at[step, 0], sems, at + 2, ahead2),
            send(grouped_ref.at[step, 0], far_ref.at[step, 1], sems, at + 3, behind2),
        ]

    def cell_terms():
        kmat = kmat_ref[...]
        for s in range(0, states, 2):
            pair = jnp.concatenate(
                [xs_ref[pl.ds(s, width, stride=states), :],
                 xs_ref[pl.ds(s + 1, width, stride=states), :]], axis=1,
            ).astype(BF16)
            out = jnp.dot(kmat, pair, preferred_element_type=F32)
            ct_ref[pl.ds(s, width, stride=states), :] = out[:, :cells] * scale
            ct_ref[pl.ds(s + 1, width, stride=states), :] = out[:, cells:] * scale

    def node_stage(step):
        left, right, far = left_ref.at[step], right_ref.at[step], far_ref.at[step]
        mine = grouped_ref.at[step]
        coef = jnp.concatenate(
            [left[0] + far[0] + mine[0], mine[1] + left[1] + right[0],
             right[1] + mine[2] + far[1]], axis=1,
        )
        coup = jnp.concatenate([coups_ref[0], coups_ref[1], coups_ref[2]], axis=1)
        rows = []
        for k in range(nproj):
            acc = jnp.zeros((states, 3 * atoms), F32)
            for l in range(nproj):
                acc = acc + (
                    coup[k * nproj + l:k * nproj + l + 1, :]
                    * coef[l * states:(l + 1) * states, :]
                )
            rows.append(acc)
        terms = jnp.dot(
            halves(jnp.concatenate(rows, axis=0), 1),
            jnp.concatenate([chosen_atom, chosen_atom], axis=0),
            preferred_element_type=F32,
        )
        terms = [terms[k * states:(k + 1) * states] for k in range(nproj)]
        ys_ref[...] = jnp.zeros_like(ys_ref)
        twice = jnp.concatenate([spread_ref[...], spread_ref[...]], axis=1)

        def body(a, carry):
            parts = []
            for j in range(group):
                proj = proj_ref[a * group + j].astype(F32)
                total = proj[0:1, :] * terms[0]
                for k in range(1, nproj):
                    total = total + proj[k:k + 1, :] * terms[k]
                parts.append(total)
            at = pl.multiple_of(a * group * states, group * states)
            value = ct_ref[pl.ds(at, group * states), :] + lax.dot_general(
                halves(jnp.concatenate(parts, axis=0), 1), twice, back, preferred_element_type=F32
            )
            for w in range(wraps):
                even = value[2 * w * states:(2 * w + 1) * states]
                odd = value[(2 * w + 1) * states:(2 * w + 2) * states]
                mixed = pltpu.roll(jnp.where(low_half, odd, even), pairs, 1)
                here = pl.multiple_of((a * wraps + w) * states, states)
                there = pl.multiple_of(((a + edge - 1) * wraps + w) * states, states)
                ys_ref[pl.ds(here, states), :] += jnp.where(low_half, even, mixed)
                ys_ref[pl.ds(there, states), :] += jnp.where(low_half, mixed, odd)
            return carry

        lax.fori_loop(0, edge, body, 0)

    def fill_masked():
        def body(layer, carry):
            base = layer * (tiles * 2 * states)
            for w in range(wraps):
                hi = hi_ref[w:w + 1, :].astype(jnp.int16)
                at = pl.multiple_of((layer * wraps + w) * states, states)
                both = halves(ys_ref[pl.ds(at, states), :], 0)
                for t in range(tiles):
                    rows = pl.ds(pl.multiple_of(base + t * 2 * states, 2 * states), 2 * states)
                    masked_ref[rows, w * cells:(w + 1) * cells] = jnp.where(hi == t, both, zero)
            return carry

        lax.fori_loop(0, layers, body, 0)

    per = tiles * 2 * states

    def joined(value, t):
        return value[t * 2 * states:t * 2 * states + states] + (
            value[t * 2 * states + states:(t + 1) * 2 * states]
        )

    def scatter_outer(step):
        for layer, into in ((0, head_ref.at[step]), (slabs, tail_ref.at[step])):
            out = jnp.dot(
                masked_ref[layer * per:(layer + 1) * per, :], oht_ref[...],
                preferred_element_type=F32,
            )
            for t in range(tiles):
                into[:, t * WIDE:(t + 1) * WIDE] = joined(out, t)

    def scatter_inner():
        mid_ref[...] = jnp.dot(
            masked_ref[per:slabs * per, :], oht_ref[...], preferred_element_type=F32
        )

    def pot_row(layer, t, half):
        row = layer * rows128 + t * 2 + half
        return potf_ref[pl.ds(row, 1), :]

    def scaled(layer, t, summed, field):
        pot = jnp.concatenate([pot_row(layer, t, 0), pot_row(layer, t, 1)], axis=1)
        return (summed + pot * field) * (1.0 / HALFWIDTH)

    def lanes(layer, t):
        at = layer * face + t * WIDE
        return pl.ds(at if isinstance(layer, int) else pl.multiple_of(at, WIDE), WIDE)

    def first_layer(layer, summed, field):
        blocks = []
        for t in range(tiles):
            value = scaled(layer, t, summed(t), field(t)).astype(BF16).astype(F32)
            first_ref[:, lanes(layer, t)] = value
            blocks.append(value)
        put(layer, blocks)

    def last_layer(layer, summed):
        for t in range(tiles):
            value = scaled(layer, t, summed(t), first_ref[:, lanes(layer, t)])
            at = lanes(layer, t)
            out_ref[:, at] = (2.0 * value - psi_ref[:, at].astype(F32)).astype(BF16)

    def mid_sum(layer):
        def summed(t):
            at = pl.multiple_of((layer - 1) * per + t * 2 * states, 2 * states)
            return mid_ref[pl.ds(at, states), :] + mid_ref[pl.ds(at + states, states), :]
        return summed

    def edge_sum(one_ref, two_ref):
        return lambda t: (
            one_ref[:, t * WIDE:(t + 1) * WIDE] + two_ref[:, t * WIDE:(t + 1) * WIDE]
        )

    gather_inner()
    accs = lax.fori_loop(1, edge - 1, partial_body, empty)
    for copy in gaps:
        copy.wait()
    potf_ref[slabs * rows128:slabs * rows128 + potg_ref.shape[0], :] = (
        potg_ref[...].astype(F32) - CENTER
    )
    put_psi(slabs, ghost_ref, 0)
    gather_outer()
    for a in (0, edge - 1):
        accs = partial_body(a, accs)
    copies = send_atoms(0, accs)
    cell_terms()
    for copy in copies:
        copy.wait()
    node_stage(0)
    fill_masked()
    scatter_outer(0)
    copies = [
        send(tail_ref.at[0], low_ref.at[0], sems, 8, ahead),
        send(head_ref.at[0], high_ref, sems, 9, behind),
    ]
    scatter_inner()

    def first_body(layer, carry):
        first_layer(
            layer, mid_sum(layer), lambda t: psi_ref[:, lanes(layer, t)].astype(F32)
        )
        return carry

    lax.fori_loop(1, slabs, first_body, 0)
    gather_inner()
    accs = lax.fori_loop(1, edge - 1, partial_body, empty)
    for copy in copies:
        copy.wait()
    first_layer(0, edge_sum(head_ref.at[0], low_ref.at[0]), lambda t: psi_ref[:, lanes(0, t)].astype(F32))
    first_layer(
        slabs, edge_sum(tail_ref.at[0], high_ref),
        lambda t: ghost_ref[:, t * WIDE:(t + 1) * WIDE].astype(F32),
    )
    gather_outer()
    for a in (0, edge - 1):
        accs = partial_body(a, accs)
    copies = send_atoms(1, accs)
    cell_terms()
    for copy in copies:
        copy.wait()
    node_stage(1)
    fill_masked()
    scatter_outer(1)
    tail = send(tail_ref.at[1], low_ref.at[1], sems, 14, ahead)
    scatter_inner()

    def last_body(layer, carry):
        last_layer(layer, mid_sum(layer))
        return carry

    lax.fori_loop(1, slabs, last_body, 0)
    half = slabs // 2
    kept = half - 1
    mine = jnp.where(band == 0, 1, half) * face
    theirs = jnp.where(band == 0, half, 1) * face

    def span(at, size):
        return pl.ds(pl.multiple_of(at, 128), size)

    swap = send(out_ref.at[:, span(theirs, kept * face)], other_ref.at[:, :kept * face], sems, 15, partner)

    def gram(own_at, at):
        own = out_ref[:, span(own_at, face)].astype(F32)
        other = other_ref[:, at:at + face].astype(F32)
        both = jnp.concatenate(
            [jnp.where(band == 0, own, other), jnp.where(band == 0, other, own)], axis=0
        ).astype(BF16)
        return lax.dot_general(both, both, back, preferred_element_type=F32)

    swap.wait()
    total = gram(mine, 0)
    for n in range(1, kept):
        total = total + gram(mine + n * face, n * face)
    tail.wait()
    last_layer(0, edge_sum(head_ref.at[1], low_ref.at[1]))
    mine = jnp.where(band == 0, 0, slabs - 1) * face
    theirs = jnp.where(band == 0, slabs - 1, 0) * face
    final = send(out_ref.at[:, span(theirs, face)], other_ref.at[:, kept * face:], sems, 16, partner)
    final.wait()
    total = total + gram(mine, kept * face)
    size = bands * states
    slots_ref[me] = jnp.concatenate(
        [total[:states], total[states:], jnp.zeros((states, 128 - 2 * size), F32)], axis=1
    )

    def push(steps, carry):
        send(slots_ref.at[me], slots_ref.at[me], sems, 17, peer(steps))
        return carry

    lax.fori_loop(1, devices * bands, push, 0)
    rest = pl.ds(0, devices * bands - 1)
    pltpu.make_async_remote_copy(
        src_ref=slots_ref.at[rest], dst_ref=slots_ref.at[rest], send_sem=sems.at[0, 17],
        recv_sem=sems.at[1, 17], device_id=partner, device_id_type=MESH_ID,
    ).wait()
    total = jnp.sum(slots_ref[...], axis=0) * (1.0 / (devices * count))
    corr_ref[...] = jnp.concatenate([total[:, :size], total[:, size:2 * size]], axis=0)


def general(
    psi,
    cell_nodes,
    cell_scale,
    cell_matrix,
    node_potential,
    proj_values,
    entry_cell,
    entry_atom,
    coupling,
):
    states, node_count = psi.shape
    width, cells = cell_nodes.shape
    atoms, nproj, _ = coupling.shape
    entries = entry_atom.shape[0]
    full = node_count + FACEP
    chunks = full // FACEP
    layers = FACEP // WIDE
    groups = width // GROUP
    span = GROUP * cells

    table = cell_nodes.reshape(groups, GROUP, cells)
    owner = table // FACEP
    ids = jnp.arange(chunks, dtype=jnp.int32)
    flags = jnp.max(
        (owner[:, None] == ids[None, :, None, None]).astype(jnp.int32), axis=(2, 3)
    )
    rank = jnp.sum(flags[:, None, :] * (ids[None, :] < ids[:, None]), axis=2)
    places = jnp.arange(chunks + 1, dtype=jnp.int32)
    used = flags[:, :, None] * (rank[:, :, None] == places)
    listed = chunks + jnp.sum(used * (ids[None, :, None] - chunks), axis=1)
    listed = jnp.concatenate(
        [listed, jnp.full((groups, 1), chunks, jnp.int32), jnp.sum(flags, axis=1, keepdims=True)],
        axis=1,
    )
    sched = listed.astype(jnp.int32).reshape(groups * (chunks + 3))
    scale_row = cell_scale.reshape(1, cells)
    ecell = entry_cell.reshape(1, entries)
    eatom = entry_atom.reshape(1, entries)
    coup = coupling.transpose(1, 2, 0).reshape(nproj * nproj, atoms)
    potential = node_potential.astype(F32).reshape(1, node_count) - CENTER

    vmem = pl.BlockSpec(memory_space=pltpu.VMEM)
    smem = pl.BlockSpec(memory_space=pltpu.SMEM)

    padded = (layers * states + 15) // 16 * 16
    gather = pl.pallas_call(
        gather_kernel,
        out_shape=jax.ShapeDtypeStruct((width * states, cells), F32),
        in_specs=[smem] + [vmem] * 2,
        out_specs=vmem,
        scratch_shapes=[
            pltpu.VMEM((chunks + 1, padded, WIDE), BF16),
            pltpu.VMEM((WIDE, span), BF16),
        ],
        name="gather_cells",
    )
    scatter = pl.pallas_call(
        scatter_kernel,
        out_shape=jax.ShapeDtypeStruct((states, full), F32),
        in_specs=[smem] + [vmem] * 7,
        out_specs=vmem,
        scratch_shapes=[
            pltpu.VMEM((WIDE, span), BF16),
            pltpu.VMEM((width * states, entries), F32),
            pltpu.VMEM((width * states, cells), F32),
            pltpu.VMEM((2 * layers * 2 * states, span), BF16),
            pltpu.VMEM((chunks + 1, layers * 2 * states, WIDE), F32),
        ],
        name="scatter_nodes",
    )

    def remote(kernel, outs, n_in, scratch, copies, ident):
        return pl.pallas_call(
            kernel,
            out_shape=tuple(jax.ShapeDtypeStruct(*out) for out in outs),
            in_specs=[vmem] * n_in,
            out_specs=(vmem,) * len(outs),
            scratch_shapes=[pltpu.VMEM(*one) for one in scratch]
            + [pltpu.SemaphoreType.DMA((2, copies))],
            compiler_params=pltpu.CompilerParams(collective_id=ident, has_side_effects=True),
            name=kernel.__name__,
        )

    pair = (nproj * states, atoms)

    def assemble(extended, ident):
        values = gather(sched, table, extended)
        cell_terms, coef = remote(
            atoms_kernel, [((width * states, cells), F32), ((3,) + pair, F32)], 6,
            [((width * states, entries), F32), ((3,) + pair, F32)] + [((2,) + pair, F32)] * 3,
            4, ident,
        )(values, cell_matrix, scale_row, proj_values, ecell, eatom)
        return scatter(sched, table, cell_terms, coef, coup_all, proj_values, ecell, eatom)

    psi_ext, pot_ext, coup_all = remote(
        start_kernel,
        [((states, full), BF16), ((1, full), F32), ((3, nproj * nproj, atoms), F32)],
        3, [], 4, 1,
    )(psi, potential, coup)
    face = (states, FACEP)
    (first,) = remote(first_kernel, [((states, full), BF16)], 3, [(face, F32), (face, F32)], 2, 3)(
        assemble(psi_ext, 2), psi_ext, pot_ext
    )
    bands, devices = lax.axis_size("band"), lax.axis_size("mesh")
    square = (bands * states, bands * states)
    filtered, correlation = remote(
        last_kernel,
        [((states, node_count), BF16), (square, F32)],
        4,
        [(face, F32), ((states, node_count), BF16), ((devices,) + square, F32)],
        4, 5,
    )(assemble(first, 4), first, psi, potential)
    return (filtered, correlation)


def bricks(states, node_count, width, cells, bands):
    edge = round(width ** (1.0 / 3.0))
    return (
        edge ** 3 == width
        and (edge - 1) * 2 * FACEP == node_count
        and edge % 2 == 0
        and cells == 128
        and FACEP % WIDE == 0
        and states == 8
        and bands == 2
    )


def local(
    psi,
    cell_nodes,
    cell_scale,
    cell_matrix,
    node_potential,
    proj_values,
    entry_cell,
    entry_atom,
    coupling,
):
    states, node_count = psi.shape
    width, cells = cell_nodes.shape
    atoms, nproj, _ = coupling.shape
    entries = entry_atom.shape[0]
    bands, devices = lax.axis_size("band"), lax.axis_size("mesh")
    operands = (
        psi, cell_nodes, cell_scale, cell_matrix, node_potential, proj_values, entry_cell,
        entry_atom, coupling,
    )
    if not bricks(states, node_count, width, cells, bands):
        return general(*operands)
    edge = round(width ** (1.0 / 3.0))
    wraps = edge * edge // 2
    layers = node_count // FACEP + 1
    tiles = FACEP // WIDE
    block = (tiles + 1) * states
    per = tiles * 2 * states
    rows = node_count // 128
    ghost_rows = (FACEP // 128 + 15) // 16 * 16
    size = bands * states
    vmem = pl.BlockSpec(memory_space=pltpu.VMEM)
    smem = pl.BlockSpec(memory_space=pltpu.SMEM)
    face = (states, FACEP)
    trio = (2, 3, nproj * states, atoms)
    duo = (2, 2, nproj * states, atoms)
    filtered, correlation, wrong = pl.pallas_call(
        fused_kernel,
        out_shape=(
            jax.ShapeDtypeStruct((states, node_count), BF16),
            jax.ShapeDtypeStruct((size, size), F32),
            jax.ShapeDtypeStruct((1, 1), F32),
        ),
        in_specs=[vmem] * 9,
        out_specs=(vmem, vmem, smem),
        scratch_shapes=[
            pltpu.VMEM((WIDE, wraps * cells), BF16),
            pltpu.VMEM((wraps * cells, WIDE), BF16),
            pltpu.VMEM(((wraps + 7) // 8 * 8, cells), jnp.int32),
            pltpu.VMEM(((2 * wraps + 7) // 8 * 8, cells), F32),
            pltpu.VMEM((width * states, cells), F32),
            pltpu.VMEM((width * states, cells), F32),
            pltpu.VMEM((wraps * states, cells), F32),
            pltpu.VMEM((layers * wraps * states, cells), F32),
            pltpu.VMEM((layers * block, WIDE), BF16),
            pltpu.VMEM((layers * per, wraps * cells), BF16),
            pltpu.VMEM(((layers - 2) * per, WIDE), F32),
            pltpu.VMEM((states, layers * FACEP), F32),
            pltpu.VMEM((rows + ghost_rows, 128), F32),
            pltpu.VMEM((2,) + face, F32),
            pltpu.VMEM((2,) + face, F32),
            pltpu.VMEM((2,) + face, F32),
            pltpu.VMEM(face, F32),
            pltpu.VMEM(trio, F32),
            pltpu.VMEM(duo, F32),
            pltpu.VMEM(duo, F32),
            pltpu.VMEM(duo, F32),
            pltpu.VMEM(face, BF16),
            pltpu.VMEM((ghost_rows, 128), BF16),
            pltpu.VMEM((3, nproj * nproj, atoms), F32),
            pltpu.VMEM((cells, entries), BF16),
            pltpu.VMEM((states, node_count // 2), BF16),
            pltpu.VMEM((devices * bands, states, 128), F32),
            pltpu.SemaphoreType.DMA((2, 18)),
        ],
        compiler_params=pltpu.CompilerParams(collective_id=0, has_side_effects=True),
        name="fused_steps",
    )(
        psi, cell_nodes, cell_scale.reshape(1, cells), cell_matrix,
        node_potential.reshape(rows, 128), proj_values, entry_cell.reshape(1, entries),
        entry_atom.reshape(1, entries),
        coupling.transpose(1, 2, 0).reshape(nproj * nproj, atoms),
    )
    return lax.cond(
        wrong[0, 0] > 0.0,
        lambda: general(*operands),
        lambda: (filtered, correlation),
    )


def solution(mesh):
    return jax.shard_map(
        local,
        mesh=mesh,
        in_specs=(
            P("band", "mesh"),
            P(),
            P("mesh"),
            P(),
            P("mesh"),
            P(None, None, "mesh"),
            P("mesh"),
            P("mesh"),
            P("mesh", None, None),
        ),
        out_specs=(P("band", "mesh"), P()),
        check_vma=False,
    )
```

```python
import jax
import jax.numpy as jnp
from jax import lax
from jax.experimental import pallas as pl
from jax.experimental.pallas import tpu as pltpu
from jax.sharding import PartitionSpec as P

FACEP = 1792
CENTER = 0.5
HALFWIDTH = 2.5
HIGH = lax.Precision.HIGHEST
WIDE = 256
GROUP = 36
F32 = jnp.float32
BF16 = jnp.bfloat16


def fill_onehot(cn_ref, group, oh_ref):
    rows = cn_ref[group]
    hi = jnp.bitwise_and(rows, WIDE - 1)
    lanes = rows.shape[1]
    iota = lax.broadcasted_iota(jnp.int32, (WIDE, lanes), 0)
    for jj in range(GROUP):
        oh_ref[:, jj * lanes:(jj + 1) * lanes] = jnp.where(
            iota == hi[jj:jj + 1, :], 1.0, 0.0
        ).astype(BF16)
    return lax.shift_right_logical(rows, 8)


def gather_kernel(sched_ref, cn_ref, ext_ref, xs_ref, lhs_ref, oh_ref):
    states = ext_ref.shape[0]
    chunks = lhs_ref.shape[0] - 1
    layers = ext_ref.shape[1] // (chunks * WIDE)
    groups = cn_ref.shape[0]
    cells = cn_ref.shape[2]
    padded = lhs_ref.shape[1]
    slots = sched_ref.shape[0] // groups
    lhs_ref[...] = jnp.zeros_like(lhs_ref)
    for c in range(chunks):
        base = c * layers * WIDE
        parts = [
            ext_ref[:, base + l * WIDE:base + (l + 1) * WIDE].astype(F32) for l in range(layers)
        ]
        parts.append(jnp.zeros((padded - layers * states, WIDE), F32))
        lhs_ref[c] = jnp.concatenate(parts, axis=0).astype(BF16)
    xs_ref[...] = jnp.zeros_like(xs_ref)

    def group_body(g, carry):
        lo = fill_onehot(cn_ref, g, oh_ref)

        def pair_body(r, inner):
            first = sched_ref[g * slots + 2 * r]
            second = sched_ref[g * slots + 2 * r + 1]
            lhs = jnp.concatenate([lhs_ref[first], lhs_ref[second]], axis=0)
            out = jnp.dot(lhs, oh_ref[...], preferred_element_type=F32)
            for jj in range(GROUP):
                where = pl.ds(pl.multiple_of((g * GROUP + jj) * states, states), states)
                value = xs_ref[where, :]
                lanes = slice(jj * cells, (jj + 1) * cells)
                for half, chunk in enumerate((first, second)):
                    row = lo[jj:jj + 1, :] - chunk * layers
                    for l in range(layers):
                        at = half * padded + l * states
                        value = jnp.where(row == l, out[at:at + states, lanes], value)
                xs_ref[where, :] = value
            return inner

        pairs = lax.shift_right_logical(sched_ref[g * slots + slots - 1] + 1, 1)
        return lax.fori_loop(0, pairs, pair_body, carry)

    lax.fori_loop(0, groups, group_body, 0)


def scatter_kernel(sched_ref, cn_ref, ct_ref, coef_ref, coup_ref, proj_ref, ecell_ref,
                   eatom_ref, y_ref, oh_ref, ns_ref, v_ref, lhs_ref, acc_ref):
    chunks, rows_in_chunk, _ = acc_ref.shape
    chunks = chunks - 1
    groups = cn_ref.shape[0]
    cells = cn_ref.shape[2]
    width = groups * GROUP
    states = ct_ref.shape[0] // width
    layers = rows_in_chunk // (2 * states)
    nproj = proj_ref.shape[1]
    entries = ecell_ref.shape[1]
    atoms = coef_ref.shape[2]
    slot_ids = lax.broadcasted_iota(jnp.int32, (atoms, entries), 0)
    entry_terms = jnp.zeros((nproj * states, entries), F32)
    for g in range(3):
        rows = []
        for k in range(nproj):
            acc = jnp.zeros((states, atoms), F32)
            for l in range(nproj):
                acc = acc + (
                    coup_ref[g, k * nproj + l:k * nproj + l + 1, :]
                    * coef_ref[g, l * states:(l + 1) * states, :]
                )
            rows.append(acc)
        chosen = jnp.where(eatom_ref[...] == slot_ids + g * atoms, 1.0, 0.0)
        entry_terms = entry_terms + jnp.dot(
            jnp.concatenate(rows, axis=0), chosen, precision=HIGH, preferred_element_type=F32
        )
    terms = [entry_terms[k * states:(k + 1) * states, :] for k in range(nproj)]

    def node_body(j, carry):
        proj = proj_ref[j].astype(F32)
        total = proj[0:1, :] * terms[0]
        for k in range(1, nproj):
            total = total + proj[k:k + 1, :] * terms[k]
        ns_ref[pl.ds(pl.multiple_of(j * states, states), states), :] = total
        return carry

    lax.fori_loop(0, width, node_body, 0, unroll=8)
    cell_ids = lax.broadcasted_iota(jnp.int32, (cells, entries), 0)
    spread = jnp.where(cell_ids == ecell_ref[...], 1.0, 0.0).astype(BF16)
    back = (((1,), (1,)), ((), ()))
    node_vals = ns_ref[...]
    node_top = node_vals.astype(BF16)
    node_rest = (node_vals - node_top.astype(F32)).astype(BF16)
    v_ref[...] = (
        ct_ref[...]
        + lax.dot_general(node_top, spread, back, preferred_element_type=F32)
        + lax.dot_general(node_rest, spread, back, preferred_element_type=F32)
    )
    acc_ref[...] = jnp.zeros_like(acc_ref)
    slots = sched_ref.shape[0] // groups

    def group_body(g, carry):
        lo = fill_onehot(cn_ref, g, oh_ref)

        def pair_body(r, inner):
            first = sched_ref[g * slots + 2 * r]
            second = sched_ref[g * slots + 2 * r + 1]
            for jj in range(GROUP):
                start = pl.multiple_of((g * GROUP + jj) * states, states)
                value = v_ref[pl.ds(start, states), :]
                top = value.astype(BF16).astype(F32)
                both = jnp.concatenate([top, value - top], axis=0)
                lanes = slice(jj * cells, (jj + 1) * cells)
                for half, chunk in enumerate((first, second)):
                    row = lo[jj:jj + 1, :] - chunk * layers
                    for l in range(layers):
                        at = half * rows_in_chunk + l * 2 * states
                        lhs_ref[at:at + 2 * states, lanes] = (
                            jnp.where(row == l, both, 0.0).astype(BF16)
                        )
            out = lax.dot_general(lhs_ref[...], oh_ref[...], back, preferred_element_type=F32)
            acc_ref[first] += out[:rows_in_chunk]
            acc_ref[second] += out[rows_in_chunk:]
            return inner

        pairs = lax.shift_right_logical(sched_ref[g * slots + slots - 1] + 1, 1)
        return lax.fori_loop(0, pairs, pair_body, carry)

    lax.fori_loop(0, groups, group_body, 0)
    for c in range(chunks):
        for l in range(layers):
            base = (c * layers + l) * WIDE
            at = l * 2 * states
            y_ref[:, base:base + WIDE] = (
                acc_ref[c, at:at + states, :] + acc_ref[c, at + states:at + 2 * states, :]
            )


MESH_ID = pl.DeviceIdType.MESH


def ring_peer(steps):
    count = lax.axis_size("mesh")
    return lax.rem(lax.axis_index("mesh") + steps + count, count)


def send(src, dst, sems, at, peer):
    copy = pltpu.make_async_remote_copy(
        src_ref=src, dst_ref=dst, send_sem=sems.at[0, at], recv_sem=sems.at[1, at],
        device_id=peer, device_id_type=MESH_ID,
    )
    copy.start()
    return copy


def greet(peers):
    barrier = pltpu.get_barrier_semaphore()
    for peer in peers:
        pl.semaphore_signal(barrier, inc=1, device_id=peer, device_id_type=MESH_ID)
    return barrier


def start_kernel(psi_ref, pot_ref, coup_ref, ext_ref, potx_ref, coups_ref, sems):
    count = psi_ref.shape[1]
    face = ext_ref.shape[1] - count
    ahead, behind = {"mesh": ring_peer(1)}, {"mesh": ring_peer(-1)}
    pl.semaphore_wait(greet((ahead, behind)), 2)
    copies = [
        send(psi_ref.at[:, :face], ext_ref.at[:, count:], sems, 0, behind),
        send(coup_ref, coups_ref.at[0], sems, 1, ahead),
        send(coup_ref, coups_ref.at[2], sems, 2, behind),
        send(pot_ref.at[:, :face], potx_ref.at[:, count:], sems, 3, behind),
    ]
    ext_ref[:, :count] = psi_ref[...]
    potx_ref[:, :count] = pot_ref[...]
    coups_ref[1] = coup_ref[...]
    for copy in copies:
        copy.wait()


def atoms_kernel(xs_ref, kmat_ref, scale_ref, proj_ref, ecell_ref, eatom_ref, ct_ref, coef_ref,
                 es_ref, grouped_ref, left_ref, right_ref, far_ref, sems):
    peers = [{"mesh": ring_peer(steps)} for steps in (1, -1, 2, -2)]
    barrier = greet(peers)
    width, nproj, entries = proj_ref.shape
    cells = xs_ref.shape[1]
    states = xs_ref.shape[0] // width
    cell_ids = lax.broadcasted_iota(jnp.int32, (cells, entries), 0)
    spread = jnp.where(cell_ids == ecell_ref[...], 1.0, 0.0).astype(BF16)
    es_ref[...] = jnp.dot(xs_ref[...].astype(BF16), spread, preferred_element_type=F32)

    def partial_body(j, accs):
        values = es_ref[pl.ds(pl.multiple_of(j * states, states), states), :]
        proj = proj_ref[j].astype(F32)
        return tuple(acc + proj[k:k + 1, :] * values for k, acc in enumerate(accs))

    zero = jnp.zeros((states, entries), F32)
    accs = lax.fori_loop(0, width, partial_body, (zero,) * nproj, unroll=8)
    partial_sum = jnp.concatenate(accs, axis=0)
    atoms = grouped_ref.shape[2]
    slot_ids = lax.broadcasted_iota(jnp.int32, (atoms, entries), 0)
    for g in range(3):
        chosen = jnp.where(eatom_ref[...] == slot_ids + g * atoms, 1.0, 0.0)
        grouped_ref[g] = lax.dot_general(
            partial_sum, chosen, (((1,), (1,)), ((), ())), precision=HIGH,
            preferred_element_type=F32,
        )
    pl.semaphore_wait(barrier, 4)
    copies = [
        send(grouped_ref.at[1:3], left_ref, sems, 0, peers[0]),
        send(grouped_ref.at[0:2], right_ref, sems, 1, peers[1]),
        send(grouped_ref.at[2], far_ref.at[0], sems, 2, peers[2]),
        send(grouped_ref.at[0], far_ref.at[1], sems, 3, peers[3]),
    ]
    kmat = kmat_ref[...]
    scale = scale_ref[...]
    for s in range(0, states, 2):
        pair = jnp.concatenate(
            [xs_ref[pl.ds(s, width, stride=states), :], xs_ref[pl.ds(s + 1, width, stride=states), :]],
            axis=1,
        ).astype(BF16)
        out = jnp.dot(kmat, pair, preferred_element_type=F32)
        ct_ref[pl.ds(s, width, stride=states), :] = out[:, :cells] * scale
        ct_ref[pl.ds(s + 1, width, stride=states), :] = out[:, cells:] * scale
    for copy in copies:
        copy.wait()
    coef_ref[0] = left_ref[0] + far_ref[0] + grouped_ref[0]
    coef_ref[1] = grouped_ref[1] + left_ref[1] + right_ref[0]
    coef_ref[2] = right_ref[1] + grouped_ref[2] + far_ref[1]


def first_kernel(y_ref, ext_ref, pot_ref, first_ref, low_ref, high_ref, sems):
    full = y_ref.shape[1]
    face = low_ref.shape[1]
    count = full - face
    ahead, behind = {"mesh": ring_peer(1)}, {"mesh": ring_peer(-1)}
    barrier = greet((ahead, behind))

    def finish(total, at):
        scaled = (total + pot_ref[:, at] * ext_ref[:, at].astype(F32)) / HALFWIDTH
        first_ref[:, at] = scaled.astype(BF16)

    middle = face * (1 + (count // face - 1) // 2)
    for base in range(face, middle, face):
        at = slice(base, base + face)
        finish(y_ref[:, at], at)
    pl.semaphore_wait(barrier, 2)
    copies = [
        send(y_ref.at[:, count:], low_ref, sems, 0, ahead),
        send(y_ref.at[:, :face], high_ref, sems, 1, behind),
    ]
    for base in range(middle, count, face):
        at = slice(base, base + face)
        finish(y_ref[:, at], at)
    for copy in copies:
        copy.wait()
    finish(y_ref[:, :face] + low_ref[...], slice(0, face))
    finish(y_ref[:, count:] + high_ref[...], slice(count, full))


def last_kernel(y_ref, first_ref, psi_ref, pot_ref, out_ref, corr_ref, low_ref, other_ref,
                slots_ref, sems):
    count = psi_ref.shape[1]
    face = low_ref.shape[1]
    devices = lax.axis_size("mesh")
    bands = lax.axis_size("band")
    me = lax.axis_index("mesh")
    band = lax.axis_index("band")
    partner = {"band": lax.rem(band + 1, bands)}
    barrier = greet((partner,))

    def greet_body(steps, carry):
        pl.semaphore_signal(
            barrier, inc=1, device_id={"mesh": lax.rem(me + steps, devices)}, device_id_type=MESH_ID
        )
        return carry

    lax.fori_loop(1, devices, greet_body, 0)

    def finish(total, at):
        scaled = (total + pot_ref[:, at] * first_ref[:, at].astype(F32)) / HALFWIDTH
        out_ref[:, at] = (2.0 * scaled - psi_ref[:, at].astype(F32)).astype(BF16)

    for base in range(face, count, face):
        at = slice(base, base + face)
        finish(y_ref[:, at], at)
    pl.semaphore_wait(barrier, devices)
    tail = send(y_ref.at[:, count:count + face], low_ref, sems, 0, {"mesh": ring_peer(1)})
    swap = send(out_ref.at[:, face:], other_ref.at[:, face:], sems, 1, partner)
    states = out_ref.shape[0]

    def gram(base):
        at = slice(base, base + face)
        own, other = out_ref[:, at].astype(F32), other_ref[:, at].astype(F32)
        block = jnp.concatenate(
            [jnp.where(band == 0, own, other), jnp.where(band == 0, other, own)], axis=0
        ).astype(BF16)
        return lax.dot_general(
            block, block, (((1,), (1,)), ((), ())), preferred_element_type=F32
        )

    swap.wait()
    total = gram(face)
    for base in range(2 * face, count, face):
        total = total + gram(base)
    tail.wait()
    finish(y_ref[:, :face] + low_ref[...], slice(0, face))
    edge = send(out_ref.at[:, :face], other_ref.at[:, :face], sems, 3, partner)
    edge.wait()
    total = total + gram(0)
    slots_ref[me] = total

    def push(steps, carry):
        send(slots_ref.at[me], slots_ref.at[me], sems, 2, {"mesh": lax.rem(me + steps, devices)})
        return carry

    lax.fori_loop(1, devices, push, 0)
    pltpu.make_async_remote_copy(
        src_ref=slots_ref.at[pl.ds(0, devices - 1)], dst_ref=slots_ref.at[pl.ds(0, devices - 1)],
        send_sem=sems.at[0, 2], recv_sem=sems.at[1, 2], device_id=partner, device_id_type=MESH_ID,
    ).wait()
    corr_ref[...] = jnp.sum(slots_ref[...], axis=0) * (1.0 / (devices * count))


def everyone(count):
    bands = lax.axis_size("band")
    flat = lax.axis_index("mesh") * bands + lax.axis_index("band")

    def peer(steps):
        other = lax.rem(flat + steps, count)
        return {"mesh": other // bands, "band": lax.rem(other, bands)}

    return flat, peer


def halves(value, axis):
    top = value.astype(BF16)
    return jnp.concatenate([top, (value - top.astype(F32)).astype(BF16)], axis=axis)


def fused_kernel(psi_ref, cn_ref, scale_ref, kmat_ref, pot_ref, proj_ref, ecell_ref, eatom_ref,
                 coup_ref, out_ref, corr_ref, flag_ref,
                 oh_ref, oht_ref, hi_ref, pd_ref, xs_ref, ct_ref, five_ref, ys_ref, lhs_ref,
                 masked_ref, mid_ref, first_ref, potf_ref, head_ref, tail_ref, low_ref, high_ref,
                 grouped_ref, left_ref, right_ref, far_ref, ghost_ref, potg_ref, coups_ref,
                 spread_ref, other_ref, slots_ref, hot_ref, couple_ref, mate_ref, mated_ref,
                 mateh_ref, matel_ref, sems):
    states, count = psi_ref.shape
    width, cells = cn_ref.shape
    face = ghost_ref.shape[1]
    slabs = count // face
    layers = slabs + 1
    _, nproj, entries = proj_ref.shape
    atoms = coup_ref.shape[1]
    edge = slabs // 2 + 1
    group = width // edge
    pairs = cells // 2
    tiles = face // WIDE
    block = (tiles + 1) * states
    wraps = group // 2
    devices, bands = lax.axis_size("mesh"), lax.axis_size("band")
    band = lax.axis_index("band")
    me, peer = everyone(devices * bands)
    ahead, behind = {"mesh": ring_peer(1)}, {"mesh": ring_peer(-1)}
    ahead2, behind2 = {"mesh": ring_peer(2)}, {"mesh": ring_peer(-2)}
    partner = {"band": lax.rem(band + 1, bands)}
    ahead_mate = {"mesh": ring_peer(1), "band": lax.rem(band + 1, bands)}
    barrier = pltpu.get_barrier_semaphore()

    def greet_body(steps, carry):
        pl.semaphore_signal(barrier, inc=1, device_id=peer(steps), device_id_type=MESH_ID)
        return carry

    lax.fori_loop(1, devices * bands, greet_body, 0)
    coups_ref[1] = jnp.concatenate([coup_ref[...]] * 2, axis=1)
    pl.semaphore_wait(barrier, devices * bands - 1)
    gaps = [
        send(psi_ref.at[:, :face], ghost_ref, sems, 0, behind),
        send(pot_ref.at[:potg_ref.shape[0], :], potg_ref, sems, 1, behind),
        send(coups_ref.at[1], coups_ref.at[0], sems, 2, ahead),
        send(coups_ref.at[1], coups_ref.at[2], sems, 3, behind),
        send(psi_ref.at[:, :face], mate_ref, sems, 18, partner),
    ]

    down = lax.broadcasted_iota(jnp.int32, (cells, cells), 0)
    across = lax.broadcasted_iota(jnp.int32, (cells, cells), 1)
    eye = down == across
    key = jnp.broadcast_to(cn_ref[0:1, :].astype(F32), (cells, cells))
    key_col = jnp.sum(jnp.where(eye, key, 0.0), axis=1, keepdims=True)
    rank = jnp.sum(jnp.where(key < key_col, 1.0, 0.0), axis=1, keepdims=True)
    chosen_cell = rank == across.astype(F32)
    order = jnp.where(chosen_cell, 1.0, 0.0).astype(BF16)
    scale_col = jnp.sum(
        jnp.where(eye, jnp.broadcast_to(scale_ref[...], (cells, cells)), 0.0), axis=1, keepdims=True
    )
    scale = jnp.sum(jnp.where(chosen_cell, scale_col, 0.0), axis=0, keepdims=True)
    entry_rank = jnp.sum(
        jnp.where(lax.broadcasted_iota(jnp.int32, (cells, entries), 0) == ecell_ref[...], rank, 0.0),
        axis=0, keepdims=True,
    )
    spread = jnp.where(
        lax.broadcasted_iota(jnp.int32, (cells, entries), 0).astype(F32) == entry_rank, 1.0, 0.0
    )
    spread_ref[...] = spread.astype(BF16)
    table = cn_ref[...]
    upper = lax.shift_right_logical(table, 8).astype(F32)
    lower = jnp.bitwise_and(table, WIDE - 1).astype(F32)
    table = WIDE * jnp.dot(upper.astype(BF16), order, preferred_element_type=F32) + jnp.dot(
        lower.astype(BF16), order, preferred_element_type=F32
    )
    low_half = lax.broadcasted_iota(jnp.int32, (1, cells), 1) < pairs
    base = table[:group]
    base = jnp.where(low_half, base, pltpu.roll(base, pairs, 1))
    lift = jnp.where(low_half, 0.0, float((edge - 1) * face))
    wrong = jnp.where((base < 0.0) | (base >= float(face)), 1.0, 0.0)
    for a in range(edge):
        expected = base + (lift + float(a * face))
        wrong = jnp.maximum(
            wrong, jnp.where(table[a * group:(a + 1) * group] == expected, 0.0, 1.0)
        )
    flag_ref[0, 0] = jnp.max(wrong)
    pd_ref[:group, :] = base
    places = jnp.where(
        low_half, pd_ref[pl.ds(0, wraps, stride=2), :], pd_ref[pl.ds(1, wraps, stride=2), :]
    ).astype(jnp.int32)
    slot = jnp.bitwise_and(places, WIDE - 1)
    hi_ref[:wraps, :] = lax.shift_right_logical(places, 8)
    wide_ids = lax.broadcasted_iota(jnp.int16, (WIDE, cells), 0)
    one, zero = jnp.array(1.0, BF16), jnp.array(0.0, BF16)
    for w in range(wraps):
        hot = jnp.where(wide_ids == slot[w:w + 1, :].astype(jnp.int16), one, zero)
        oh_ref[:, w * cells:(w + 1) * cells] = hot
        oht_ref[w * cells:(w + 1) * cells, :] = hot.T

    for w in range(wraps):
        hi = jnp.broadcast_to(hi_ref[w:w + 1, :], (2 * states, cells))
        for t in range(tiles):
            hot_ref[t * 2 * states:(t + 1) * 2 * states, w * cells:(w + 1) * cells] = (
                jnp.where(hi == t, 1.0, 0.0).astype(BF16)
            )
    rows128 = face // 128
    potf_ref[:slabs * rows128, :] = pot_ref[...].astype(F32) - CENTER

    def place(layer):
        if isinstance(layer, int):
            return 0 if layer == 0 else 1 if layer == slabs else layer + 1
        return layer + 1

    def put(layer, blocks):
        both = jnp.concatenate(blocks + [blocks[-1]], axis=0).astype(BF16)
        start = place(layer) * block
        if not isinstance(layer, int):
            start = pl.multiple_of(start, block)
        lhs_ref[pl.ds(start, block), :] = both

    def put_psi(layer, source, at):
        put(layer, [
            source[:, pl.ds(pl.multiple_of(at + t * WIDE, WIDE), WIDE)].astype(F32)
            for t in range(tiles)
        ])

    def psi_body(layer, carry):
        put_psi(layer, psi_ref, layer * face)
        return carry

    put_psi(0, psi_ref, 0)
    lax.fori_loop(1, slabs, psi_body, 0)

    def gather(first_row, chosen, finish):
        rows = len(chosen) * block
        trip = wraps // 3

        def body(n, carry):
            hot = oh_ref[:, pl.ds(pl.multiple_of(n * trip * cells, trip * cells), trip * cells)]
            out = jnp.dot(lhs_ref[first_row:first_row + rows, :], hot, preferred_element_type=F32)
            for c in range(trip):
                w = n * trip + c
                hi = jnp.broadcast_to(hi_ref[pl.ds(w, 1), :], (states, cells))
                masks = [hi == t for t in range(1, tiles)]
                found = {}
                for k, layer in enumerate(chosen):
                    part = out[k * block:(k + 1) * block, c * cells:(c + 1) * cells]
                    value = part[:states]
                    for t in range(1, tiles):
                        value = jnp.where(
                            masks[t - 1], part[t * states:(t + 1) * states], value
                        )
                    found[layer] = value
                finish(w, found)
            return carry

        lax.fori_loop(0, 3, body, 0)

    def store_pair(a, w, lower_cells, upper_cells):
        mixed = pltpu.roll(jnp.where(low_half, upper_cells, lower_cells), pairs, 1)
        at = pl.multiple_of((a * group + 2 * w) * states, 2 * states)
        xs_ref[pl.ds(at, states), :] = jnp.where(low_half, lower_cells, mixed)
        xs_ref[pl.ds(at + states, states), :] = jnp.where(low_half, mixed, upper_cells)

    def inner_found(w, found):
        for a in range(1, edge - 1):
            store_pair(a, w, found[a], found[edge - 1 + a])
        five_ref[pl.ds(pl.multiple_of(w * states, states), states), :] = found[edge - 1]

    def outer_found(w, found):
        middle = five_ref[pl.ds(pl.multiple_of(w * states, states), states), :]
        store_pair(0, w, found[0], middle)
        store_pair(edge - 1, w, middle, found[slabs])

    def gather_inner():
        gather(2 * block, tuple(range(1, slabs)), inner_found)

    def gather_outer():
        gather(0, (0, slabs), outer_found)

    def partial_body(a, accs):
        at = pl.multiple_of(a * group * states, group * states)
        values = jnp.dot(
            xs_ref[pl.ds(at, group * states), :].astype(BF16), spread_ref[...],
            preferred_element_type=F32,
        )
        accs = list(accs)
        for j in range(group):
            proj = proj_ref[a * group + j].astype(F32)
            value = values[j * states:(j + 1) * states]
            for k in range(nproj):
                accs[k] = accs[k] + proj[k:k + 1, :] * value
        return tuple(accs)

    slot_ids = lax.broadcasted_iota(jnp.int32, (4 * atoms, entries), 0)
    chosen_atom = jnp.where(slot_ids == eatom_ref[...], 1.0, 0.0).astype(BF16)
    chosen_send = jnp.concatenate(
        [chosen_atom[:2 * atoms], chosen_atom[atoms:3 * atoms], chosen_atom[2 * atoms:3 * atoms],
         chosen_atom[:atoms]], axis=0,
    )
    back = (((1,), (1,)), ((), ()))
    empty = tuple(jnp.zeros((states, entries), F32) for _ in range(nproj))
    low_atoms = lax.broadcasted_iota(jnp.int32, (1, 2 * atoms), 1) < atoms

    def send_atoms(step, accs):
        grouped = lax.dot_general(
            halves(jnp.concatenate(accs, axis=0), 1),
            jnp.concatenate([chosen_send, chosen_send], axis=1),
            back, preferred_element_type=F32,
        )
        for g in range(3):
            grouped_ref[step, g] = grouped[:, 2 * g * atoms:2 * (g + 1) * atoms]
        at = 4 + 6 * step
        return [
            send(grouped_ref.at[step, 1], left_ref.at[step], sems, at, ahead),
            send(grouped_ref.at[step, 0], right_ref.at[step], sems, at + 1, behind),
            send(grouped_ref.at[step, 2], far_ref.at[step, 0], sems, at + 2, ahead2),
            send(grouped_ref.at[step, 2], far_ref.at[step, 1], sems, at + 3, behind2),
        ]

    def cell_terms():
        kmat = kmat_ref[...]
        for s in range(0, states, 2):
            pair = jnp.concatenate(
                [xs_ref[pl.ds(s, width, stride=states), :],
                 xs_ref[pl.ds(s + 1, width, stride=states), :]], axis=1,
            ).astype(BF16)
            out = jnp.dot(kmat, pair, preferred_element_type=F32)
            ct_ref[pl.ds(s, width, stride=states), :] = out[:, :cells] * scale
            ct_ref[pl.ds(s + 1, width, stride=states), :] = out[:, cells:] * scale

    def node_stage(step):
        right = pltpu.roll(right_ref[step], atoms, 1)
        coef = (
            grouped_ref[step, 0] + left_ref[step]
            + jnp.where(low_atoms, far_ref[step, 0], right),
            grouped_ref[step, 2] + right + pltpu.roll(far_ref[step, 1], atoms, 1),
        )
        rows = []
        for c in range(2):
            parts = []
            for k in range(nproj):
                acc = jnp.zeros((states, 2 * atoms), F32)
                for l in range(nproj):
                    at = k * nproj + l
                    acc = acc + (
                        couple_ref[c, at:at + 1, :] * coef[c][l * states:(l + 1) * states, :]
                    )
                parts.append(acc)
            rows.append(halves(jnp.concatenate(parts, axis=0), 1))
        half_atoms = [chosen_atom[:2 * atoms]] * 2 + [chosen_atom[2 * atoms:]] * 2
        terms = jnp.dot(
            jnp.concatenate(rows, axis=1), jnp.concatenate(half_atoms, axis=0),
            preferred_element_type=F32,
        )
        terms = [terms[k * states:(k + 1) * states] for k in range(nproj)]
        ys_ref[...] = jnp.zeros_like(ys_ref)
        twice = jnp.concatenate([spread_ref[...], spread_ref[...]], axis=1)

        def body(a, carry):
            parts = []
            for j in range(group):
                proj = proj_ref[a * group + j].astype(F32)
                total = proj[0:1, :] * terms[0]
                for k in range(1, nproj):
                    total = total + proj[k:k + 1, :] * terms[k]
                parts.append(total)
            at = pl.multiple_of(a * group * states, group * states)
            value = ct_ref[pl.ds(at, group * states), :] + lax.dot_general(
                halves(jnp.concatenate(parts, axis=0), 1), twice, back, preferred_element_type=F32
            )
            for w in range(wraps):
                even = value[2 * w * states:(2 * w + 1) * states]
                odd = value[(2 * w + 1) * states:(2 * w + 2) * states]
                mixed = pltpu.roll(jnp.where(low_half, odd, even), pairs, 1)
                here = pl.multiple_of((a * wraps + w) * states, states)
                there = pl.multiple_of(((a + edge - 1) * wraps + w) * states, states)
                ys_ref[pl.ds(here, states), :] += jnp.where(low_half, even, mixed)
                ys_ref[pl.ds(there, states), :] += jnp.where(low_half, mixed, odd)
            return carry

        lax.fori_loop(0, edge, body, 0)

    def fill_masked(first, last):
        for w in range(wraps):
            for layer in range(first, last):
                at = (layer * wraps + w) * states
                both = halves(ys_ref[at:at + states, :], 0)
                for t in range(tiles):
                    rows = (layer * tiles + t) * 2 * states
                    masked_ref[rows:rows + 2 * states, w * cells:(w + 1) * cells] = (
                        both * hot_ref[t * 2 * states:(t + 1) * 2 * states,
                                       w * cells:(w + 1) * cells]
                    )

    per = tiles * 2 * states

    def joined(value, t):
        return value[t * 2 * states:t * 2 * states + states] + (
            value[t * 2 * states + states:(t + 1) * 2 * states]
        )

    def scatter_outer(step):
        for layer, into in ((0, head_ref.at[step]), (slabs, tail_ref.at[step])):
            out = jnp.dot(
                masked_ref[layer * per:(layer + 1) * per, :], oht_ref[...],
                preferred_element_type=F32,
            )
            for t in range(tiles):
                into[:, t * WIDE:(t + 1) * WIDE] = joined(out, t)

    def scatter_inner():
        mid_ref[...] = jnp.dot(
            masked_ref[per:slabs * per, :], oht_ref[...], preferred_element_type=F32
        )

    def pot_row(layer, t, half):
        row = layer * rows128 + t * 2 + half
        return potf_ref[pl.ds(row, 1), :]

    def scaled(layer, t, summed, field):
        pot = jnp.concatenate([pot_row(layer, t, 0), pot_row(layer, t, 1)], axis=1)
        return (summed + pot * field) * (1.0 / HALFWIDTH)

    def lanes(layer, t):
        at = layer * face + t * WIDE
        return pl.ds(at if isinstance(layer, int) else pl.multiple_of(at, WIDE), WIDE)

    def first_layer(layer, summed, field):
        blocks = []
        for t in range(tiles):
            value = scaled(layer, t, summed(t), field(t)).astype(BF16).astype(F32)
            first_ref[:, lanes(layer, t)] = value
            blocks.append(value)
        put(layer, blocks)

    def last_layer(layer, summed):
        for t in range(tiles):
            value = scaled(layer, t, summed(t), first_ref[:, lanes(layer, t)])
            at = lanes(layer, t)
            out_ref[:, at] = (2.0 * value - psi_ref[:, at].astype(F32)).astype(BF16)

    def mid_sum(layer):
        def summed(t):
            at = pl.multiple_of((layer - 1) * per + t * 2 * states, 2 * states)
            return mid_ref[pl.ds(at, states), :] + mid_ref[pl.ds(at + states, states), :]
        return summed

    def edge_sum(one_ref, two_ref):
        return lambda t: (
            one_ref[:, t * WIDE:(t + 1) * WIDE] + two_ref[:, t * WIDE:(t + 1) * WIDE]
        )

    gather_inner()
    accs = lax.fori_loop(1, edge - 1, partial_body, empty)
    for copy in gaps:
        copy.wait()
    couple_ref[0] = jnp.where(low_atoms, coups_ref[0], coups_ref[1])
    couple_ref[1] = coups_ref[2]
    potf_ref[slabs * rows128:slabs * rows128 + potg_ref.shape[0], :] = (
        potg_ref[...].astype(F32) - CENTER
    )
    put_psi(slabs, ghost_ref, 0)
    gather_outer()
    for a in (0, edge - 1):
        accs = partial_body(a, accs)
    copies = send_atoms(0, accs)
    cell_terms()
    for copy in copies:
        copy.wait()
    node_stage(0)
    fill_masked(0, 1)
    fill_masked(slabs, layers)
    scatter_outer(0)
    copies = [
        send(tail_ref.at[0], low_ref.at[0], sems, 8, ahead),
        send(head_ref.at[0], high_ref, sems, 9, behind),
    ]
    fill_masked(1, slabs)
    scatter_inner()

    def first_body(layer, carry):
        first_layer(
            layer, mid_sum(layer), lambda t: psi_ref[:, lanes(layer, t)].astype(F32)
        )
        return carry

    lax.fori_loop(1, slabs, first_body, 0)
    gather_inner()
    accs = lax.fori_loop(1, edge - 1, partial_body, empty)
    for copy in copies:
        copy.wait()
    first_layer(0, edge_sum(head_ref.at[0], low_ref.at[0]), lambda t: psi_ref[:, lanes(0, t)].astype(F32))
    first_layer(
        slabs, edge_sum(tail_ref.at[0], high_ref),
        lambda t: ghost_ref[:, t * WIDE:(t + 1) * WIDE].astype(F32),
    )
    mated = [send(first_ref.at[:, :face], mated_ref, sems, 20, partner)]
    gather_outer()
    for a in (0, edge - 1):
        accs = partial_body(a, accs)
    copies = send_atoms(1, accs)
    cell_terms()
    for copy in copies:
        copy.wait()
    node_stage(1)
    fill_masked(0, 1)
    fill_masked(slabs, layers)
    scatter_outer(1)
    tails = [
        send(tail_ref.at[1], low_ref.at[1], sems, 14, ahead),
        send(tail_ref.at[1], matel_ref, sems, 16, ahead_mate),
        send(head_ref.at[1], mateh_ref, sems, 19, partner),
    ]
    fill_masked(1, slabs)
    scatter_inner()

    def last_body(layer, carry):
        last_layer(layer, mid_sum(layer))
        return carry

    lax.fori_loop(1, slabs, last_body, 0)
    half = slabs // 2
    kept = half - 1
    mine = jnp.where(band == 0, 1, half) * face
    theirs = jnp.where(band == 0, half, 1) * face

    def span(at, size):
        return pl.ds(pl.multiple_of(at, 128), size)

    swap = send(out_ref.at[:, span(theirs, half * face)], other_ref, sems, 15, partner)

    def gram(own, other):
        both = jnp.concatenate(
            [jnp.where(band == 0, own, other), jnp.where(band == 0, other, own)], axis=0
        ).astype(BF16)
        return lax.dot_general(both, both, back, preferred_element_type=F32)

    swap.wait()
    total = jnp.zeros((bands * states, bands * states), F32)
    for n in range(kept):
        total = total + gram(
            out_ref[:, span(mine + n * face, face)].astype(F32),
            other_ref[:, n * face:(n + 1) * face].astype(F32),
        )
    for copy in tails + mated:
        copy.wait()
    last_layer(0, edge_sum(head_ref.at[1], low_ref.at[1]))
    blocks = []
    summed = edge_sum(mateh_ref, matel_ref)
    for t in range(tiles):
        at = slice(t * WIDE, (t + 1) * WIDE)
        value = scaled(0, t, summed(t), mated_ref[:, at])
        value = (2.0 * value - mate_ref[:, at].astype(F32)).astype(BF16).astype(F32)
        blocks.append(jnp.where(band == 0, value, other_ref[:, span(kept * face + t * WIDE, WIDE)].astype(F32)))
    total = total + gram(
        out_ref[:, span(jnp.where(band == 0, 0, slabs - 1) * face, face)].astype(F32),
        jnp.concatenate(blocks, axis=1),
    )
    size = bands * states
    lump = size * size // 128
    pieces = size // lump
    slots_ref[me] = jnp.concatenate(
        [total[r * lump:(r + 1) * lump] for r in range(pieces)], axis=1
    )

    def push(steps, carry):
        send(slots_ref.at[me], slots_ref.at[me], sems, 17, peer(steps))
        return carry

    lax.fori_loop(1, devices * bands, push, 0)
    rest = pl.ds(0, devices * bands - 1)
    pltpu.make_async_remote_copy(
        src_ref=slots_ref.at[rest], dst_ref=slots_ref.at[rest], send_sem=sems.at[0, 17],
        recv_sem=sems.at[1, 17], device_id=partner, device_id_type=MESH_ID,
    ).wait()
    total = jnp.sum(slots_ref[...], axis=0) * (1.0 / (devices * count))
    corr_ref[...] = jnp.concatenate(
        [total[:, r * size:(r + 1) * size] for r in range(pieces)], axis=0
    )


def general(
    psi,
    cell_nodes,
    cell_scale,
    cell_matrix,
    node_potential,
    proj_values,
    entry_cell,
    entry_atom,
    coupling,
):
    states, node_count = psi.shape
    width, cells = cell_nodes.shape
    atoms, nproj, _ = coupling.shape
    entries = entry_atom.shape[0]
    full = node_count + FACEP
    chunks = full // FACEP
    layers = FACEP // WIDE
    groups = width // GROUP
    span = GROUP * cells

    table = cell_nodes.reshape(groups, GROUP, cells)
    owner = table // FACEP
    ids = jnp.arange(chunks, dtype=jnp.int32)
    flags = jnp.max(
        (owner[:, None] == ids[None, :, None, None]).astype(jnp.int32), axis=(2, 3)
    )
    rank = jnp.sum(flags[:, None, :] * (ids[None, :] < ids[:, None]), axis=2)
    places = jnp.arange(chunks + 1, dtype=jnp.int32)
    used = flags[:, :, None] * (rank[:, :, None] == places)
    listed = chunks + jnp.sum(used * (ids[None, :, None] - chunks), axis=1)
    listed = jnp.concatenate(
        [listed, jnp.full((groups, 1), chunks, jnp.int32), jnp.sum(flags, axis=1, keepdims=True)],
        axis=1,
    )
    sched = listed.astype(jnp.int32).reshape(groups * (chunks + 3))
    scale_row = cell_scale.reshape(1, cells)
    ecell = entry_cell.reshape(1, entries)
    eatom = entry_atom.reshape(1, entries)
    coup = coupling.transpose(1, 2, 0).reshape(nproj * nproj, atoms)
    potential = node_potential.astype(F32).reshape(1, node_count) - CENTER

    vmem = pl.BlockSpec(memory_space=pltpu.VMEM)
    smem = pl.BlockSpec(memory_space=pltpu.SMEM)

    padded = (layers * states + 15) // 16 * 16
    gather = pl.pallas_call(
        gather_kernel,
        out_shape=jax.ShapeDtypeStruct((width * states, cells), F32),
        in_specs=[smem] + [vmem] * 2,
        out_specs=vmem,
        scratch_shapes=[
            pltpu.VMEM((chunks + 1, padded, WIDE), BF16),
            pltpu.VMEM((WIDE, span), BF16),
        ],
        name="gather_cells",
    )
    scatter = pl.pallas_call(
        scatter_kernel,
        out_shape=jax.ShapeDtypeStruct((states, full), F32),
        in_specs=[smem] + [vmem] * 7,
        out_specs=vmem,
        scratch_shapes=[
            pltpu.VMEM((WIDE, span), BF16),
            pltpu.VMEM((width * states, entries), F32),
            pltpu.VMEM((width * states, cells), F32),
            pltpu.VMEM((2 * layers * 2 * states, span), BF16),
            pltpu.VMEM((chunks + 1, layers * 2 * states, WIDE), F32),
        ],
        name="scatter_nodes",
    )

    def remote(kernel, outs, n_in, scratch, copies, ident):
        return pl.pallas_call(
            kernel,
            out_shape=tuple(jax.ShapeDtypeStruct(*out) for out in outs),
            in_specs=[vmem] * n_in,
            out_specs=(vmem,) * len(outs),
            scratch_shapes=[pltpu.VMEM(*one) for one in scratch]
            + [pltpu.SemaphoreType.DMA((2, copies))],
            compiler_params=pltpu.CompilerParams(collective_id=ident, has_side_effects=True),
            name=kernel.__name__,
        )

    pair = (nproj * states, atoms)

    def assemble(extended, ident):
        values = gather(sched, table, extended)
        cell_terms, coef = remote(
            atoms_kernel, [((width * states, cells), F32), ((3,) + pair, F32)], 6,
            [((width * states, entries), F32), ((3,) + pair, F32)] + [((2,) + pair, F32)] * 3,
            4, ident,
        )(values, cell_matrix, scale_row, proj_values, ecell, eatom)
        return scatter(sched, table, cell_terms, coef, coup_all, proj_values, ecell, eatom)

    psi_ext, pot_ext, coup_all = remote(
        start_kernel,
        [((states, full), BF16), ((1, full), F32), ((3, nproj * nproj, atoms), F32)],
        3, [], 4, 1,
    )(psi, potential, coup)
    face = (states, FACEP)
    (first,) = remote(first_kernel, [((states, full), BF16)], 3, [(face, F32), (face, F32)], 2, 3)(
        assemble(psi_ext, 2), psi_ext, pot_ext
    )
    bands, devices = lax.axis_size("band"), lax.axis_size("mesh")
    square = (bands * states, bands * states)
    filtered, correlation = remote(
        last_kernel,
        [((states, node_count), BF16), (square, F32)],
        4,
        [(face, F32), ((states, node_count), BF16), ((devices,) + square, F32)],
        4, 5,
    )(assemble(first, 4), first, psi, potential)
    return (filtered, correlation)


def bricks(states, node_count, width, cells, bands):
    edge = round(width ** (1.0 / 3.0))
    return (
        edge ** 3 == width
        and (edge - 1) * 2 * FACEP == node_count
        and edge % 2 == 0
        and cells == 128
        and FACEP % WIDE == 0
        and states == 8
        and bands == 2
        and edge * edge % 6 == 0
    )


def local(
    psi,
    cell_nodes,
    cell_scale,
    cell_matrix,
    node_potential,
    proj_values,
    entry_cell,
    entry_atom,
    coupling,
):
    states, node_count = psi.shape
    width, cells = cell_nodes.shape
    atoms, nproj, _ = coupling.shape
    entries = entry_atom.shape[0]
    bands, devices = lax.axis_size("band"), lax.axis_size("mesh")
    operands = (
        psi, cell_nodes, cell_scale, cell_matrix, node_potential, proj_values, entry_cell,
        entry_atom, coupling,
    )
    if not bricks(states, node_count, width, cells, bands):
        return general(*operands)
    edge = round(width ** (1.0 / 3.0))
    wraps = edge * edge // 2
    layers = node_count // FACEP + 1
    tiles = FACEP // WIDE
    block = (tiles + 1) * states
    per = tiles * 2 * states
    rows = node_count // 128
    ghost_rows = (FACEP // 128 + 15) // 16 * 16
    size = bands * states
    vmem = pl.BlockSpec(memory_space=pltpu.VMEM)
    smem = pl.BlockSpec(memory_space=pltpu.SMEM)
    face = (states, FACEP)
    duo = (nproj * states, 2 * atoms)
    filtered, correlation, wrong = pl.pallas_call(
        fused_kernel,
        out_shape=(
            jax.ShapeDtypeStruct((states, node_count), BF16),
            jax.ShapeDtypeStruct((size, size), F32),
            jax.ShapeDtypeStruct((1, 1), F32),
        ),
        in_specs=[vmem] * 9,
        out_specs=(vmem, vmem, smem),
        scratch_shapes=[
            pltpu.VMEM((WIDE, wraps * cells), BF16),
            pltpu.VMEM((wraps * cells, WIDE), BF16),
            pltpu.VMEM(((wraps + 7) // 8 * 8, cells), jnp.int32),
            pltpu.VMEM(((2 * wraps + 7) // 8 * 8, cells), F32),
            pltpu.VMEM((width * states, cells), F32),
            pltpu.VMEM((width * states, cells), F32),
            pltpu.VMEM((wraps * states, cells), F32),
            pltpu.VMEM((layers * wraps * states, cells), F32),
            pltpu.VMEM((layers * block, WIDE), BF16),
            pltpu.VMEM((layers * per, wraps * cells), BF16),
            pltpu.VMEM(((layers - 2) * per, WIDE), F32),
            pltpu.VMEM((states, layers * FACEP), F32),
            pltpu.VMEM((rows + ghost_rows, 128), F32),
            pltpu.VMEM((2,) + face, F32),
            pltpu.VMEM((2,) + face, F32),
            pltpu.VMEM((2,) + face, F32),
            pltpu.VMEM(face, F32),
            pltpu.VMEM((2, 3) + duo, F32),
            pltpu.VMEM((2,) + duo, F32),
            pltpu.VMEM((2,) + duo, F32),
            pltpu.VMEM((2, 2) + duo, F32),
            pltpu.VMEM(face, BF16),
            pltpu.VMEM((ghost_rows, 128), BF16),
            pltpu.VMEM((3, nproj * nproj, 2 * atoms), F32),
            pltpu.VMEM((cells, entries), BF16),
            pltpu.VMEM((states, node_count // 2), BF16),
            pltpu.VMEM((devices * bands, size * size // 128, 128), F32),
            pltpu.VMEM((per, wraps * cells), BF16),
            pltpu.VMEM((2, nproj * nproj, 2 * atoms), F32),
            pltpu.VMEM(face, BF16),
            pltpu.VMEM(face, F32),
            pltpu.VMEM(face, F32),
            pltpu.VMEM(face, F32),
            pltpu.SemaphoreType.DMA((2, 21)),
        ],
        compiler_params=pltpu.CompilerParams(collective_id=0, has_side_effects=True),
        name="fused_steps",
    )(
        psi, cell_nodes, cell_scale.reshape(1, cells), cell_matrix,
        node_potential.reshape(rows, 128), proj_values, entry_cell.reshape(1, entries),
        entry_atom.reshape(1, entries),
        coupling.transpose(1, 2, 0).reshape(nproj * nproj, atoms),
    )
    return lax.cond(
        wrong[0, 0] > 0.0,
        lambda: general(*operands),
        lambda: (filtered, correlation),
    )


def solution(mesh):
    return jax.shard_map(
        local,
        mesh=mesh,
        in_specs=(
            P("band", "mesh"),
            P(),
            P("mesh"),
            P(),
            P("mesh"),
            P(None, None, "mesh"),
            P("mesh"),
            P("mesh"),
            P("mesh", None, None),
        ),
        out_specs=(P("band", "mesh"), P()),
        check_vma=False,
    )
```

```python
import jax
import jax.numpy as jnp
from jax import lax
from jax.experimental import pallas as pl
from jax.experimental.pallas import tpu as pltpu
from jax.sharding import PartitionSpec as P

FACEP = 1792
CENTER = 0.5
HALFWIDTH = 2.5
HIGH = lax.Precision.HIGHEST
WIDE = 256
GROUP = 36
F32 = jnp.float32
BF16 = jnp.bfloat16


def fill_onehot(cn_ref, group, oh_ref):
    rows = cn_ref[group]
    hi = jnp.bitwise_and(rows, WIDE - 1)
    lanes = rows.shape[1]
    iota = lax.broadcasted_iota(jnp.int32, (WIDE, lanes), 0)
    for jj in range(GROUP):
        oh_ref[:, jj * lanes:(jj + 1) * lanes] = jnp.where(
            iota == hi[jj:jj + 1, :], 1.0, 0.0
        ).astype(BF16)
    return lax.shift_right_logical(rows, 8)


def gather_kernel(sched_ref, cn_ref, ext_ref, xs_ref, lhs_ref, oh_ref):
    states = ext_ref.shape[0]
    chunks = lhs_ref.shape[0] - 1
    layers = ext_ref.shape[1] // (chunks * WIDE)
    groups = cn_ref.shape[0]
    cells = cn_ref.shape[2]
    padded = lhs_ref.shape[1]
    slots = sched_ref.shape[0] // groups
    lhs_ref[...] = jnp.zeros_like(lhs_ref)
    for c in range(chunks):
        base = c * layers * WIDE
        parts = [
            ext_ref[:, base + l * WIDE:base + (l + 1) * WIDE].astype(F32) for l in range(layers)
        ]
        parts.append(jnp.zeros((padded - layers * states, WIDE), F32))
        lhs_ref[c] = jnp.concatenate(parts, axis=0).astype(BF16)
    xs_ref[...] = jnp.zeros_like(xs_ref)

    def group_body(g, carry):
        lo = fill_onehot(cn_ref, g, oh_ref)

        def pair_body(r, inner):
            first = sched_ref[g * slots + 2 * r]
            second = sched_ref[g * slots + 2 * r + 1]
            lhs = jnp.concatenate([lhs_ref[first], lhs_ref[second]], axis=0)
            out = jnp.dot(lhs, oh_ref[...], preferred_element_type=F32)
            for jj in range(GROUP):
                where = pl.ds(pl.multiple_of((g * GROUP + jj) * states, states), states)
                value = xs_ref[where, :]
                lanes = slice(jj * cells, (jj + 1) * cells)
                for half, chunk in enumerate((first, second)):
                    row = lo[jj:jj + 1, :] - chunk * layers
                    for l in range(layers):
                        at = half * padded + l * states
                        value = jnp.where(row == l, out[at:at + states, lanes], value)
                xs_ref[where, :] = value
            return inner

        pairs = lax.shift_right_logical(sched_ref[g * slots + slots - 1] + 1, 1)
        return lax.fori_loop(0, pairs, pair_body, carry)

    lax.fori_loop(0, groups, group_body, 0)


def scatter_kernel(sched_ref, cn_ref, ct_ref, coef_ref, coup_ref, proj_ref, ecell_ref,
                   eatom_ref, y_ref, oh_ref, ns_ref, v_ref, lhs_ref, acc_ref):
    chunks, rows_in_chunk, _ = acc_ref.shape
    chunks = chunks - 1
    groups = cn_ref.shape[0]
    cells = cn_ref.shape[2]
    width = groups * GROUP
    states = ct_ref.shape[0] // width
    layers = rows_in_chunk // (2 * states)
    nproj = proj_ref.shape[1]
    entries = ecell_ref.shape[1]
    atoms = coef_ref.shape[2]
    slot_ids = lax.broadcasted_iota(jnp.int32, (atoms, entries), 0)
    entry_terms = jnp.zeros((nproj * states, entries), F32)
    for g in range(3):
        rows = []
        for k in range(nproj):
            acc = jnp.zeros((states, atoms), F32)
            for l in range(nproj):
                acc = acc + (
                    coup_ref[g, k * nproj + l:k * nproj + l + 1, :]
                    * coef_ref[g, l * states:(l + 1) * states, :]
                )
            rows.append(acc)
        chosen = jnp.where(eatom_ref[...] == slot_ids + g * atoms, 1.0, 0.0)
        entry_terms = entry_terms + jnp.dot(
            jnp.concatenate(rows, axis=0), chosen, precision=HIGH, preferred_element_type=F32
        )
    terms = [entry_terms[k * states:(k + 1) * states, :] for k in range(nproj)]

    def node_body(j, carry):
        proj = proj_ref[j].astype(F32)
        total = proj[0:1, :] * terms[0]
        for k in range(1, nproj):
            total = total + proj[k:k + 1, :] * terms[k]
        ns_ref[pl.ds(pl.multiple_of(j * states, states), states), :] = total
        return carry

    lax.fori_loop(0, width, node_body, 0, unroll=8)
    cell_ids = lax.broadcasted_iota(jnp.int32, (cells, entries), 0)
    spread = jnp.where(cell_ids == ecell_ref[...], 1.0, 0.0).astype(BF16)
    back = (((1,), (1,)), ((), ()))
    node_vals = ns_ref[...]
    node_top = node_vals.astype(BF16)
    node_rest = (node_vals - node_top.astype(F32)).astype(BF16)
    v_ref[...] = (
        ct_ref[...]
        + lax.dot_general(node_top, spread, back, preferred_element_type=F32)
        + lax.dot_general(node_rest, spread, back, preferred_element_type=F32)
    )
    acc_ref[...] = jnp.zeros_like(acc_ref)
    slots = sched_ref.shape[0] // groups

    def group_body(g, carry):
        lo = fill_onehot(cn_ref, g, oh_ref)

        def pair_body(r, inner):
            first = sched_ref[g * slots + 2 * r]
            second = sched_ref[g * slots + 2 * r + 1]
            for jj in range(GROUP):
                start = pl.multiple_of((g * GROUP + jj) * states, states)
                value = v_ref[pl.ds(start, states), :]
                top = value.astype(BF16).astype(F32)
                both = jnp.concatenate([top, value - top], axis=0)
                lanes = slice(jj * cells, (jj + 1) * cells)
                for half, chunk in enumerate((first, second)):
                    row = lo[jj:jj + 1, :] - chunk * layers
                    for l in range(layers):
                        at = half * rows_in_chunk + l * 2 * states
                        lhs_ref[at:at + 2 * states, lanes] = (
                            jnp.where(row == l, both, 0.0).astype(BF16)
                        )
            out = lax.dot_general(lhs_ref[...], oh_ref[...], back, preferred_element_type=F32)
            acc_ref[first] += out[:rows_in_chunk]
            acc_ref[second] += out[rows_in_chunk:]
            return inner

        pairs = lax.shift_right_logical(sched_ref[g * slots + slots - 1] + 1, 1)
        return lax.fori_loop(0, pairs, pair_body, carry)

    lax.fori_loop(0, groups, group_body, 0)
    for c in range(chunks):
        for l in range(layers):
            base = (c * layers + l) * WIDE
            at = l * 2 * states
            y_ref[:, base:base + WIDE] = (
                acc_ref[c, at:at + states, :] + acc_ref[c, at + states:at + 2 * states, :]
            )


MESH_ID = pl.DeviceIdType.MESH


def ring_peer(steps):
    count = lax.axis_size("mesh")
    return lax.rem(lax.axis_index("mesh") + steps + count, count)


def send(src, dst, sems, at, peer):
    copy = pltpu.make_async_remote_copy(
        src_ref=src, dst_ref=dst, send_sem=sems.at[0, at], recv_sem=sems.at[1, at],
        device_id=peer, device_id_type=MESH_ID,
    )
    copy.start()
    return copy


def greet(peers):
    barrier = pltpu.get_barrier_semaphore()
    for peer in peers:
        pl.semaphore_signal(barrier, inc=1, device_id=peer, device_id_type=MESH_ID)
    return barrier


def start_kernel(psi_ref, pot_ref, coup_ref, ext_ref, potx_ref, coups_ref, sems):
    count = psi_ref.shape[1]
    face = ext_ref.shape[1] - count
    ahead, behind = {"mesh": ring_peer(1)}, {"mesh": ring_peer(-1)}
    pl.semaphore_wait(greet((ahead, behind)), 2)
    copies = [
        send(psi_ref.at[:, :face], ext_ref.at[:, count:], sems, 0, behind),
        send(coup_ref, coups_ref.at[0], sems, 1, ahead),
        send(coup_ref, coups_ref.at[2], sems, 2, behind),
        send(pot_ref.at[:, :face], potx_ref.at[:, count:], sems, 3, behind),
    ]
    ext_ref[:, :count] = psi_ref[...]
    potx_ref[:, :count] = pot_ref[...]
    coups_ref[1] = coup_ref[...]
    for copy in copies:
        copy.wait()


def atoms_kernel(xs_ref, kmat_ref, scale_ref, proj_ref, ecell_ref, eatom_ref, ct_ref, coef_ref,
                 es_ref, grouped_ref, left_ref, right_ref, far_ref, sems):
    peers = [{"mesh": ring_peer(steps)} for steps in (1, -1, 2, -2)]
    barrier = greet(peers)
    width, nproj, entries = proj_ref.shape
    cells = xs_ref.shape[1]
    states = xs_ref.shape[0] // width
    cell_ids = lax.broadcasted_iota(jnp.int32, (cells, entries), 0)
    spread = jnp.where(cell_ids == ecell_ref[...], 1.0, 0.0).astype(BF16)
    es_ref[...] = jnp.dot(xs_ref[...].astype(BF16), spread, preferred_element_type=F32)

    def partial_body(j, accs):
        values = es_ref[pl.ds(pl.multiple_of(j * states, states), states), :]
        proj = proj_ref[j].astype(F32)
        return tuple(acc + proj[k:k + 1, :] * values for k, acc in enumerate(accs))

    zero = jnp.zeros((states, entries), F32)
    accs = lax.fori_loop(0, width, partial_body, (zero,) * nproj, unroll=8)
    partial_sum = jnp.concatenate(accs, axis=0)
    atoms = grouped_ref.shape[2]
    slot_ids = lax.broadcasted_iota(jnp.int32, (atoms, entries), 0)
    for g in range(3):
        chosen = jnp.where(eatom_ref[...] == slot_ids + g * atoms, 1.0, 0.0)
        grouped_ref[g] = lax.dot_general(
            partial_sum, chosen, (((1,), (1,)), ((), ())), precision=HIGH,
            preferred_element_type=F32,
        )
    pl.semaphore_wait(barrier, 4)
    copies = [
        send(grouped_ref.at[1:3], left_ref, sems, 0, peers[0]),
        send(grouped_ref.at[0:2], right_ref, sems, 1, peers[1]),
        send(grouped_ref.at[2], far_ref.at[0], sems, 2, peers[2]),
        send(grouped_ref.at[0], far_ref.at[1], sems, 3, peers[3]),
    ]
    kmat = kmat_ref[...]
    scale = scale_ref[...]
    for s in range(0, states, 2):
        pair = jnp.concatenate(
            [xs_ref[pl.ds(s, width, stride=states), :], xs_ref[pl.ds(s + 1, width, stride=states), :]],
            axis=1,
        ).astype(BF16)
        out = jnp.dot(kmat, pair, preferred_element_type=F32)
        ct_ref[pl.ds(s, width, stride=states), :] = out[:, :cells] * scale
        ct_ref[pl.ds(s + 1, width, stride=states), :] = out[:, cells:] * scale
    for copy in copies:
        copy.wait()
    coef_ref[0] = left_ref[0] + far_ref[0] + grouped_ref[0]
    coef_ref[1] = grouped_ref[1] + left_ref[1] + right_ref[0]
    coef_ref[2] = right_ref[1] + grouped_ref[2] + far_ref[1]


def first_kernel(y_ref, ext_ref, pot_ref, first_ref, low_ref, high_ref, sems):
    full = y_ref.shape[1]
    face = low_ref.shape[1]
    count = full - face
    ahead, behind = {"mesh": ring_peer(1)}, {"mesh": ring_peer(-1)}
    barrier = greet((ahead, behind))

    def finish(total, at):
        scaled = (total + pot_ref[:, at] * ext_ref[:, at].astype(F32)) / HALFWIDTH
        first_ref[:, at] = scaled.astype(BF16)

    middle = face * (1 + (count // face - 1) // 2)
    for base in range(face, middle, face):
        at = slice(base, base + face)
        finish(y_ref[:, at], at)
    pl.semaphore_wait(barrier, 2)
    copies = [
        send(y_ref.at[:, count:], low_ref, sems, 0, ahead),
        send(y_ref.at[:, :face], high_ref, sems, 1, behind),
    ]
    for base in range(middle, count, face):
        at = slice(base, base + face)
        finish(y_ref[:, at], at)
    for copy in copies:
        copy.wait()
    finish(y_ref[:, :face] + low_ref[...], slice(0, face))
    finish(y_ref[:, count:] + high_ref[...], slice(count, full))


def last_kernel(y_ref, first_ref, psi_ref, pot_ref, out_ref, corr_ref, low_ref, other_ref,
                slots_ref, sems):
    count = psi_ref.shape[1]
    face = low_ref.shape[1]
    devices = lax.axis_size("mesh")
    bands = lax.axis_size("band")
    me = lax.axis_index("mesh")
    band = lax.axis_index("band")
    partner = {"band": lax.rem(band + 1, bands)}
    barrier = greet((partner,))

    def greet_body(steps, carry):
        pl.semaphore_signal(
            barrier, inc=1, device_id={"mesh": lax.rem(me + steps, devices)}, device_id_type=MESH_ID
        )
        return carry

    lax.fori_loop(1, devices, greet_body, 0)

    def finish(total, at):
        scaled = (total + pot_ref[:, at] * first_ref[:, at].astype(F32)) / HALFWIDTH
        out_ref[:, at] = (2.0 * scaled - psi_ref[:, at].astype(F32)).astype(BF16)

    for base in range(face, count, face):
        at = slice(base, base + face)
        finish(y_ref[:, at], at)
    pl.semaphore_wait(barrier, devices)
    tail = send(y_ref.at[:, count:count + face], low_ref, sems, 0, {"mesh": ring_peer(1)})
    swap = send(out_ref.at[:, face:], other_ref.at[:, face:], sems, 1, partner)
    states = out_ref.shape[0]

    def gram(base):
        at = slice(base, base + face)
        own, other = out_ref[:, at].astype(F32), other_ref[:, at].astype(F32)
        block = jnp.concatenate(
            [jnp.where(band == 0, own, other), jnp.where(band == 0, other, own)], axis=0
        ).astype(BF16)
        return lax.dot_general(
            block, block, (((1,), (1,)), ((), ())), preferred_element_type=F32
        )

    swap.wait()
    total = gram(face)
    for base in range(2 * face, count, face):
        total = total + gram(base)
    tail.wait()
    finish(y_ref[:, :face] + low_ref[...], slice(0, face))
    edge = send(out_ref.at[:, :face], other_ref.at[:, :face], sems, 3, partner)
    edge.wait()
    total = total + gram(0)
    slots_ref[me] = total

    def push(steps, carry):
        send(slots_ref.at[me], slots_ref.at[me], sems, 2, {"mesh": lax.rem(me + steps, devices)})
        return carry

    lax.fori_loop(1, devices, push, 0)
    pltpu.make_async_remote_copy(
        src_ref=slots_ref.at[pl.ds(0, devices - 1)], dst_ref=slots_ref.at[pl.ds(0, devices - 1)],
        send_sem=sems.at[0, 2], recv_sem=sems.at[1, 2], device_id=partner, device_id_type=MESH_ID,
    ).wait()
    corr_ref[...] = jnp.sum(slots_ref[...], axis=0) * (1.0 / (devices * count))


def everyone(count):
    bands = lax.axis_size("band")
    flat = lax.axis_index("mesh") * bands + lax.axis_index("band")

    def peer(steps):
        other = lax.rem(flat + steps, count)
        return {"mesh": other // bands, "band": lax.rem(other, bands)}

    return flat, peer


def halves(value, axis):
    top = value.astype(BF16)
    return jnp.concatenate([top, (value - top.astype(F32)).astype(BF16)], axis=axis)


def fused_kernel(psi_hbm, cn_hbm, scale_ref, kmat_hbm, pot_hbm, proj_hbm, ecell_ref, eatom_ref,
                 coup_ref, out_ref, corr_ref, flag_ref,
                 psi_ref, cn_ref, kmat_ref, pot_ref, proj_ref,
                 oh_ref, oht_ref, hi_ref, pd_ref, xs_ref, ct_ref, ends_ref, five_ref, ys_ref, lhs_ref,
                 masked_ref, first_ref, potf_ref, head_ref, tail_ref, low_ref, high_ref,
                 grouped_ref, left_ref, right_ref, far_ref, ghost_ref, potg_ref, coups_ref,
                 spread_ref, other_ref, slots_ref, hot_ref, couple_ref, mate_ref, mated_ref,
                 mateh_ref, matel_ref, projf_ref, fetch_sems, sems):
    fetches = [
        pltpu.make_async_copy(src, dst, fetch_sems.at[n])
        for n, (src, dst) in enumerate((
            (cn_hbm, cn_ref), (psi_hbm, psi_ref), (proj_hbm, proj_ref), (pot_hbm, pot_ref),
            (kmat_hbm, kmat_ref),
        ))
    ]
    for fetch in fetches:
        fetch.start()
    states, count = psi_ref.shape
    width, cells = cn_ref.shape
    face = ghost_ref.shape[1]
    slabs = count // face
    layers = slabs + 1
    _, nproj, entries = proj_ref.shape
    atoms = coup_ref.shape[1]
    edge = slabs // 2 + 1
    group = width // edge
    pairs = cells // 2
    tiles = face // WIDE
    block = (tiles + 1) * states
    wraps = group // 2
    devices, bands = lax.axis_size("mesh"), lax.axis_size("band")
    band = lax.axis_index("band")
    me, peer = everyone(devices * bands)
    ahead, behind = {"mesh": ring_peer(1)}, {"mesh": ring_peer(-1)}
    ahead2, behind2 = {"mesh": ring_peer(2)}, {"mesh": ring_peer(-2)}
    partner = {"band": lax.rem(band + 1, bands)}
    ahead_mate = {"mesh": ring_peer(1), "band": lax.rem(band + 1, bands)}
    barrier = pltpu.get_barrier_semaphore()

    def greet_body(steps, carry):
        pl.semaphore_signal(barrier, inc=1, device_id=peer(steps), device_id_type=MESH_ID)
        return carry

    lax.fori_loop(1, devices * bands, greet_body, 0)
    coups_ref[1] = jnp.concatenate([coup_ref[...]] * 2, axis=1)
    pl.semaphore_wait(barrier, devices * bands - 1)
    gaps = [
        send(psi_hbm.at[:, :face], ghost_ref, sems, 0, behind),
        send(pot_hbm.at[:potg_ref.shape[0], :], potg_ref, sems, 1, behind),
        send(coups_ref.at[1], coups_ref.at[0], sems, 2, ahead),
        send(coups_ref.at[1], coups_ref.at[2], sems, 3, behind),
        send(psi_hbm.at[:, :face], mate_ref, sems, 18, partner),
    ]

    fetches[0].wait()
    down = lax.broadcasted_iota(jnp.int32, (cells, cells), 0)
    across = lax.broadcasted_iota(jnp.int32, (cells, cells), 1)
    eye = down == across
    key = jnp.broadcast_to(cn_ref[0:1, :].astype(F32), (cells, cells))
    key_col = jnp.sum(jnp.where(eye, key, 0.0), axis=1, keepdims=True)
    rank = jnp.sum(jnp.where(key < key_col, 1.0, 0.0), axis=1, keepdims=True)
    chosen_cell = rank == across.astype(F32)
    order = jnp.where(chosen_cell, 1.0, 0.0).astype(BF16)
    scale_col = jnp.sum(
        jnp.where(eye, jnp.broadcast_to(scale_ref[...], (cells, cells)), 0.0), axis=1, keepdims=True
    )
    scale = jnp.sum(jnp.where(chosen_cell, scale_col, 0.0), axis=0, keepdims=True)
    entry_rank = jnp.sum(
        jnp.where(lax.broadcasted_iota(jnp.int32, (cells, entries), 0) == ecell_ref[...], rank, 0.0),
        axis=0, keepdims=True,
    )
    spread = jnp.where(
        lax.broadcasted_iota(jnp.int32, (cells, entries), 0).astype(F32) == entry_rank, 1.0, 0.0
    )
    spread_ref[...] = spread.astype(BF16)
    table = cn_ref[...]
    upper = lax.shift_right_logical(table, 8).astype(F32)
    lower = jnp.bitwise_and(table, WIDE - 1).astype(F32)
    table = WIDE * jnp.dot(upper.astype(BF16), order, preferred_element_type=F32) + jnp.dot(
        lower.astype(BF16), order, preferred_element_type=F32
    )
    low_half = lax.broadcasted_iota(jnp.int32, (1, cells), 1) < pairs
    base = table[:group]
    base = jnp.where(low_half, base, pltpu.roll(base, pairs, 1))
    lift = jnp.where(low_half, 0.0, float((edge - 1) * face))
    wrong = jnp.where((base < 0.0) | (base >= float(face)), 1.0, 0.0)
    for a in range(edge):
        expected = base + (lift + float(a * face))
        wrong = jnp.maximum(
            wrong, jnp.where(table[a * group:(a + 1) * group] == expected, 0.0, 1.0)
        )
    flag_ref[0, 0] = jnp.max(wrong)
    pd_ref[:group, :] = base
    places = jnp.where(
        low_half, pd_ref[pl.ds(0, wraps, stride=2), :], pd_ref[pl.ds(1, wraps, stride=2), :]
    ).astype(jnp.int32)
    slot = jnp.bitwise_and(places, WIDE - 1)
    hi_ref[:wraps, :] = lax.shift_right_logical(places, 8)
    wide_ids = lax.broadcasted_iota(jnp.int16, (WIDE, cells), 0)
    one, zero = jnp.array(1.0, BF16), jnp.array(0.0, BF16)
    for w in range(wraps):
        hot = jnp.where(wide_ids == slot[w:w + 1, :].astype(jnp.int16), one, zero)
        oh_ref[:, w * cells:(w + 1) * cells] = hot
        oht_ref[w * cells:(w + 1) * cells, :] = hot.T

    for w in range(wraps):
        hi = jnp.broadcast_to(hi_ref[w:w + 1, :], (2 * states, cells))
        for t in range(tiles):
            hot_ref[t * 2 * states:(t + 1) * 2 * states, w * cells:(w + 1) * cells] = (
                jnp.where(hi == t, 1.0, 0.0).astype(BF16)
            )
    rows128 = face // 128
    for fetch in fetches[1:]:
        fetch.wait()
    in_lower = entry_rank < float(pairs)
    last = (edge - 1) * group

    def proj_body(j, carry):
        rows = pl.ds(pl.multiple_of(j * nproj, nproj), nproj)
        projf_ref[rows, :] = proj_ref[j].astype(F32)
        return carry

    lax.fori_loop(0, width, proj_body, 0, unroll=8)

    def ends_body(i, carry):
        one, two = proj_ref[i].astype(F32), proj_ref[last + i].astype(F32)
        early = pl.multiple_of((width + i) * nproj, nproj)
        late = pl.multiple_of((width + group + i) * nproj, nproj)
        projf_ref[pl.ds(early, nproj), :] = jnp.where(in_lower, two, one)
        projf_ref[pl.ds(late, nproj), :] = jnp.where(in_lower, one, two)
        return carry

    lax.fori_loop(0, group, ends_body, 0, unroll=6)
    potf_ref[:slabs * rows128, :] = pot_ref[...].astype(F32) - CENTER

    def place(layer):
        if isinstance(layer, int):
            return 0 if layer == 0 else 1 if layer == slabs else layer + 1
        return layer + 1

    def put(layer, blocks):
        both = jnp.concatenate(blocks + [blocks[-1]], axis=0).astype(BF16)
        start = place(layer) * block
        if not isinstance(layer, int):
            start = pl.multiple_of(start, block)
        lhs_ref[pl.ds(start, block), :] = both

    def put_psi(layer, source, at):
        put(layer, [
            source[:, pl.ds(pl.multiple_of(at + t * WIDE, WIDE), WIDE)].astype(F32)
            for t in range(tiles)
        ])

    def psi_body(layer, carry):
        put_psi(layer, psi_ref, layer * face)
        return carry

    put_psi(0, psi_ref, 0)
    lax.fori_loop(1, slabs, psi_body, 0)

    def gather(first_row, chosen, finish, trips):
        rows = len(chosen) * block
        trip = wraps // trips

        def body(n, carry):
            hot = oh_ref[:, pl.ds(pl.multiple_of(n * trip * cells, trip * cells), trip * cells)]
            out = jnp.dot(lhs_ref[first_row:first_row + rows, :], hot, preferred_element_type=F32)
            for c in range(trip):
                w = n * trip + c
                hi = jnp.broadcast_to(hi_ref[pl.ds(w, 1), :], (states, cells))
                masks = [hi == t for t in range(1, tiles)]
                found = {}
                for k, layer in enumerate(chosen):
                    part = out[k * block:(k + 1) * block, c * cells:(c + 1) * cells]
                    value = part[:states]
                    for t in range(1, tiles):
                        value = jnp.where(
                            masks[t - 1], part[t * states:(t + 1) * states], value
                        )
                    found[layer] = value
                finish(w, found)
            return carry

        lax.fori_loop(0, trips, body, 0)

    def store_pair(into, row, w, lower_cells, upper_cells):
        mixed = pltpu.roll(jnp.where(low_half, upper_cells, lower_cells), pairs, 1)
        at = pl.multiple_of((row + 2 * w) * states, 2 * states)
        into[pl.ds(at, states), :] = jnp.where(low_half, lower_cells, mixed)
        into[pl.ds(at + states, states), :] = jnp.where(low_half, mixed, upper_cells)

    def inner_found(w, found):
        for a in range(1, edge - 1):
            store_pair(xs_ref, a * group, w, found[a], found[edge - 1 + a])
        store_pair(ends_ref, 0, w, found[edge - 1], found[edge - 1])

    def outer_found(w, found):
        store_pair(ends_ref, group, w, found[0], found[slabs])

    def gather_inner():
        gather(2 * block, tuple(range(1, slabs)), inner_found, 3)

    def gather_outer():
        gather(0, (0, slabs), outer_found, 1)

    def bcast(row):
        return projf_ref[pl.ds(row, states, stride=0), :]

    def partial_rows(source, at, proj_at, accs):
        values = jnp.dot(
            source[pl.ds(at, group * states), :].astype(BF16), spread_ref[...],
            preferred_element_type=F32,
        )
        accs = list(accs)
        for j in range(group):
            value = values[j * states:(j + 1) * states]
            for k in range(nproj):
                accs[k] = accs[k] + bcast(proj_at + j * nproj + k) * value
        return tuple(accs)

    def partial_body(a, accs):
        return partial_rows(
            xs_ref, pl.multiple_of(a * group * states, group * states), a * group * nproj, accs
        )

    def partial_inner():
        accs = lax.fori_loop(1, edge - 1, partial_body, empty)
        return partial_rows(ends_ref, 0, width * nproj, accs)

    def partial_outer(accs):
        return partial_rows(ends_ref, group * states, (width + group) * nproj, accs)

    slot_ids = lax.broadcasted_iota(jnp.int32, (4 * atoms, entries), 0)
    chosen_atom = jnp.where(slot_ids == eatom_ref[...], 1.0, 0.0).astype(BF16)
    chosen_send = jnp.concatenate(
        [chosen_atom[:2 * atoms], chosen_atom[atoms:3 * atoms], chosen_atom[2 * atoms:3 * atoms],
         chosen_atom[:atoms]], axis=0,
    )
    back = (((1,), (1,)), ((), ()))
    empty = tuple(jnp.zeros((states, entries), F32) for _ in range(nproj))
    low_atoms = lax.broadcasted_iota(jnp.int32, (1, 2 * atoms), 1) < atoms

    def send_atoms(step, accs):
        grouped = lax.dot_general(
            halves(jnp.concatenate(accs, axis=0), 1),
            jnp.concatenate([chosen_send, chosen_send], axis=1),
            back, preferred_element_type=F32,
        )
        for g in range(3):
            grouped_ref[step, g] = grouped[:, 2 * g * atoms:2 * (g + 1) * atoms]
        at = 4 + 6 * step
        return [
            send(grouped_ref.at[step, 1], left_ref.at[step], sems, at, ahead),
            send(grouped_ref.at[step, 0], right_ref.at[step], sems, at + 1, behind),
            send(grouped_ref.at[step, 2], far_ref.at[step, 0], sems, at + 2, ahead2),
            send(grouped_ref.at[step, 2], far_ref.at[step, 1], sems, at + 3, behind2),
        ]

    def cell_terms():
        size = group * states
        early, late = ends_ref[:size, :], ends_ref[size:, :]
        xs_ref[:size, :] = jnp.where(low_half, late, early)
        xs_ref[last * states:, :] = jnp.where(low_half, early, late)
        kmat = kmat_ref[...]
        for s in range(0, states, 2):
            pair = jnp.concatenate(
                [xs_ref[pl.ds(s, width, stride=states), :],
                 xs_ref[pl.ds(s + 1, width, stride=states), :]], axis=1,
            ).astype(BF16)
            out = jnp.dot(kmat, pair, preferred_element_type=F32)
            ct_ref[pl.ds(s, width, stride=states), :] = out[:, :cells] * scale
            ct_ref[pl.ds(s + 1, width, stride=states), :] = out[:, cells:] * scale

    def entry_terms(step):
        right = pltpu.roll(right_ref[step], atoms, 1)
        coef = (
            grouped_ref[step, 0] + left_ref[step]
            + jnp.where(low_atoms, far_ref[step, 0], right),
            grouped_ref[step, 2] + right + pltpu.roll(far_ref[step, 1], atoms, 1),
        )
        rows = []
        for c in range(2):
            parts = []
            for k in range(nproj):
                acc = jnp.zeros((states, 2 * atoms), F32)
                for l in range(nproj):
                    at = k * nproj + l
                    acc = acc + (
                        couple_ref[c, at:at + 1, :] * coef[c][l * states:(l + 1) * states, :]
                    )
                parts.append(acc)
            rows.append(halves(jnp.concatenate(parts, axis=0), 1))
        half_atoms = [chosen_atom[:2 * atoms]] * 2 + [chosen_atom[2 * atoms:]] * 2
        terms = jnp.dot(
            jnp.concatenate(rows, axis=1), jnp.concatenate(half_atoms, axis=0),
            preferred_element_type=F32,
        )
        return [terms[k * states:(k + 1) * states] for k in range(nproj)]

    def node_terms(a, terms):
        parts = []
        for j in range(group):
            row = (a * group + j) * nproj
            total = bcast(row) * terms[0]
            for k in range(1, nproj):
                total = total + bcast(row + k) * terms[k]
            parts.append(total)
        at = pl.multiple_of(a * group * states, group * states)
        twice = jnp.concatenate([spread_ref[...], spread_ref[...]], axis=1)
        value = ct_ref[pl.ds(at, group * states), :] + lax.dot_general(
            halves(jnp.concatenate(parts, axis=0), 1), twice, back, preferred_element_type=F32
        )
        for w in range(wraps):
            even = value[2 * w * states:(2 * w + 1) * states]
            odd = value[(2 * w + 1) * states:(2 * w + 2) * states]
            mixed = pltpu.roll(jnp.where(low_half, odd, even), pairs, 1)
            here = pl.multiple_of((a * wraps + w) * states, states)
            there = pl.multiple_of(((a + edge - 1) * wraps + w) * states, states)
            ys_ref[pl.ds(here, states), :] += jnp.where(low_half, even, mixed)
            ys_ref[pl.ds(there, states), :] += jnp.where(low_half, mixed, odd)

    per = tiles * 2 * states

    def scatter(into, chosen):
        for w in range(wraps):
            for n, layer in enumerate(chosen):
                at = pl.multiple_of((layer * wraps + w) * states, states)
                both = halves(ys_ref[pl.ds(at, states), :], 0)
                for t in range(tiles):
                    rows = into + (n * tiles + t) * 2 * states
                    masked_ref[rows:rows + 2 * states, w * cells:(w + 1) * cells] = (
                        both * hot_ref[t * 2 * states:(t + 1) * 2 * states,
                                       w * cells:(w + 1) * cells]
                    )
        rows = len(chosen) * per
        out = jnp.dot(masked_ref[into:into + rows, :], oht_ref[...], preferred_element_type=F32)
        return [
            [joined(out[n * per:(n + 1) * per], t) for t in range(tiles)]
            for n in range(len(chosen))
        ]

    def joined(value, t):
        return value[t * 2 * states:t * 2 * states + states] + (
            value[t * 2 * states + states:(t + 1) * 2 * states]
        )

    def scatter_outer(step, terms):
        def body(n, carry):
            node_terms(lax.rem(n + edge - 1, edge), terms)
            return carry

        lax.fori_loop(0, 2, body, 0)
        head, tail = scatter(0, (0, slabs))
        for t in range(tiles):
            head_ref[step, :, t * WIDE:(t + 1) * WIDE] = head[t]
            tail_ref[step, :, t * WIDE:(t + 1) * WIDE] = tail[t]

    def scatter_five():
        (out,) = scatter(2 * per, (edge - 1,))
        return lambda t: out[t]

    def scatter_rest(terms, finish):
        def body(a, carry):
            node_terms(a, terms)
            one, two = scatter(3 * per, (a, a + edge - 1))
            finish(a, lambda t: one[t], lambda t: two[t])
            return carry

        lax.fori_loop(1, edge - 1, body, 0)

    def pot_row(layer, t, half):
        row = layer * rows128 + t * 2 + half
        return potf_ref[pl.ds(row, 1), :]

    def scaled(layer, t, summed, field):
        pot = jnp.concatenate([pot_row(layer, t, 0), pot_row(layer, t, 1)], axis=1)
        return (summed + pot * field) * (1.0 / HALFWIDTH)

    def lanes(layer, t):
        at = layer * face + t * WIDE
        return pl.ds(at if isinstance(layer, int) else pl.multiple_of(at, WIDE), WIDE)

    def first_layer(layer, summed, field):
        blocks = []
        for t in range(tiles):
            value = scaled(layer, t, summed(t), field(t)).astype(BF16).astype(F32)
            first_ref[:, lanes(layer, t)] = value
            blocks.append(value)
        put(layer, blocks)

    def last_layer(layer, summed):
        for t in range(tiles):
            value = scaled(layer, t, summed(t), first_ref[:, lanes(layer, t)])
            at = lanes(layer, t)
            out_ref[:, at] = (2.0 * value - psi_ref[:, at].astype(F32)).astype(BF16)

    def edge_sum(one_ref, two_ref):
        return lambda t: (
            one_ref[:, t * WIDE:(t + 1) * WIDE] + two_ref[:, t * WIDE:(t + 1) * WIDE]
        )

    gather_inner()
    accs = partial_inner()
    ys_ref[...] = jnp.zeros_like(ys_ref)
    for copy in gaps:
        copy.wait()
    couple_ref[0] = jnp.where(low_atoms, coups_ref[0], coups_ref[1])
    couple_ref[1] = coups_ref[2]
    put_psi(slabs, ghost_ref, 0)
    gather_outer()
    copies = send_atoms(0, partial_outer(accs))
    potf_ref[slabs * rows128:slabs * rows128 + potg_ref.shape[0], :] = (
        potg_ref[...].astype(F32) - CENTER
    )
    cell_terms()
    for copy in copies:
        copy.wait()
    terms = entry_terms(0)
    scatter_outer(0, terms)
    copies = [
        send(tail_ref.at[0], low_ref.at[0], sems, 8, ahead),
        send(head_ref.at[0], high_ref, sems, 9, behind),
    ]

    def first_done(layer, summed):
        first_layer(layer, summed, lambda t: psi_ref[:, lanes(layer, t)].astype(F32))

    def first_pair(a, one, two):
        first_done(a, one)
        first_done(a + edge - 1, two)

    first_done(edge - 1, scatter_five())
    scatter_rest(terms, first_pair)
    gather_inner()
    accs = partial_inner()
    ys_ref[...] = jnp.zeros_like(ys_ref)
    for copy in copies:
        copy.wait()
    first_done(0, edge_sum(head_ref.at[0], low_ref.at[0]))
    first_layer(
        slabs, edge_sum(tail_ref.at[0], high_ref),
        lambda t: ghost_ref[:, t * WIDE:(t + 1) * WIDE].astype(F32),
    )
    gather_outer()
    copies = send_atoms(1, partial_outer(accs))
    mated = [send(first_ref.at[:, :face], mated_ref, sems, 20, partner)]
    cell_terms()
    for copy in copies:
        copy.wait()
    terms = entry_terms(1)
    scatter_outer(1, terms)
    tails = [
        send(tail_ref.at[1], low_ref.at[1], sems, 14, ahead),
        send(tail_ref.at[1], matel_ref, sems, 16, ahead_mate),
        send(head_ref.at[1], mateh_ref, sems, 19, partner),
    ]
    half = edge - 1

    def span(at, size):
        return pl.ds(pl.multiple_of(at, 128), size)

    def swap(n, layer):
        return pltpu.make_async_remote_copy(
            src_ref=out_ref.at[:, span(layer * face, face)],
            dst_ref=other_ref.at[:, span(n * face, face)],
            send_sem=sems.at[0, 21 + n], recv_sem=sems.at[1, 21 + n],
            device_id=partner, device_id_type=MESH_ID,
        )

    last_layer(half, scatter_five())
    swap(0, half).start()

    def last_pair(a, one, two):
        last_layer(a, one)
        last_layer(a + half, two)
        swap(a, jnp.where(band == 0, a + half, a)).start()

    scatter_rest(terms, last_pair)

    def gram(own, other):
        both = jnp.concatenate(
            [jnp.where(band == 0, own, other), jnp.where(band == 0, other, own)], axis=0
        ).astype(BF16)
        return lax.dot_general(both, both, back, preferred_element_type=F32)

    swap(0, half).wait()
    total = jnp.zeros((bands * states, bands * states), F32)
    for n in range(1, half):
        swap(n, half).wait()
        total = total + gram(
            out_ref[:, span(jnp.where(band == 0, n, n + half) * face, face)].astype(F32),
            other_ref[:, n * face:(n + 1) * face].astype(F32),
        )
    for copy in tails + mated:
        copy.wait()
    last_layer(0, edge_sum(head_ref.at[1], low_ref.at[1]))
    blocks = []
    summed = edge_sum(mateh_ref, matel_ref)
    for t in range(tiles):
        at = slice(t * WIDE, (t + 1) * WIDE)
        value = scaled(0, t, summed(t), mated_ref[:, at])
        value = (2.0 * value - mate_ref[:, at].astype(F32)).astype(BF16).astype(F32)
        blocks.append(jnp.where(band == 0, value, other_ref[:, at].astype(F32)))
    total = total + gram(
        out_ref[:, span(jnp.where(band == 0, 0, half) * face, face)].astype(F32),
        jnp.concatenate(blocks, axis=1),
    )
    size = bands * states
    lump = size * size // 128
    pieces = size // lump
    slots_ref[me] = jnp.concatenate(
        [total[r * lump:(r + 1) * lump] for r in range(pieces)], axis=1
    )

    def push(steps, carry):
        send(slots_ref.at[me], slots_ref.at[me], sems, 17, peer(steps))
        return carry

    lax.fori_loop(1, devices * bands, push, 0)
    rest = pl.ds(0, devices * bands - 1)
    pltpu.make_async_remote_copy(
        src_ref=slots_ref.at[rest], dst_ref=slots_ref.at[rest], send_sem=sems.at[0, 17],
        recv_sem=sems.at[1, 17], device_id=partner, device_id_type=MESH_ID,
    ).wait()
    total = jnp.sum(slots_ref[...], axis=0) * (1.0 / (devices * count))
    corr_ref[...] = jnp.concatenate(
        [total[:, r * size:(r + 1) * size] for r in range(pieces)], axis=0
    )


def general(
    psi,
    cell_nodes,
    cell_scale,
    cell_matrix,
    node_potential,
    proj_values,
    entry_cell,
    entry_atom,
    coupling,
):
    states, node_count = psi.shape
    width, cells = cell_nodes.shape
    atoms, nproj, _ = coupling.shape
    entries = entry_atom.shape[0]
    full = node_count + FACEP
    chunks = full // FACEP
    layers = FACEP // WIDE
    groups = width // GROUP
    span = GROUP * cells

    table = cell_nodes.reshape(groups, GROUP, cells)
    owner = table // FACEP
    ids = jnp.arange(chunks, dtype=jnp.int32)
    flags = jnp.max(
        (owner[:, None] == ids[None, :, None, None]).astype(jnp.int32), axis=(2, 3)
    )
    rank = jnp.sum(flags[:, None, :] * (ids[None, :] < ids[:, None]), axis=2)
    places = jnp.arange(chunks + 1, dtype=jnp.int32)
    used = flags[:, :, None] * (rank[:, :, None] == places)
    listed = chunks + jnp.sum(used * (ids[None, :, None] - chunks), axis=1)
    listed = jnp.concatenate(
        [listed, jnp.full((groups, 1), chunks, jnp.int32), jnp.sum(flags, axis=1, keepdims=True)],
        axis=1,
    )
    sched = listed.astype(jnp.int32).reshape(groups * (chunks + 3))
    scale_row = cell_scale.reshape(1, cells)
    ecell = entry_cell.reshape(1, entries)
    eatom = entry_atom.reshape(1, entries)
    coup = coupling.transpose(1, 2, 0).reshape(nproj * nproj, atoms)
    potential = node_potential.astype(F32).reshape(1, node_count) - CENTER

    vmem = pl.BlockSpec(memory_space=pltpu.VMEM)
    smem = pl.BlockSpec(memory_space=pltpu.SMEM)

    padded = (layers * states + 15) // 16 * 16
    gather = pl.pallas_call(
        gather_kernel,
        out_shape=jax.ShapeDtypeStruct((width * states, cells), F32),
        in_specs=[smem] + [vmem] * 2,
        out_specs=vmem,
        scratch_shapes=[
            pltpu.VMEM((chunks + 1, padded, WIDE), BF16),
            pltpu.VMEM((WIDE, span), BF16),
        ],
        name="gather_cells",
    )
    scatter = pl.pallas_call(
        scatter_kernel,
        out_shape=jax.ShapeDtypeStruct((states, full), F32),
        in_specs=[smem] + [vmem] * 7,
        out_specs=vmem,
        scratch_shapes=[
            pltpu.VMEM((WIDE, span), BF16),
            pltpu.VMEM((width * states, entries), F32),
            pltpu.VMEM((width * states, cells), F32),
            pltpu.VMEM((2 * layers * 2 * states, span), BF16),
            pltpu.VMEM((chunks + 1, layers * 2 * states, WIDE), F32),
        ],
        name="scatter_nodes",
    )

    def remote(kernel, outs, n_in, scratch, copies, ident):
        return pl.pallas_call(
            kernel,
            out_shape=tuple(jax.ShapeDtypeStruct(*out) for out in outs),
            in_specs=[vmem] * n_in,
            out_specs=(vmem,) * len(outs),
            scratch_shapes=[pltpu.VMEM(*one) for one in scratch]
            + [pltpu.SemaphoreType.DMA((2, copies))],
            compiler_params=pltpu.CompilerParams(collective_id=ident, has_side_effects=True),
            name=kernel.__name__,
        )

    pair = (nproj * states, atoms)

    def assemble(extended, ident):
        values = gather(sched, table, extended)
        cell_terms, coef = remote(
            atoms_kernel, [((width * states, cells), F32), ((3,) + pair, F32)], 6,
            [((width * states, entries), F32), ((3,) + pair, F32)] + [((2,) + pair, F32)] * 3,
            4, ident,
        )(values, cell_matrix, scale_row, proj_values, ecell, eatom)
        return scatter(sched, table, cell_terms, coef, coup_all, proj_values, ecell, eatom)

    psi_ext, pot_ext, coup_all = remote(
        start_kernel,
        [((states, full), BF16), ((1, full), F32), ((3, nproj * nproj, atoms), F32)],
        3, [], 4, 1,
    )(psi, potential, coup)
    face = (states, FACEP)
    (first,) = remote(first_kernel, [((states, full), BF16)], 3, [(face, F32), (face, F32)], 2, 3)(
        assemble(psi_ext, 2), psi_ext, pot_ext
    )
    bands, devices = lax.axis_size("band"), lax.axis_size("mesh")
    square = (bands * states, bands * states)
    filtered, correlation = remote(
        last_kernel,
        [((states, node_count), BF16), (square, F32)],
        4,
        [(face, F32), ((states, node_count), BF16), ((devices,) + square, F32)],
        4, 5,
    )(assemble(first, 4), first, psi, potential)
    return (filtered, correlation)


def bricks(states, node_count, width, cells, bands):
    edge = round(width ** (1.0 / 3.0))
    return (
        edge ** 3 == width
        and (edge - 1) * 2 * FACEP == node_count
        and edge % 2 == 0
        and cells == 128
        and FACEP % WIDE == 0
        and states == 8
        and bands == 2
        and edge * edge % 6 == 0
    )


def local(
    psi,
    cell_nodes,
    cell_scale,
    cell_matrix,
    node_potential,
    proj_values,
    entry_cell,
    entry_atom,
    coupling,
):
    states, node_count = psi.shape
    width, cells = cell_nodes.shape
    atoms, nproj, _ = coupling.shape
    entries = entry_atom.shape[0]
    bands, devices = lax.axis_size("band"), lax.axis_size("mesh")
    operands = (
        psi, cell_nodes, cell_scale, cell_matrix, node_potential, proj_values, entry_cell,
        entry_atom, coupling,
    )
    if not bricks(states, node_count, width, cells, bands):
        return general(*operands)
    edge = round(width ** (1.0 / 3.0))
    wraps = edge * edge // 2
    layers = node_count // FACEP + 1
    tiles = FACEP // WIDE
    block = (tiles + 1) * states
    per = tiles * 2 * states
    rows = node_count // 128
    ghost_rows = (FACEP // 128 + 15) // 16 * 16
    size = bands * states
    vmem = pl.BlockSpec(memory_space=pltpu.VMEM)
    smem = pl.BlockSpec(memory_space=pltpu.SMEM)
    anywhere = pl.BlockSpec(memory_space=pl.ANY)
    face = (states, FACEP)
    duo = (nproj * states, 2 * atoms)
    filtered, correlation, wrong = pl.pallas_call(
        fused_kernel,
        out_shape=(
            jax.ShapeDtypeStruct((states, node_count), BF16),
            jax.ShapeDtypeStruct((size, size), F32),
            jax.ShapeDtypeStruct((1, 1), F32),
        ),
        in_specs=[anywhere, anywhere, vmem, anywhere, anywhere, anywhere, vmem, vmem, vmem],
        out_specs=(vmem, vmem, smem),
        scratch_shapes=[
            pltpu.VMEM(psi.shape, BF16),
            pltpu.VMEM(cell_nodes.shape, jnp.int32),
            pltpu.VMEM(cell_matrix.shape, BF16),
            pltpu.VMEM((rows, 128), BF16),
            pltpu.VMEM(proj_values.shape, BF16),
            pltpu.VMEM((WIDE, wraps * cells), BF16),
            pltpu.VMEM((wraps * cells, WIDE), BF16),
            pltpu.VMEM(((wraps + 7) // 8 * 8, cells), jnp.int32),
            pltpu.VMEM(((2 * wraps + 7) // 8 * 8, cells), F32),
            pltpu.VMEM((width * states, cells), F32),
            pltpu.VMEM((width * states, cells), F32),
            pltpu.VMEM((4 * wraps * states, cells), F32),
            pltpu.VMEM((wraps * states, cells), F32),
            pltpu.VMEM((layers * wraps * states, cells), F32),
            pltpu.VMEM((layers * block, WIDE), BF16),
            pltpu.VMEM((5 * per, wraps * cells), BF16),
            pltpu.VMEM((states, layers * FACEP), F32),
            pltpu.VMEM((rows + ghost_rows, 128), F32),
            pltpu.VMEM((2,) + face, F32),
            pltpu.VMEM((2,) + face, F32),
            pltpu.VMEM((2,) + face, F32),
            pltpu.VMEM(face, F32),
            pltpu.VMEM((2, 3) + duo, F32),
            pltpu.VMEM((2,) + duo, F32),
            pltpu.VMEM((2,) + duo, F32),
            pltpu.VMEM((2, 2) + duo, F32),
            pltpu.VMEM(face, BF16),
            pltpu.VMEM((ghost_rows, 128), BF16),
            pltpu.VMEM((3, nproj * nproj, 2 * atoms), F32),
            pltpu.VMEM((cells, entries), BF16),
            pltpu.VMEM((states, node_count // 2), BF16),
            pltpu.VMEM((devices * bands, size * size // 128, 128), F32),
            pltpu.VMEM((per, wraps * cells), BF16),
            pltpu.VMEM((2, nproj * nproj, 2 * atoms), F32),
            pltpu.VMEM(face, BF16),
            pltpu.VMEM(face, F32),
            pltpu.VMEM(face, F32),
            pltpu.VMEM(face, F32),
            pltpu.VMEM(((width + 4 * wraps) * nproj, entries), F32),
            pltpu.SemaphoreType.DMA((5,)),
            pltpu.SemaphoreType.DMA((2, 26)),
        ],
        compiler_params=pltpu.CompilerParams(collective_id=0, has_side_effects=True),
        name="fused_steps",
    )(
        psi, cell_nodes, cell_scale.reshape(1, cells), cell_matrix,
        node_potential.reshape(rows, 128), proj_values, entry_cell.reshape(1, entries),
        entry_atom.reshape(1, entries),
        coupling.transpose(1, 2, 0).reshape(nproj * nproj, atoms),
    )
    return lax.cond(
        wrong[0, 0] > 0.0,
        lambda: general(*operands),
        lambda: (filtered, correlation),
    )


def solution(mesh):
    return jax.shard_map(
        local,
        mesh=mesh,
        in_specs=(
            P("band", "mesh"),
            P(),
            P("mesh"),
            P(),
            P("mesh"),
            P(None, None, "mesh"),
            P("mesh"),
            P("mesh"),
            P("mesh", None, None),
        ),
        out_specs=(P("band", "mesh"), P()),
        check_vma=False,
    )
```

```python
import jax
import jax.numpy as jnp
from jax import lax
from jax.experimental import pallas as pl
from jax.experimental.pallas import tpu as pltpu
from jax.sharding import PartitionSpec as P

FACEP = 1792
CENTER = 0.5
HALFWIDTH = 2.5
HIGH = lax.Precision.HIGHEST
WIDE = 256
GROUP = 36
F32 = jnp.float32
BF16 = jnp.bfloat16


def fill_onehot(cn_ref, group, oh_ref):
    rows = cn_ref[group]
    hi = jnp.bitwise_and(rows, WIDE - 1)
    lanes = rows.shape[1]
    iota = lax.broadcasted_iota(jnp.int32, (WIDE, lanes), 0)
    for jj in range(GROUP):
        oh_ref[:, jj * lanes:(jj + 1) * lanes] = jnp.where(
            iota == hi[jj:jj + 1, :], 1.0, 0.0
        ).astype(BF16)
    return lax.shift_right_logical(rows, 8)


def gather_kernel(sched_ref, cn_ref, ext_ref, xs_ref, lhs_ref, oh_ref):
    states = ext_ref.shape[0]
    chunks = lhs_ref.shape[0] - 1
    layers = ext_ref.shape[1] // (chunks * WIDE)
    groups = cn_ref.shape[0]
    cells = cn_ref.shape[2]
    padded = lhs_ref.shape[1]
    slots = sched_ref.shape[0] // groups
    lhs_ref[...] = jnp.zeros_like(lhs_ref)
    for c in range(chunks):
        base = c * layers * WIDE
        parts = [
            ext_ref[:, base + l * WIDE:base + (l + 1) * WIDE].astype(F32) for l in range(layers)
        ]
        parts.append(jnp.zeros((padded - layers * states, WIDE), F32))
        lhs_ref[c] = jnp.concatenate(parts, axis=0).astype(BF16)
    xs_ref[...] = jnp.zeros_like(xs_ref)

    def group_body(g, carry):
        lo = fill_onehot(cn_ref, g, oh_ref)

        def pair_body(r, inner):
            first = sched_ref[g * slots + 2 * r]
            second = sched_ref[g * slots + 2 * r + 1]
            lhs = jnp.concatenate([lhs_ref[first], lhs_ref[second]], axis=0)
            out = jnp.dot(lhs, oh_ref[...], preferred_element_type=F32)
            for jj in range(GROUP):
                where = pl.ds(pl.multiple_of((g * GROUP + jj) * states, states), states)
                value = xs_ref[where, :]
                lanes = slice(jj * cells, (jj + 1) * cells)
                for half, chunk in enumerate((first, second)):
                    row = lo[jj:jj + 1, :] - chunk * layers
                    for l in range(layers):
                        at = half * padded + l * states
                        value = jnp.where(row == l, out[at:at + states, lanes], value)
                xs_ref[where, :] = value
            return inner

        pairs = lax.shift_right_logical(sched_ref[g * slots + slots - 1] + 1, 1)
        return lax.fori_loop(0, pairs, pair_body, carry)

    lax.fori_loop(0, groups, group_body, 0)


def scatter_kernel(sched_ref, cn_ref, ct_ref, coef_ref, coup_ref, proj_ref, ecell_ref,
                   eatom_ref, y_ref, oh_ref, ns_ref, v_ref, lhs_ref, acc_ref):
    chunks, rows_in_chunk, _ = acc_ref.shape
    chunks = chunks - 1
    groups = cn_ref.shape[0]
    cells = cn_ref.shape[2]
    width = groups * GROUP
    states = ct_ref.shape[0] // width
    layers = rows_in_chunk // (2 * states)
    nproj = proj_ref.shape[1]
    entries = ecell_ref.shape[1]
    atoms = coef_ref.shape[2]
    slot_ids = lax.broadcasted_iota(jnp.int32, (atoms, entries), 0)
    entry_terms = jnp.zeros((nproj * states, entries), F32)
    for g in range(3):
        rows = []
        for k in range(nproj):
            acc = jnp.zeros((states, atoms), F32)
            for l in range(nproj):
                acc = acc + (
                    coup_ref[g, k * nproj + l:k * nproj + l + 1, :]
                    * coef_ref[g, l * states:(l + 1) * states, :]
                )
            rows.append(acc)
        chosen = jnp.where(eatom_ref[...] == slot_ids + g * atoms, 1.0, 0.0)
        entry_terms = entry_terms + jnp.dot(
            jnp.concatenate(rows, axis=0), chosen, precision=HIGH, preferred_element_type=F32
        )
    terms = [entry_terms[k * states:(k + 1) * states, :] for k in range(nproj)]

    def node_body(j, carry):
        proj = proj_ref[j].astype(F32)
        total = proj[0:1, :] * terms[0]
        for k in range(1, nproj):
            total = total + proj[k:k + 1, :] * terms[k]
        ns_ref[pl.ds(pl.multiple_of(j * states, states), states), :] = total
        return carry

    lax.fori_loop(0, width, node_body, 0, unroll=8)
    cell_ids = lax.broadcasted_iota(jnp.int32, (cells, entries), 0)
    spread = jnp.where(cell_ids == ecell_ref[...], 1.0, 0.0).astype(BF16)
    back = (((1,), (1,)), ((), ()))
    node_vals = ns_ref[...]
    node_top = node_vals.astype(BF16)
    node_rest = (node_vals - node_top.astype(F32)).astype(BF16)
    v_ref[...] = (
        ct_ref[...]
        + lax.dot_general(node_top, spread, back, preferred_element_type=F32)
        + lax.dot_general(node_rest, spread, back, preferred_element_type=F32)
    )
    acc_ref[...] = jnp.zeros_like(acc_ref)
    slots = sched_ref.shape[0] // groups

    def group_body(g, carry):
        lo = fill_onehot(cn_ref, g, oh_ref)

        def pair_body(r, inner):
            first = sched_ref[g * slots + 2 * r]
            second = sched_ref[g * slots + 2 * r + 1]
            for jj in range(GROUP):
                start = pl.multiple_of((g * GROUP + jj) * states, states)
                value = v_ref[pl.ds(start, states), :]
                top = value.astype(BF16).astype(F32)
                both = jnp.concatenate([top, value - top], axis=0)
                lanes = slice(jj * cells, (jj + 1) * cells)
                for half, chunk in enumerate((first, second)):
                    row = lo[jj:jj + 1, :] - chunk * layers
                    for l in range(layers):
                        at = half * rows_in_chunk + l * 2 * states
                        lhs_ref[at:at + 2 * states, lanes] = (
                            jnp.where(row == l, both, 0.0).astype(BF16)
                        )
            out = lax.dot_general(lhs_ref[...], oh_ref[...], back, preferred_element_type=F32)
            acc_ref[first] += out[:rows_in_chunk]
            acc_ref[second] += out[rows_in_chunk:]
            return inner

        pairs = lax.shift_right_logical(sched_ref[g * slots + slots - 1] + 1, 1)
        return lax.fori_loop(0, pairs, pair_body, carry)

    lax.fori_loop(0, groups, group_body, 0)
    for c in range(chunks):
        for l in range(layers):
            base = (c * layers + l) * WIDE
            at = l * 2 * states
            y_ref[:, base:base + WIDE] = (
                acc_ref[c, at:at + states, :] + acc_ref[c, at + states:at + 2 * states, :]
            )


MESH_ID = pl.DeviceIdType.MESH


def ring_peer(steps):
    count = lax.axis_size("mesh")
    return lax.rem(lax.axis_index("mesh") + steps + count, count)


def send(src, dst, sems, at, peer):
    copy = pltpu.make_async_remote_copy(
        src_ref=src, dst_ref=dst, send_sem=sems.at[0, at], recv_sem=sems.at[1, at],
        device_id=peer, device_id_type=MESH_ID,
    )
    copy.start()
    return copy


def greet(peers):
    barrier = pltpu.get_barrier_semaphore()
    for peer in peers:
        pl.semaphore_signal(barrier, inc=1, device_id=peer, device_id_type=MESH_ID)
    return barrier


def start_kernel(psi_ref, pot_ref, coup_ref, ext_ref, potx_ref, coups_ref, sems):
    count = psi_ref.shape[1]
    face = ext_ref.shape[1] - count
    ahead, behind = {"mesh": ring_peer(1)}, {"mesh": ring_peer(-1)}
    pl.semaphore_wait(greet((ahead, behind)), 2)
    copies = [
        send(psi_ref.at[:, :face], ext_ref.at[:, count:], sems, 0, behind),
        send(coup_ref, coups_ref.at[0], sems, 1, ahead),
        send(coup_ref, coups_ref.at[2], sems, 2, behind),
        send(pot_ref.at[:, :face], potx_ref.at[:, count:], sems, 3, behind),
    ]
    ext_ref[:, :count] = psi_ref[...]
    potx_ref[:, :count] = pot_ref[...]
    coups_ref[1] = coup_ref[...]
    for copy in copies:
        copy.wait()


def atoms_kernel(xs_ref, kmat_ref, scale_ref, proj_ref, ecell_ref, eatom_ref, ct_ref, coef_ref,
                 es_ref, grouped_ref, left_ref, right_ref, far_ref, sems):
    peers = [{"mesh": ring_peer(steps)} for steps in (1, -1, 2, -2)]
    barrier = greet(peers)
    width, nproj, entries = proj_ref.shape
    cells = xs_ref.shape[1]
    states = xs_ref.shape[0] // width
    cell_ids = lax.broadcasted_iota(jnp.int32, (cells, entries), 0)
    spread = jnp.where(cell_ids == ecell_ref[...], 1.0, 0.0).astype(BF16)
    es_ref[...] = jnp.dot(xs_ref[...].astype(BF16), spread, preferred_element_type=F32)

    def partial_body(j, accs):
        values = es_ref[pl.ds(pl.multiple_of(j * states, states), states), :]
        proj = proj_ref[j].astype(F32)
        return tuple(acc + proj[k:k + 1, :] * values for k, acc in enumerate(accs))

    zero = jnp.zeros((states, entries), F32)
    accs = lax.fori_loop(0, width, partial_body, (zero,) * nproj, unroll=8)
    partial_sum = jnp.concatenate(accs, axis=0)
    atoms = grouped_ref.shape[2]
    slot_ids = lax.broadcasted_iota(jnp.int32, (atoms, entries), 0)
    for g in range(3):
        chosen = jnp.where(eatom_ref[...] == slot_ids + g * atoms, 1.0, 0.0)
        grouped_ref[g] = lax.dot_general(
            partial_sum, chosen, (((1,), (1,)), ((), ())), precision=HIGH,
            preferred_element_type=F32,
        )
    pl.semaphore_wait(barrier, 4)
    copies = [
        send(grouped_ref.at[1:3], left_ref, sems, 0, peers[0]),
        send(grouped_ref.at[0:2], right_ref, sems, 1, peers[1]),
        send(grouped_ref.at[2], far_ref.at[0], sems, 2, peers[2]),
        send(grouped_ref.at[0], far_ref.at[1], sems, 3, peers[3]),
    ]
    kmat = kmat_ref[...]
    scale = scale_ref[...]
    for s in range(0, states, 2):
        pair = jnp.concatenate(
            [xs_ref[pl.ds(s, width, stride=states), :], xs_ref[pl.ds(s + 1, width, stride=states), :]],
            axis=1,
        ).astype(BF16)
        out = jnp.dot(kmat, pair, preferred_element_type=F32)
        ct_ref[pl.ds(s, width, stride=states), :] = out[:, :cells] * scale
        ct_ref[pl.ds(s + 1, width, stride=states), :] = out[:, cells:] * scale
    for copy in copies:
        copy.wait()
    coef_ref[0] = left_ref[0] + far_ref[0] + grouped_ref[0]
    coef_ref[1] = grouped_ref[1] + left_ref[1] + right_ref[0]
    coef_ref[2] = right_ref[1] + grouped_ref[2] + far_ref[1]


def first_kernel(y_ref, ext_ref, pot_ref, first_ref, low_ref, high_ref, sems):
    full = y_ref.shape[1]
    face = low_ref.shape[1]
    count = full - face
    ahead, behind = {"mesh": ring_peer(1)}, {"mesh": ring_peer(-1)}
    barrier = greet((ahead, behind))

    def finish(total, at):
        scaled = (total + pot_ref[:, at] * ext_ref[:, at].astype(F32)) / HALFWIDTH
        first_ref[:, at] = scaled.astype(BF16)

    middle = face * (1 + (count // face - 1) // 2)
    for base in range(face, middle, face):
        at = slice(base, base + face)
        finish(y_ref[:, at], at)
    pl.semaphore_wait(barrier, 2)
    copies = [
        send(y_ref.at[:, count:], low_ref, sems, 0, ahead),
        send(y_ref.at[:, :face], high_ref, sems, 1, behind),
    ]
    for base in range(middle, count, face):
        at = slice(base, base + face)
        finish(y_ref[:, at], at)
    for copy in copies:
        copy.wait()
    finish(y_ref[:, :face] + low_ref[...], slice(0, face))
    finish(y_ref[:, count:] + high_ref[...], slice(count, full))


def last_kernel(y_ref, first_ref, psi_ref, pot_ref, out_ref, corr_ref, low_ref, other_ref,
                slots_ref, sems):
    count = psi_ref.shape[1]
    face = low_ref.shape[1]
    devices = lax.axis_size("mesh")
    bands = lax.axis_size("band")
    me = lax.axis_index("mesh")
    band = lax.axis_index("band")
    partner = {"band": lax.rem(band + 1, bands)}
    barrier = greet((partner,))

    def greet_body(steps, carry):
        pl.semaphore_signal(
            barrier, inc=1, device_id={"mesh": lax.rem(me + steps, devices)}, device_id_type=MESH_ID
        )
        return carry

    lax.fori_loop(1, devices, greet_body, 0)

    def finish(total, at):
        scaled = (total + pot_ref[:, at] * first_ref[:, at].astype(F32)) / HALFWIDTH
        out_ref[:, at] = (2.0 * scaled - psi_ref[:, at].astype(F32)).astype(BF16)

    for base in range(face, count, face):
        at = slice(base, base + face)
        finish(y_ref[:, at], at)
    pl.semaphore_wait(barrier, devices)
    tail = send(y_ref.at[:, count:count + face], low_ref, sems, 0, {"mesh": ring_peer(1)})
    swap = send(out_ref.at[:, face:], other_ref.at[:, face:], sems, 1, partner)
    states = out_ref.shape[0]

    def gram(base):
        at = slice(base, base + face)
        own, other = out_ref[:, at].astype(F32), other_ref[:, at].astype(F32)
        block = jnp.concatenate(
            [jnp.where(band == 0, own, other), jnp.where(band == 0, other, own)], axis=0
        ).astype(BF16)
        return lax.dot_general(
            block, block, (((1,), (1,)), ((), ())), preferred_element_type=F32
        )

    swap.wait()
    total = gram(face)
    for base in range(2 * face, count, face):
        total = total + gram(base)
    tail.wait()
    finish(y_ref[:, :face] + low_ref[...], slice(0, face))
    edge = send(out_ref.at[:, :face], other_ref.at[:, :face], sems, 3, partner)
    edge.wait()
    total = total + gram(0)
    slots_ref[me] = total

    def push(steps, carry):
        send(slots_ref.at[me], slots_ref.at[me], sems, 2, {"mesh": lax.rem(me + steps, devices)})
        return carry

    lax.fori_loop(1, devices, push, 0)
    pltpu.make_async_remote_copy(
        src_ref=slots_ref.at[pl.ds(0, devices - 1)], dst_ref=slots_ref.at[pl.ds(0, devices - 1)],
        send_sem=sems.at[0, 2], recv_sem=sems.at[1, 2], device_id=partner, device_id_type=MESH_ID,
    ).wait()
    corr_ref[...] = jnp.sum(slots_ref[...], axis=0) * (1.0 / (devices * count))


def everyone(count):
    bands = lax.axis_size("band")
    flat = lax.axis_index("mesh") * bands + lax.axis_index("band")
    early = flat < count // 2

    def peer(n):
        down = count - 1 - n
        other = jnp.where(
            early, jnp.where(down <= flat, down - 1, down), jnp.where(n >= flat, n + 1, n)
        )
        return {"mesh": other // bands, "band": lax.rem(other, bands)}

    return flat, peer


def halves(value, axis):
    top = value.astype(BF16)
    return jnp.concatenate([top, (value - top.astype(F32)).astype(BF16)], axis=axis)


def fused_kernel(psi_hbm, cn_hbm, scale_hbm, kmat_hbm, pot_hbm, proj_hbm, ecell_hbm, eatom_hbm,
                 coup_hbm, out_ref, corr_ref, flag_ref,
                 psi_ref, cn_ref, kmat_ref, pot_ref, proj_ref, scale_ref, ecell_ref, eatom_ref, coup_ref,
                 oh_ref, oht_ref, hi_ref, pd_ref, xs_ref, ct_ref, ends_ref, lhs_ref,
                 masked_ref, first_ref, potf_ref, head_ref, tail_ref, low_ref, high_ref,
                 grouped_ref, left_ref, right_ref, far_ref, ghost_ref, potg_ref, coups_ref,
                 spread_ref, other_ref, slots_ref, hot_ref, couple_ref, mate_ref, mated_ref,
                 mateh_ref, matel_ref, projf_ref, fetch_sems, sems):
    fetches = [
        pltpu.make_async_copy(src, dst, fetch_sems.at[n])
        for n, (src, dst) in enumerate((
            (cn_hbm, cn_ref), (scale_hbm, scale_ref), (ecell_hbm, ecell_ref),
            (coup_hbm, coup_ref), (eatom_hbm, eatom_ref), (psi_hbm, psi_ref),
            (proj_hbm, proj_ref), (pot_hbm, pot_ref), (kmat_hbm, kmat_ref),
        ))
    ]
    for fetch in fetches:
        fetch.start()
    states, count = psi_ref.shape
    width, cells = cn_ref.shape
    face = ghost_ref.shape[1]
    slabs = count // face
    layers = slabs + 1
    _, nproj, entries = proj_ref.shape
    atoms = coup_ref.shape[1]
    edge = slabs // 2 + 1
    group = width // edge
    pairs = cells // 2
    tiles = face // WIDE
    block = (tiles + 1) * states
    wraps = group // 2
    devices, bands = lax.axis_size("mesh"), lax.axis_size("band")
    band = lax.axis_index("band")
    me, peer = everyone(devices * bands)
    ahead, behind = {"mesh": ring_peer(1)}, {"mesh": ring_peer(-1)}
    ahead2, behind2 = {"mesh": ring_peer(2)}, {"mesh": ring_peer(-2)}
    partner = {"band": lax.rem(band + 1, bands)}
    ahead_mate = {"mesh": ring_peer(1), "band": lax.rem(band + 1, bands)}
    barrier = pltpu.get_barrier_semaphore()

    def greet_body(steps, carry):
        pl.semaphore_signal(barrier, inc=1, device_id=peer(steps), device_id_type=MESH_ID)
        return carry

    lax.fori_loop(0, devices * bands - 1, greet_body, 0)
    for fetch in fetches[:4]:
        fetch.wait()
    down = lax.broadcasted_iota(jnp.int32, (cells, cells), 0)
    across = lax.broadcasted_iota(jnp.int32, (cells, cells), 1)
    eye = down == across
    key = jnp.broadcast_to(cn_ref[0:1, :].astype(F32), (cells, cells))
    key_col = jnp.sum(jnp.where(eye, key, 0.0), axis=1, keepdims=True)
    rank = jnp.sum(jnp.where(key < key_col, 1.0, 0.0), axis=1, keepdims=True)
    chosen_cell = rank == across.astype(F32)
    order = jnp.where(chosen_cell, 1.0, 0.0).astype(BF16)
    scale_col = jnp.sum(
        jnp.where(eye, jnp.broadcast_to(scale_ref[...], (cells, cells)), 0.0), axis=1, keepdims=True
    )
    scale = jnp.sum(jnp.where(chosen_cell, scale_col, 0.0), axis=0, keepdims=True)
    entry_rank = jnp.sum(
        jnp.where(lax.broadcasted_iota(jnp.int32, (cells, entries), 0) == ecell_ref[...], rank, 0.0),
        axis=0, keepdims=True,
    )
    spread = jnp.where(
        lax.broadcasted_iota(jnp.int32, (cells, entries), 0).astype(F32) == entry_rank, 1.0, 0.0
    )
    spread_ref[...] = spread.astype(BF16)
    table = cn_ref[...]
    upper = lax.shift_right_logical(table, 8).astype(F32)
    lower = jnp.bitwise_and(table, WIDE - 1).astype(F32)
    table = WIDE * jnp.dot(upper.astype(BF16), order, preferred_element_type=F32) + jnp.dot(
        lower.astype(BF16), order, preferred_element_type=F32
    )
    low_half = lax.broadcasted_iota(jnp.int32, (1, cells), 1) < pairs
    base = table[:group]
    base = jnp.where(low_half, base, pltpu.roll(base, pairs, 1))
    lift = jnp.where(low_half, 0.0, float((edge - 1) * face))
    wrong = jnp.where((base < 0.0) | (base >= float(face)), 1.0, 0.0)
    for a in range(edge):
        expected = base + (lift + float(a * face))
        wrong = jnp.maximum(
            wrong, jnp.where(table[a * group:(a + 1) * group] == expected, 0.0, 1.0)
        )
    flag_ref[0, 0] = jnp.max(wrong)
    pd_ref[:group, :] = base
    places = jnp.where(
        low_half, pd_ref[pl.ds(0, wraps, stride=2), :], pd_ref[pl.ds(1, wraps, stride=2), :]
    ).astype(jnp.int32)
    slot = jnp.bitwise_and(places, WIDE - 1)
    hi_ref[:wraps, :] = lax.shift_right_logical(places, 8)
    wide_ids = lax.broadcasted_iota(jnp.int16, (WIDE, cells), 0)
    one, zero = jnp.array(1.0, BF16), jnp.array(0.0, BF16)
    for w in range(wraps):
        hot = jnp.where(wide_ids == slot[w:w + 1, :].astype(jnp.int16), one, zero)
        oh_ref[:, w * cells:(w + 1) * cells] = hot
        oht_ref[w * cells:(w + 1) * cells, :] = hot.T

    for w in range(wraps):
        hi = jnp.broadcast_to(hi_ref[w:w + 1, :], (2 * states, cells))
        for t in range(tiles):
            hot_ref[t * 2 * states:(t + 1) * 2 * states, w * cells:(w + 1) * cells] = (
                jnp.where(hi == t, 1.0, 0.0).astype(BF16)
            )
    coups_ref[1] = jnp.concatenate([coup_ref[...]] * 2, axis=1)
    pl.semaphore_wait(barrier, devices * bands - 1)
    gaps = [
        send(psi_hbm.at[:, :face], ghost_ref, sems, 0, behind),
        send(pot_hbm.at[:potg_ref.shape[0], :], potg_ref, sems, 1, behind),
        send(coups_ref.at[1], coups_ref.at[0], sems, 2, ahead),
        send(coups_ref.at[1], coups_ref.at[2], sems, 3, behind),
        send(psi_hbm.at[:, :face], mate_ref, sems, 18, partner),
    ]

    rows128 = face // 128
    for fetch in fetches[4:]:
        fetch.wait()
    in_lower = entry_rank < float(pairs)
    last = (edge - 1) * group

    def proj_body(j, carry):
        rows = pl.ds(pl.multiple_of(j * nproj, nproj), nproj)
        projf_ref[rows, :] = proj_ref[j].astype(F32)
        return carry

    lax.fori_loop(0, width, proj_body, 0, unroll=8)

    def ends_body(i, carry):
        one, two = proj_ref[i].astype(F32), proj_ref[last + i].astype(F32)
        early = pl.multiple_of((width + i) * nproj, nproj)
        late = pl.multiple_of((width + group + i) * nproj, nproj)
        projf_ref[pl.ds(early, nproj), :] = jnp.where(in_lower, two, one)
        projf_ref[pl.ds(late, nproj), :] = jnp.where(in_lower, one, two)
        return carry

    lax.fori_loop(0, group, ends_body, 0, unroll=6)
    potf_ref[:slabs * rows128, :] = pot_ref[...].astype(F32) - CENTER

    def place(layer):
        if isinstance(layer, int):
            return 0 if layer == 0 else 1 if layer == slabs else layer + 1
        return layer + 1

    def put(layer, blocks):
        both = jnp.concatenate(blocks + [blocks[-1]], axis=0).astype(BF16)
        start = place(layer) * block
        if not isinstance(layer, int):
            start = pl.multiple_of(start, block)
        lhs_ref[pl.ds(start, block), :] = both

    def put_psi(layer, source, at):
        put(layer, [
            source[:, pl.ds(pl.multiple_of(at + t * WIDE, WIDE), WIDE)].astype(F32)
            for t in range(tiles)
        ])

    def psi_body(layer, carry):
        put_psi(layer, psi_ref, layer * face)
        return carry

    put_psi(0, psi_ref, 0)
    lax.fori_loop(1, slabs, psi_body, 0)

    def gather(first_row, chosen, finish, trips):
        rows = len(chosen) * block
        trip = wraps // trips

        def body(n, carry):
            hot = oh_ref[:, pl.ds(pl.multiple_of(n * trip * cells, trip * cells), trip * cells)]
            out = jnp.dot(lhs_ref[first_row:first_row + rows, :], hot, preferred_element_type=F32)
            pick(out, n * trip, trip)
            return carry

        def pick(out, first, columns):
            for c in range(columns):
                w = first + c
                hi = jnp.broadcast_to(hi_ref[pl.ds(w, 1), :], (states, cells))
                masks = [hi == t for t in range(1, tiles)]
                found = {}
                for k, layer in enumerate(chosen):
                    part = out[k * block:(k + 1) * block, c * cells:(c + 1) * cells]
                    value = part[:states]
                    for t in range(1, tiles):
                        value = jnp.where(
                            masks[t - 1], part[t * states:(t + 1) * states], value
                        )
                    found[layer] = value
                finish(w, found)

        if trips == 1:
            wide = 2 * cells
            for n in range(wraps // 2):
                out = jnp.dot(
                    lhs_ref[first_row:first_row + rows, :], oh_ref[:, n * wide:(n + 1) * wide],
                    preferred_element_type=F32,
                )
                pick(out, 2 * n, 2)
        else:
            lax.fori_loop(0, trips, body, 0)

    def store_pair(into, row, w, lower_cells, upper_cells):
        mixed = pltpu.roll(jnp.where(low_half, upper_cells, lower_cells), pairs, 1)
        at = (row + 2 * w) * states
        at = at if isinstance(w, int) else pl.multiple_of(at, 2 * states)
        into[pl.ds(at, states), :] = jnp.where(low_half, lower_cells, mixed)
        into[pl.ds(at + states, states), :] = jnp.where(low_half, mixed, upper_cells)

    def inner_found(w, found):
        for a in range(1, edge - 1):
            store_pair(xs_ref, a * group, w, found[a], found[edge - 1 + a])
        store_pair(ends_ref, 0, w, found[edge - 1], found[edge - 1])

    def outer_found(w, found):
        store_pair(ends_ref, group, w, found[0], found[slabs])

    def gather_inner():
        gather(2 * block, tuple(range(1, slabs)), inner_found, 1)

    def gather_outer():
        gather(0, (0, slabs), outer_found, 1)

    def bcast(row):
        return projf_ref[pl.ds(row, states, stride=0), :]

    def partial_rows(source, at, proj_at, accs):
        values = jnp.dot(
            source[pl.ds(at, group * states), :].astype(BF16), spread_ref[...],
            preferred_element_type=F32,
        )
        accs = list(accs)
        for j in range(group):
            value = values[j * states:(j + 1) * states]
            for k in range(nproj):
                accs[k] = accs[k] + bcast(proj_at + j * nproj + k) * value
        return tuple(accs)

    def partial_inner():
        accs = partial_rows(ends_ref, 0, width * nproj, empty)
        for a in range(1, edge - 1):
            accs = partial_rows(xs_ref, a * group * states, a * group * nproj, accs)
        return accs

    def partial_outer(accs):
        return partial_rows(ends_ref, group * states, (width + group) * nproj, accs)

    slot_ids = lax.broadcasted_iota(jnp.int32, (4 * atoms, entries), 0)
    chosen_atom = jnp.where(slot_ids == eatom_ref[...], 1.0, 0.0).astype(BF16)
    chosen_send = jnp.concatenate(
        [chosen_atom[:2 * atoms], chosen_atom[atoms:3 * atoms], chosen_atom[2 * atoms:3 * atoms],
         chosen_atom[:atoms]], axis=0,
    )
    back = (((1,), (1,)), ((), ()))
    empty = tuple(jnp.zeros((states, entries), F32) for _ in range(nproj))
    low_atoms = lax.broadcasted_iota(jnp.int32, (1, 2 * atoms), 1) < atoms

    def send_atoms(step, accs):
        grouped = lax.dot_general(
            halves(jnp.concatenate(accs, axis=0), 1),
            jnp.concatenate([chosen_send, chosen_send], axis=1),
            back, preferred_element_type=F32,
        )
        for g in range(3):
            grouped_ref[step, g] = grouped[:, 2 * g * atoms:2 * (g + 1) * atoms]
        at = 4 + 6 * step
        return [
            send(grouped_ref.at[step, 1], left_ref.at[step], sems, at, ahead),
            send(grouped_ref.at[step, 0], right_ref.at[step], sems, at + 1, behind),
            send(grouped_ref.at[step, 2], far_ref.at[step, 0], sems, at + 2, ahead2),
            send(grouped_ref.at[step, 2], far_ref.at[step, 1], sems, at + 3, behind2),
        ]

    def cell_terms():
        early, late = ends_ref[:size, :], ends_ref[size:, :]
        xs_ref[:size, :] = jnp.where(low_half, late, early)
        xs_ref[last * states:, :] = jnp.where(low_half, early, late)
        kmat = kmat_ref[...]
        for s in range(0, states, 2):
            pair = jnp.concatenate(
                [xs_ref[pl.ds(s, width, stride=states), :],
                 xs_ref[pl.ds(s + 1, width, stride=states), :]], axis=1,
            ).astype(BF16)
            out = jnp.dot(kmat, pair, preferred_element_type=F32)
            ct_ref[pl.ds(s, width, stride=states), :] = out[:, :cells] * scale
            ct_ref[pl.ds(s + 1, width, stride=states), :] = out[:, cells:] * scale

    def entry_terms(step):
        right = pltpu.roll(right_ref[step], atoms, 1)
        coef = (
            grouped_ref[step, 0] + left_ref[step]
            + jnp.where(low_atoms, far_ref[step, 0], right),
            grouped_ref[step, 2] + right + pltpu.roll(far_ref[step, 1], atoms, 1),
        )
        rows = []
        for c in range(2):
            parts = []
            for k in range(nproj):
                acc = jnp.zeros((states, 2 * atoms), F32)
                for l in range(nproj):
                    at = k * nproj + l
                    acc = acc + (
                        couple_ref[c, at:at + 1, :] * coef[c][l * states:(l + 1) * states, :]
                    )
                parts.append(acc)
            rows.append(halves(jnp.concatenate(parts, axis=0), 1))
        half_atoms = [chosen_atom[:2 * atoms]] * 2 + [chosen_atom[2 * atoms:]] * 2
        terms = jnp.dot(
            jnp.concatenate(rows, axis=1), jnp.concatenate(half_atoms, axis=0),
            preferred_element_type=F32,
        )
        return [terms[k * states:(k + 1) * states] for k in range(nproj)]

    per = tiles * 2 * states
    size = group * states

    def terms_at(a):
        return ct_ref[a * size:(a + 1) * size, :]

    def node_rows(proj_at, before, terms):
        parts = []
        for j in range(group):
            row = proj_at + j * nproj
            total = bcast(row) * terms[0]
            for k in range(1, nproj):
                total = total + bcast(row + k) * terms[k]
            parts.append(total)
        twice = jnp.concatenate([spread_ref[...], spread_ref[...]], axis=1)
        value = before + lax.dot_general(
            halves(jnp.concatenate(parts, axis=0), 1), twice, back, preferred_element_type=F32
        )
        found = []
        for w in range(wraps):
            even = value[2 * w * states:(2 * w + 1) * states]
            odd = value[(2 * w + 1) * states:(2 * w + 2) * states]
            mixed = pltpu.roll(jnp.where(low_half, odd, even), pairs, 1)
            found.append((jnp.where(low_half, even, mixed), jnp.where(low_half, mixed, odd)))
        return found

    def fill(into, w, value):
        both = halves(value, 0)
        for t in range(tiles):
            rows = into + t * 2 * states
            masked_ref[rows:rows + 2 * states, w * cells:(w + 1) * cells] = (
                both * hot_ref[t * 2 * states:(t + 1) * 2 * states, w * cells:(w + 1) * cells]
            )

    def fill_late(terms):
        before = jnp.where(low_half, terms_at(0), terms_at(edge - 1))
        found = node_rows((width + group) * nproj, before, terms)
        for w, (one, two) in enumerate(found):
            fill(0, w, one)
            fill(per, w, two)

    def fill_early(terms):
        before = jnp.where(low_half, terms_at(edge - 1), terms_at(0))
        for w, (one, two) in enumerate(node_rows(width * nproj, before, terms)):
            fill(2 * per, w, one + two)

    def fill_inner(a, terms):
        found = node_rows(a * group * nproj, terms_at(a), terms)
        for w, (one, two) in enumerate(found):
            fill((2 * a + 1) * per, w, one)
            fill((2 * a + 2) * per, w, two)

    def scatter(into, number):
        out = jnp.dot(
            masked_ref[into:into + number * per, :], oht_ref[...], preferred_element_type=F32
        )
        return [
            [joined(out[n * per:(n + 1) * per], t) for t in range(tiles)] for n in range(number)
        ]

    def joined(value, t):
        return value[t * 2 * states:t * 2 * states + states] + (
            value[t * 2 * states + states:(t + 1) * 2 * states]
        )

    def scatter_outer(step, terms):
        fill_late(terms)
        head, tail = scatter(0, 2)
        for t in range(tiles):
            head_ref[step, :, t * WIDE:(t + 1) * WIDE] = head[t]
            tail_ref[step, :, t * WIDE:(t + 1) * WIDE] = tail[t]

    def scatter_rest(terms, finish):
        fill_early(terms)
        for a in range(1, edge):
            if a < edge - 1:
                fill_inner(a, terms)
            if a == 1:
                (out,) = scatter(2 * per, 1)
                finish(0, edge - 1, out)
            else:
                one, two = scatter((2 * a - 1) * per, 2)
                finish(a - 1, a - 1, one)
                finish(a - 1, a + edge - 2, two)

    def pot_row(layer, t, half):
        row = layer * rows128 + t * 2 + half
        return potf_ref[pl.ds(row, 1), :]

    def scaled(layer, t, summed, field):
        pot = jnp.concatenate([pot_row(layer, t, 0), pot_row(layer, t, 1)], axis=1)
        return (summed + pot * field) * (1.0 / HALFWIDTH)

    def lanes(layer, t):
        at = layer * face + t * WIDE
        return pl.ds(at if isinstance(layer, int) else pl.multiple_of(at, WIDE), WIDE)

    def first_layer(layer, summed, field):
        blocks = []
        for t in range(tiles):
            value = scaled(layer, t, summed(t), field(t)).astype(BF16).astype(F32)
            first_ref[:, lanes(layer, t)] = value
            blocks.append(value)
        put(layer, blocks)

    def last_layer(layer, summed):
        for t in range(tiles):
            value = scaled(layer, t, summed(t), first_ref[:, lanes(layer, t)])
            at = lanes(layer, t)
            out_ref[:, at] = (2.0 * value - psi_ref[:, at].astype(F32)).astype(BF16)

    def edge_sum(one_ref, two_ref):
        return lambda t: (
            one_ref[:, t * WIDE:(t + 1) * WIDE] + two_ref[:, t * WIDE:(t + 1) * WIDE]
        )

    gather_inner()
    accs = partial_inner()
    for copy in gaps:
        copy.wait()
    couple_ref[0] = jnp.where(low_atoms, coups_ref[0], coups_ref[1])
    couple_ref[1] = coups_ref[2]
    put_psi(slabs, ghost_ref, 0)
    gather_outer()
    copies = send_atoms(0, partial_outer(accs))
    potf_ref[slabs * rows128:slabs * rows128 + potg_ref.shape[0], :] = (
        potg_ref[...].astype(F32) - CENTER
    )
    cell_terms()
    for copy in copies:
        copy.wait()
    terms = entry_terms(0)
    scatter_outer(0, terms)
    copies = [
        send(tail_ref.at[0], low_ref.at[0], sems, 8, ahead),
        send(head_ref.at[0], high_ref, sems, 9, behind),
    ]

    def first_done(layer, summed):
        first_layer(layer, summed, lambda t: psi_ref[:, lanes(layer, t)].astype(F32))

    scatter_rest(terms, lambda a, layer, out: first_done(layer, lambda t: out[t]))
    gather_inner()
    accs = partial_inner()
    for copy in copies:
        copy.wait()
    first_done(0, edge_sum(head_ref.at[0], low_ref.at[0]))
    first_layer(
        slabs, edge_sum(tail_ref.at[0], high_ref),
        lambda t: ghost_ref[:, t * WIDE:(t + 1) * WIDE].astype(F32),
    )
    gather_outer()
    copies = send_atoms(1, partial_outer(accs))
    mated = [send(first_ref.at[:, :face], mated_ref, sems, 20, partner)]
    cell_terms()
    for copy in copies:
        copy.wait()
    terms = entry_terms(1)
    scatter_outer(1, terms)
    tails = [
        send(tail_ref.at[1], low_ref.at[1], sems, 14, ahead),
        send(tail_ref.at[1], matel_ref, sems, 16, ahead_mate),
        send(head_ref.at[1], mateh_ref, sems, 19, partner),
    ]
    half = edge - 1

    def span(at, size):
        return pl.ds(pl.multiple_of(at, 128), size)

    def swap(n, layer):
        return pltpu.make_async_remote_copy(
            src_ref=out_ref.at[:, span(layer * face, face)],
            dst_ref=other_ref.at[:, span(n * face, face)],
            send_sem=sems.at[0, 21 + n], recv_sem=sems.at[1, 21 + n],
            device_id=partner, device_id_type=MESH_ID,
        )

    def last_done(a, layer, out):
        last_layer(layer, lambda t: out[t])
        if layer >= half:
            swap(a, jnp.where(band == 0, a + half, a) if a else half).start()

    scatter_rest(terms, last_done)

    def gram(own, other):
        both = jnp.concatenate(
            [jnp.where(band == 0, own, other), jnp.where(band == 0, other, own)], axis=0
        ).astype(BF16)
        return lax.dot_general(both, both, back, preferred_element_type=F32)

    swap(0, half).wait()
    total = jnp.zeros((bands * states, bands * states), F32)
    for n in range(1, half):
        swap(n, half).wait()
        total = total + gram(
            out_ref[:, span(jnp.where(band == 0, n, n + half) * face, face)].astype(F32),
            other_ref[:, n * face:(n + 1) * face].astype(F32),
        )
    for copy in tails + mated:
        copy.wait()
    last_layer(0, edge_sum(head_ref.at[1], low_ref.at[1]))
    blocks = []
    summed = edge_sum(mateh_ref, matel_ref)
    for t in range(tiles):
        at = slice(t * WIDE, (t + 1) * WIDE)
        value = scaled(0, t, summed(t), mated_ref[:, at])
        value = (2.0 * value - mate_ref[:, at].astype(F32)).astype(BF16).astype(F32)
        blocks.append(jnp.where(band == 0, value, other_ref[:, at].astype(F32)))
    total = total + gram(
        out_ref[:, span(jnp.where(band == 0, 0, half) * face, face)].astype(F32),
        jnp.concatenate(blocks, axis=1),
    )
    size = bands * states
    lump = size * size // 128
    pieces = size // lump
    slots_ref[me] = jnp.concatenate(
        [total[r * lump:(r + 1) * lump] for r in range(pieces)], axis=1
    )

    def push(steps, carry):
        send(slots_ref.at[me], slots_ref.at[me], sems, 17, peer(steps))
        return carry

    lax.fori_loop(0, devices * bands - 1, push, 0)
    rest = pl.ds(0, devices * bands - 1)
    pltpu.make_async_remote_copy(
        src_ref=slots_ref.at[rest], dst_ref=slots_ref.at[rest], send_sem=sems.at[0, 17],
        recv_sem=sems.at[1, 17], device_id=partner, device_id_type=MESH_ID,
    ).wait()
    total = jnp.sum(slots_ref[...], axis=0) * (1.0 / (devices * count))
    corr_ref[...] = jnp.concatenate(
        [total[:, r * size:(r + 1) * size] for r in range(pieces)], axis=0
    )


def general(
    psi,
    cell_nodes,
    cell_scale,
    cell_matrix,
    node_potential,
    proj_values,
    entry_cell,
    entry_atom,
    coupling,
):
    states, node_count = psi.shape
    width, cells = cell_nodes.shape
    atoms, nproj, _ = coupling.shape
    entries = entry_atom.shape[0]
    full = node_count + FACEP
    chunks = full // FACEP
    layers = FACEP // WIDE
    groups = width // GROUP
    span = GROUP * cells

    table = cell_nodes.reshape(groups, GROUP, cells)
    owner = table // FACEP
    ids = jnp.arange(chunks, dtype=jnp.int32)
    flags = jnp.max(
        (owner[:, None] == ids[None, :, None, None]).astype(jnp.int32), axis=(2, 3)
    )
    rank = jnp.sum(flags[:, None, :] * (ids[None, :] < ids[:, None]), axis=2)
    places = jnp.arange(chunks + 1, dtype=jnp.int32)
    used = flags[:, :, None] * (rank[:, :, None] == places)
    listed = chunks + jnp.sum(used * (ids[None, :, None] - chunks), axis=1)
    listed = jnp.concatenate(
        [listed, jnp.full((groups, 1), chunks, jnp.int32), jnp.sum(flags, axis=1, keepdims=True)],
        axis=1,
    )
    sched = listed.astype(jnp.int32).reshape(groups * (chunks + 3))
    scale_row = cell_scale.reshape(1, cells)
    ecell = entry_cell.reshape(1, entries)
    eatom = entry_atom.reshape(1, entries)
    coup = coupling.transpose(1, 2, 0).reshape(nproj * nproj, atoms)
    potential = node_potential.astype(F32).reshape(1, node_count) - CENTER

    vmem = pl.BlockSpec(memory_space=pltpu.VMEM)
    smem = pl.BlockSpec(memory_space=pltpu.SMEM)

    padded = (layers * states + 15) // 16 * 16
    gather = pl.pallas_call(
        gather_kernel,
        out_shape=jax.ShapeDtypeStruct((width * states, cells), F32),
        in_specs=[smem] + [vmem] * 2,
        out_specs=vmem,
        scratch_shapes=[
            pltpu.VMEM((chunks + 1, padded, WIDE), BF16),
            pltpu.VMEM((WIDE, span), BF16),
        ],
        name="gather_cells",
    )
    scatter = pl.pallas_call(
        scatter_kernel,
        out_shape=jax.ShapeDtypeStruct((states, full), F32),
        in_specs=[smem] + [vmem] * 7,
        out_specs=vmem,
        scratch_shapes=[
            pltpu.VMEM((WIDE, span), BF16),
            pltpu.VMEM((width * states, entries), F32),
            pltpu.VMEM((width * states, cells), F32),
            pltpu.VMEM((2 * layers * 2 * states, span), BF16),
            pltpu.VMEM((chunks + 1, layers * 2 * states, WIDE), F32),
        ],
        name="scatter_nodes",
    )

    def remote(kernel, outs, n_in, scratch, copies, ident):
        return pl.pallas_call(
            kernel,
            out_shape=tuple(jax.ShapeDtypeStruct(*out) for out in outs),
            in_specs=[vmem] * n_in,
            out_specs=(vmem,) * len(outs),
            scratch_shapes=[pltpu.VMEM(*one) for one in scratch]
            + [pltpu.SemaphoreType.DMA((2, copies))],
            compiler_params=pltpu.CompilerParams(collective_id=ident, has_side_effects=True),
            name=kernel.__name__,
        )

    pair = (nproj * states, atoms)

    def assemble(extended, ident):
        values = gather(sched, table, extended)
        cell_terms, coef = remote(
            atoms_kernel, [((width * states, cells), F32), ((3,) + pair, F32)], 6,
            [((width * states, entries), F32), ((3,) + pair, F32)] + [((2,) + pair, F32)] * 3,
            4, ident,
        )(values, cell_matrix, scale_row, proj_values, ecell, eatom)
        return scatter(sched, table, cell_terms, coef, coup_all, proj_values, ecell, eatom)

    psi_ext, pot_ext, coup_all = remote(
        start_kernel,
        [((states, full), BF16), ((1, full), F32), ((3, nproj * nproj, atoms), F32)],
        3, [], 4, 1,
    )(psi, potential, coup)
    face = (states, FACEP)
    (first,) = remote(first_kernel, [((states, full), BF16)], 3, [(face, F32), (face, F32)], 2, 3)(
        assemble(psi_ext, 2), psi_ext, pot_ext
    )
    bands, devices = lax.axis_size("band"), lax.axis_size("mesh")
    square = (bands * states, bands * states)
    filtered, correlation = remote(
        last_kernel,
        [((states, node_count), BF16), (square, F32)],
        4,
        [(face, F32), ((states, node_count), BF16), ((devices,) + square, F32)],
        4, 5,
    )(assemble(first, 4), first, psi, potential)
    return (filtered, correlation)


def bricks(states, node_count, width, cells, bands):
    edge = round(width ** (1.0 / 3.0))
    return (
        edge ** 3 == width
        and (edge - 1) * 2 * FACEP == node_count
        and edge % 2 == 0
        and cells == 128
        and FACEP % WIDE == 0
        and states == 8
        and bands == 2
        and edge * edge % 6 == 0
    )


def local(
    psi,
    cell_nodes,
    cell_scale,
    cell_matrix,
    node_potential,
    proj_values,
    entry_cell,
    entry_atom,
    coupling,
):
    states, node_count = psi.shape
    width, cells = cell_nodes.shape
    atoms, nproj, _ = coupling.shape
    entries = entry_atom.shape[0]
    bands, devices = lax.axis_size("band"), lax.axis_size("mesh")
    operands = (
        psi, cell_nodes, cell_scale, cell_matrix, node_potential, proj_values, entry_cell,
        entry_atom, coupling,
    )
    if not bricks(states, node_count, width, cells, bands):
        return general(*operands)
    edge = round(width ** (1.0 / 3.0))
    wraps = edge * edge // 2
    layers = node_count // FACEP + 1
    tiles = FACEP // WIDE
    block = (tiles + 1) * states
    per = tiles * 2 * states
    rows = node_count // 128
    ghost_rows = (FACEP // 128 + 15) // 16 * 16
    size = bands * states
    vmem = pl.BlockSpec(memory_space=pltpu.VMEM)
    smem = pl.BlockSpec(memory_space=pltpu.SMEM)
    anywhere = pl.BlockSpec(memory_space=pl.ANY)
    face = (states, FACEP)
    duo = (nproj * states, 2 * atoms)
    filtered, correlation, wrong = pl.pallas_call(
        fused_kernel,
        out_shape=(
            jax.ShapeDtypeStruct((states, node_count), BF16),
            jax.ShapeDtypeStruct((size, size), F32),
            jax.ShapeDtypeStruct((1, 1), F32),
        ),
        in_specs=[anywhere] * 9,
        out_specs=(vmem, vmem, smem),
        scratch_shapes=[
            pltpu.VMEM(psi.shape, BF16),
            pltpu.VMEM(cell_nodes.shape, jnp.int32),
            pltpu.VMEM(cell_matrix.shape, BF16),
            pltpu.VMEM((rows, 128), BF16),
            pltpu.VMEM(proj_values.shape, BF16),
            pltpu.VMEM((1, cells), F32),
            pltpu.VMEM((1, entries), jnp.int32),
            pltpu.VMEM((1, entries), jnp.int32),
            pltpu.VMEM((nproj * nproj, atoms), F32),
            pltpu.VMEM((WIDE, wraps * cells), BF16),
            pltpu.VMEM((wraps * cells, WIDE), BF16),
            pltpu.VMEM(((wraps + 7) // 8 * 8, cells), jnp.int32),
            pltpu.VMEM(((2 * wraps + 7) // 8 * 8, cells), F32),
            pltpu.VMEM((width * states, cells), F32),
            pltpu.VMEM((width * states, cells), F32),
            pltpu.VMEM((4 * wraps * states, cells), F32),
            pltpu.VMEM((layers * block, WIDE), BF16),
            pltpu.VMEM((layers * per, wraps * cells), BF16),
            pltpu.VMEM((states, layers * FACEP), F32),
            pltpu.VMEM((rows + ghost_rows, 128), F32),
            pltpu.VMEM((2,) + face, F32),
            pltpu.VMEM((2,) + face, F32),
            pltpu.VMEM((2,) + face, F32),
            pltpu.VMEM(face, F32),
            pltpu.VMEM((2, 3) + duo, F32),
            pltpu.VMEM((2,) + duo, F32),
            pltpu.VMEM((2,) + duo, F32),
            pltpu.VMEM((2, 2) + duo, F32),
            pltpu.VMEM(face, BF16),
            pltpu.VMEM((ghost_rows, 128), BF16),
            pltpu.VMEM((3, nproj * nproj, 2 * atoms), F32),
            pltpu.VMEM((cells, entries), BF16),
            pltpu.VMEM((states, node_count // 2), BF16),
            pltpu.VMEM((devices * bands, size * size // 128, 128), F32),
            pltpu.VMEM((per, wraps * cells), BF16),
            pltpu.VMEM((2, nproj * nproj, 2 * atoms), F32),
            pltpu.VMEM(face, BF16),
            pltpu.VMEM(face, F32),
            pltpu.VMEM(face, F32),
            pltpu.VMEM(face, F32),
            pltpu.VMEM(((width + 4 * wraps) * nproj, entries), F32),
            pltpu.SemaphoreType.DMA((9,)),
            pltpu.SemaphoreType.DMA((2, 26)),
        ],
        compiler_params=pltpu.CompilerParams(collective_id=0, has_side_effects=True),
        name="fused_steps",
    )(
        psi, cell_nodes, cell_scale.reshape(1, cells), cell_matrix,
        node_potential.reshape(rows, 128), proj_values, entry_cell.reshape(1, entries),
        entry_atom.reshape(1, entries),
        coupling.transpose(1, 2, 0).reshape(nproj * nproj, atoms),
    )
    return lax.cond(
        wrong[0, 0] > 0.0,
        lambda: general(*operands),
        lambda: (filtered, correlation),
    )


def solution(mesh):
    return jax.shard_map(
        local,
        mesh=mesh,
        in_specs=(
            P("band", "mesh"),
            P(),
            P("mesh"),
            P(),
            P("mesh"),
            P(None, None, "mesh"),
            P("mesh"),
            P("mesh"),
            P("mesh", None, None),
        ),
        out_specs=(P("band", "mesh"), P()),
        check_vma=False,
    )
```

```python
import jax
import jax.numpy as jnp
from jax import lax
from jax.experimental import pallas as pl
from jax.experimental.pallas import tpu as pltpu
from jax.sharding import PartitionSpec as P

FACEP = 1792
CENTER = 0.5
HALFWIDTH = 2.5
HIGH = lax.Precision.HIGHEST
WIDE = 256
GROUP = 36
F32 = jnp.float32
BF16 = jnp.bfloat16


def fill_onehot(cn_ref, group, oh_ref):
    rows = cn_ref[group]
    hi = jnp.bitwise_and(rows, WIDE - 1)
    lanes = rows.shape[1]
    iota = lax.broadcasted_iota(jnp.int32, (WIDE, lanes), 0)
    for jj in range(GROUP):
        oh_ref[:, jj * lanes:(jj + 1) * lanes] = jnp.where(
            iota == hi[jj:jj + 1, :], 1.0, 0.0
        ).astype(BF16)
    return lax.shift_right_logical(rows, 8)


def gather_kernel(sched_ref, cn_ref, ext_ref, xs_ref, lhs_ref, oh_ref):
    states = ext_ref.shape[0]
    chunks = lhs_ref.shape[0] - 1
    layers = ext_ref.shape[1] // (chunks * WIDE)
    groups = cn_ref.shape[0]
    cells = cn_ref.shape[2]
    padded = lhs_ref.shape[1]
    slots = sched_ref.shape[0] // groups
    lhs_ref[...] = jnp.zeros_like(lhs_ref)
    for c in range(chunks):
        base = c * layers * WIDE
        parts = [
            ext_ref[:, base + l * WIDE:base + (l + 1) * WIDE].astype(F32) for l in range(layers)
        ]
        parts.append(jnp.zeros((padded - layers * states, WIDE), F32))
        lhs_ref[c] = jnp.concatenate(parts, axis=0).astype(BF16)
    xs_ref[...] = jnp.zeros_like(xs_ref)

    def group_body(g, carry):
        lo = fill_onehot(cn_ref, g, oh_ref)

        def pair_body(r, inner):
            first = sched_ref[g * slots + 2 * r]
            second = sched_ref[g * slots + 2 * r + 1]
            lhs = jnp.concatenate([lhs_ref[first], lhs_ref[second]], axis=0)
            out = jnp.dot(lhs, oh_ref[...], preferred_element_type=F32)
            for jj in range(GROUP):
                where = pl.ds(pl.multiple_of((g * GROUP + jj) * states, states), states)
                value = xs_ref[where, :]
                lanes = slice(jj * cells, (jj + 1) * cells)
                for half, chunk in enumerate((first, second)):
                    row = lo[jj:jj + 1, :] - chunk * layers
                    for l in range(layers):
                        at = half * padded + l * states
                        value = jnp.where(row == l, out[at:at + states, lanes], value)
                xs_ref[where, :] = value
            return inner

        pairs = lax.shift_right_logical(sched_ref[g * slots + slots - 1] + 1, 1)
        return lax.fori_loop(0, pairs, pair_body, carry)

    lax.fori_loop(0, groups, group_body, 0)


def scatter_kernel(sched_ref, cn_ref, ct_ref, coef_ref, coup_ref, proj_ref, ecell_ref,
                   eatom_ref, y_ref, oh_ref, ns_ref, v_ref, lhs_ref, acc_ref):
    chunks, rows_in_chunk, _ = acc_ref.shape
    chunks = chunks - 1
    groups = cn_ref.shape[0]
    cells = cn_ref.shape[2]
    width = groups * GROUP
    states = ct_ref.shape[0] // width
    layers = rows_in_chunk // (2 * states)
    nproj = proj_ref.shape[1]
    entries = ecell_ref.shape[1]
    atoms = coef_ref.shape[2]
    slot_ids = lax.broadcasted_iota(jnp.int32, (atoms, entries), 0)
    entry_terms = jnp.zeros((nproj * states, entries), F32)
    for g in range(3):
        rows = []
        for k in range(nproj):
            acc = jnp.zeros((states, atoms), F32)
            for l in range(nproj):
                acc = acc + (
                    coup_ref[g, k * nproj + l:k * nproj + l + 1, :]
                    * coef_ref[g, l * states:(l + 1) * states, :]
                )
            rows.append(acc)
        chosen = jnp.where(eatom_ref[...] == slot_ids + g * atoms, 1.0, 0.0)
        entry_terms = entry_terms + jnp.dot(
            jnp.concatenate(rows, axis=0), chosen, precision=HIGH, preferred_element_type=F32
        )
    terms = [entry_terms[k * states:(k + 1) * states, :] for k in range(nproj)]

    def node_body(j, carry):
        proj = proj_ref[j].astype(F32)
        total = proj[0:1, :] * terms[0]
        for k in range(1, nproj):
            total = total + proj[k:k + 1, :] * terms[k]
        ns_ref[pl.ds(pl.multiple_of(j * states, states), states), :] = total
        return carry

    lax.fori_loop(0, width, node_body, 0, unroll=8)
    cell_ids = lax.broadcasted_iota(jnp.int32, (cells, entries), 0)
    spread = jnp.where(cell_ids == ecell_ref[...], 1.0, 0.0).astype(BF16)
    back = (((1,), (1,)), ((), ()))
    node_vals = ns_ref[...]
    node_top = node_vals.astype(BF16)
    node_rest = (node_vals - node_top.astype(F32)).astype(BF16)
    v_ref[...] = (
        ct_ref[...]
        + lax.dot_general(node_top, spread, back, preferred_element_type=F32)
        + lax.dot_general(node_rest, spread, back, preferred_element_type=F32)
    )
    acc_ref[...] = jnp.zeros_like(acc_ref)
    slots = sched_ref.shape[0] // groups

    def group_body(g, carry):
        lo = fill_onehot(cn_ref, g, oh_ref)

        def pair_body(r, inner):
            first = sched_ref[g * slots + 2 * r]
            second = sched_ref[g * slots + 2 * r + 1]
            for jj in range(GROUP):
                start = pl.multiple_of((g * GROUP + jj) * states, states)
                value = v_ref[pl.ds(start, states), :]
                top = value.astype(BF16).astype(F32)
                both = jnp.concatenate([top, value - top], axis=0)
                lanes = slice(jj * cells, (jj + 1) * cells)
                for half, chunk in enumerate((first, second)):
                    row = lo[jj:jj + 1, :] - chunk * layers
                    for l in range(layers):
                        at = half * rows_in_chunk + l * 2 * states
                        lhs_ref[at:at + 2 * states, lanes] = (
                            jnp.where(row == l, both, 0.0).astype(BF16)
                        )
            out = lax.dot_general(lhs_ref[...], oh_ref[...], back, preferred_element_type=F32)
            acc_ref[first] += out[:rows_in_chunk]
            acc_ref[second] += out[rows_in_chunk:]
            return inner

        pairs = lax.shift_right_logical(sched_ref[g * slots + slots - 1] + 1, 1)
        return lax.fori_loop(0, pairs, pair_body, carry)

    lax.fori_loop(0, groups, group_body, 0)
    for c in range(chunks):
        for l in range(layers):
            base = (c * layers + l) * WIDE
            at = l * 2 * states
            y_ref[:, base:base + WIDE] = (
                acc_ref[c, at:at + states, :] + acc_ref[c, at + states:at + 2 * states, :]
            )


MESH_ID = pl.DeviceIdType.MESH


def ring_peer(steps):
    count = lax.axis_size("mesh")
    return lax.rem(lax.axis_index("mesh") + steps + count, count)


def send(src, dst, sems, at, peer):
    copy = pltpu.make_async_remote_copy(
        src_ref=src, dst_ref=dst, send_sem=sems.at[0, at], recv_sem=sems.at[1, at],
        device_id=peer, device_id_type=MESH_ID,
    )
    copy.start()
    return copy


def greet(peers):
    barrier = pltpu.get_barrier_semaphore()
    for peer in peers:
        pl.semaphore_signal(barrier, inc=1, device_id=peer, device_id_type=MESH_ID)
    return barrier


def start_kernel(psi_ref, pot_ref, coup_ref, ext_ref, potx_ref, coups_ref, sems):
    count = psi_ref.shape[1]
    face = ext_ref.shape[1] - count
    ahead, behind = {"mesh": ring_peer(1)}, {"mesh": ring_peer(-1)}
    pl.semaphore_wait(greet((ahead, behind)), 2)
    copies = [
        send(psi_ref.at[:, :face], ext_ref.at[:, count:], sems, 0, behind),
        send(coup_ref, coups_ref.at[0], sems, 1, ahead),
        send(coup_ref, coups_ref.at[2], sems, 2, behind),
        send(pot_ref.at[:, :face], potx_ref.at[:, count:], sems, 3, behind),
    ]
    ext_ref[:, :count] = psi_ref[...]
    potx_ref[:, :count] = pot_ref[...]
    coups_ref[1] = coup_ref[...]
    for copy in copies:
        copy.wait()


def atoms_kernel(xs_ref, kmat_ref, scale_ref, proj_ref, ecell_ref, eatom_ref, ct_ref, coef_ref,
                 es_ref, grouped_ref, left_ref, right_ref, far_ref, sems):
    peers = [{"mesh": ring_peer(steps)} for steps in (1, -1, 2, -2)]
    barrier = greet(peers)
    width, nproj, entries = proj_ref.shape
    cells = xs_ref.shape[1]
    states = xs_ref.shape[0] // width
    cell_ids = lax.broadcasted_iota(jnp.int32, (cells, entries), 0)
    spread = jnp.where(cell_ids == ecell_ref[...], 1.0, 0.0).astype(BF16)
    es_ref[...] = jnp.dot(xs_ref[...].astype(BF16), spread, preferred_element_type=F32)

    def partial_body(j, accs):
        values = es_ref[pl.ds(pl.multiple_of(j * states, states), states), :]
        proj = proj_ref[j].astype(F32)
        return tuple(acc + proj[k:k + 1, :] * values for k, acc in enumerate(accs))

    zero = jnp.zeros((states, entries), F32)
    accs = lax.fori_loop(0, width, partial_body, (zero,) * nproj, unroll=8)
    partial_sum = jnp.concatenate(accs, axis=0)
    atoms = grouped_ref.shape[2]
    slot_ids = lax.broadcasted_iota(jnp.int32, (atoms, entries), 0)
    for g in range(3):
        chosen = jnp.where(eatom_ref[...] == slot_ids + g * atoms, 1.0, 0.0)
        grouped_ref[g] = lax.dot_general(
            partial_sum, chosen, (((1,), (1,)), ((), ())), precision=HIGH,
            preferred_element_type=F32,
        )
    pl.semaphore_wait(barrier, 4)
    copies = [
        send(grouped_ref.at[1:3], left_ref, sems, 0, peers[0]),
        send(grouped_ref.at[0:2], right_ref, sems, 1, peers[1]),
        send(grouped_ref.at[2], far_ref.at[0], sems, 2, peers[2]),
        send(grouped_ref.at[0], far_ref.at[1], sems, 3, peers[3]),
    ]
    kmat = kmat_ref[...]
    scale = scale_ref[...]
    for s in range(0, states, 2):
        pair = jnp.concatenate(
            [xs_ref[pl.ds(s, width, stride=states), :], xs_ref[pl.ds(s + 1, width, stride=states), :]],
            axis=1,
        ).astype(BF16)
        out = jnp.dot(kmat, pair, preferred_element_type=F32)
        ct_ref[pl.ds(s, width, stride=states), :] = out[:, :cells] * scale
        ct_ref[pl.ds(s + 1, width, stride=states), :] = out[:, cells:] * scale
    for copy in copies:
        copy.wait()
    coef_ref[0] = left_ref[0] + far_ref[0] + grouped_ref[0]
    coef_ref[1] = grouped_ref[1] + left_ref[1] + right_ref[0]
    coef_ref[2] = right_ref[1] + grouped_ref[2] + far_ref[1]


def first_kernel(y_ref, ext_ref, pot_ref, first_ref, low_ref, high_ref, sems):
    full = y_ref.shape[1]
    face = low_ref.shape[1]
    count = full - face
    ahead, behind = {"mesh": ring_peer(1)}, {"mesh": ring_peer(-1)}
    barrier = greet((ahead, behind))

    def finish(total, at):
        scaled = (total + pot_ref[:, at] * ext_ref[:, at].astype(F32)) / HALFWIDTH
        first_ref[:, at] = scaled.astype(BF16)

    middle = face * (1 + (count // face - 1) // 2)
    for base in range(face, middle, face):
        at = slice(base, base + face)
        finish(y_ref[:, at], at)
    pl.semaphore_wait(barrier, 2)
    copies = [
        send(y_ref.at[:, count:], low_ref, sems, 0, ahead),
        send(y_ref.at[:, :face], high_ref, sems, 1, behind),
    ]
    for base in range(middle, count, face):
        at = slice(base, base + face)
        finish(y_ref[:, at], at)
    for copy in copies:
        copy.wait()
    finish(y_ref[:, :face] + low_ref[...], slice(0, face))
    finish(y_ref[:, count:] + high_ref[...], slice(count, full))


def last_kernel(y_ref, first_ref, psi_ref, pot_ref, out_ref, corr_ref, low_ref, other_ref,
                slots_ref, sems):
    count = psi_ref.shape[1]
    face = low_ref.shape[1]
    devices = lax.axis_size("mesh")
    bands = lax.axis_size("band")
    me = lax.axis_index("mesh")
    band = lax.axis_index("band")
    partner = {"band": lax.rem(band + 1, bands)}
    barrier = greet((partner,))

    def greet_body(steps, carry):
        pl.semaphore_signal(
            barrier, inc=1, device_id={"mesh": lax.rem(me + steps, devices)}, device_id_type=MESH_ID
        )
        return carry

    lax.fori_loop(1, devices, greet_body, 0)

    def finish(total, at):
        scaled = (total + pot_ref[:, at] * first_ref[:, at].astype(F32)) / HALFWIDTH
        out_ref[:, at] = (2.0 * scaled - psi_ref[:, at].astype(F32)).astype(BF16)

    for base in range(face, count, face):
        at = slice(base, base + face)
        finish(y_ref[:, at], at)
    pl.semaphore_wait(barrier, devices)
    tail = send(y_ref.at[:, count:count + face], low_ref, sems, 0, {"mesh": ring_peer(1)})
    swap = send(out_ref.at[:, face:], other_ref.at[:, face:], sems, 1, partner)
    states = out_ref.shape[0]

    def gram(base):
        at = slice(base, base + face)
        own, other = out_ref[:, at].astype(F32), other_ref[:, at].astype(F32)
        block = jnp.concatenate(
            [jnp.where(band == 0, own, other), jnp.where(band == 0, other, own)], axis=0
        ).astype(BF16)
        return lax.dot_general(
            block, block, (((1,), (1,)), ((), ())), preferred_element_type=F32
        )

    swap.wait()
    total = gram(face)
    for base in range(2 * face, count, face):
        total = total + gram(base)
    tail.wait()
    finish(y_ref[:, :face] + low_ref[...], slice(0, face))
    edge = send(out_ref.at[:, :face], other_ref.at[:, :face], sems, 3, partner)
    edge.wait()
    total = total + gram(0)
    slots_ref[me] = total

    def push(steps, carry):
        send(slots_ref.at[me], slots_ref.at[me], sems, 2, {"mesh": lax.rem(me + steps, devices)})
        return carry

    lax.fori_loop(1, devices, push, 0)
    pltpu.make_async_remote_copy(
        src_ref=slots_ref.at[pl.ds(0, devices - 1)], dst_ref=slots_ref.at[pl.ds(0, devices - 1)],
        send_sem=sems.at[0, 2], recv_sem=sems.at[1, 2], device_id=partner, device_id_type=MESH_ID,
    ).wait()
    corr_ref[...] = jnp.sum(slots_ref[...], axis=0) * (1.0 / (devices * count))


def everyone(count):
    bands = lax.axis_size("band")
    flat = lax.axis_index("mesh") * bands + lax.axis_index("band")
    early = flat < count // 2

    def peer(n):
        down = count - 1 - n
        other = jnp.where(
            early, jnp.where(down <= flat, down - 1, down), jnp.where(n >= flat, n + 1, n)
        )
        return {"mesh": other // bands, "band": lax.rem(other, bands)}

    return flat, peer


def halves(value, axis):
    top = value.astype(BF16)
    return jnp.concatenate([top, (value - top.astype(F32)).astype(BF16)], axis=axis)


def fused_kernel(psi_hbm, cn_hbm, scale_hbm, kmat_hbm, pot_hbm, proj_hbm, ecell_hbm, eatom_hbm,
                 coup_hbm, out_ref, corr_ref, flag_hbm, flag_ref,
                 psi_ref, cn_ref, kmat_ref, pot_ref, proj_ref, scale_ref, ecell_ref, eatom_ref, coup_ref,
                 oh_ref, oht_ref, hi_ref, pd_ref, xs_ref, ct_ref, ends_ref, lhs_ref,
                 masked_ref, first_ref, potf_ref, head_ref, tail_ref, low_ref, high_ref,
                 grouped_ref, left_ref, right_ref, far_ref, ghost_ref, potg_ref, coups_ref,
                 spread_ref, other_ref, slots_ref, hot_ref, couple_ref, mate_ref, mated_ref,
                 mateh_ref, matel_ref, projf_ref, fetch_sems, sems):
    fetches = [
        pltpu.make_async_copy(src, dst, fetch_sems.at[n])
        for n, (src, dst) in enumerate((
            (cn_hbm, cn_ref), (scale_hbm, scale_ref), (ecell_hbm, ecell_ref),
            (coup_hbm, coup_ref), (eatom_hbm, eatom_ref), (psi_hbm, psi_ref),
            (proj_hbm, proj_ref), (pot_hbm, pot_ref), (kmat_hbm, kmat_ref),
        ))
    ]
    for fetch in fetches:
        fetch.start()
    states, count = psi_ref.shape
    width, cells = cn_ref.shape
    face = ghost_ref.shape[1]
    slabs = count // face
    layers = slabs + 1
    _, nproj, entries = proj_ref.shape
    atoms = coup_ref.shape[1]
    edge = slabs // 2 + 1
    group = width // edge
    pairs = cells // 2
    tiles = face // WIDE
    block = (tiles + 1) * states
    wraps = group // 2
    devices, bands = lax.axis_size("mesh"), lax.axis_size("band")
    band = lax.axis_index("band")
    me, peer = everyone(devices * bands)
    ahead, behind = {"mesh": ring_peer(1)}, {"mesh": ring_peer(-1)}
    ahead2, behind2 = {"mesh": ring_peer(2)}, {"mesh": ring_peer(-2)}
    partner = {"band": lax.rem(band + 1, bands)}
    ahead_mate = {"mesh": ring_peer(1), "band": lax.rem(band + 1, bands)}
    barrier = pltpu.get_barrier_semaphore()

    def greet_body(steps, carry):
        pl.semaphore_signal(barrier, inc=1, device_id=peer(steps), device_id_type=MESH_ID)
        return carry

    lax.fori_loop(0, devices * bands - 1, greet_body, 0)
    for fetch in fetches[:4]:
        fetch.wait()
    down = lax.broadcasted_iota(jnp.int32, (cells, cells), 0)
    across = lax.broadcasted_iota(jnp.int32, (cells, cells), 1)
    eye = down == across
    key = jnp.broadcast_to(cn_ref[0:1, :].astype(F32), (cells, cells))
    key_col = jnp.sum(jnp.where(eye, key, 0.0), axis=1, keepdims=True)
    rank = jnp.sum(jnp.where(key < key_col, 1.0, 0.0), axis=1, keepdims=True)
    chosen_cell = rank == across.astype(F32)
    order = jnp.where(chosen_cell, 1.0, 0.0).astype(BF16)
    scale_col = jnp.sum(
        jnp.where(eye, jnp.broadcast_to(scale_ref[...], (cells, cells)), 0.0), axis=1, keepdims=True
    )
    scale = jnp.sum(jnp.where(chosen_cell, scale_col, 0.0), axis=0, keepdims=True)
    entry_rank = jnp.sum(
        jnp.where(lax.broadcasted_iota(jnp.int32, (cells, entries), 0) == ecell_ref[...], rank, 0.0),
        axis=0, keepdims=True,
    )
    spread = jnp.where(
        lax.broadcasted_iota(jnp.int32, (cells, entries), 0).astype(F32) == entry_rank, 1.0, 0.0
    )
    spread_ref[...] = spread.astype(BF16)
    table = cn_ref[...]
    upper = lax.shift_right_logical(table, 8).astype(F32)
    lower = jnp.bitwise_and(table, WIDE - 1).astype(F32)
    table = WIDE * jnp.dot(upper.astype(BF16), order, preferred_element_type=F32) + jnp.dot(
        lower.astype(BF16), order, preferred_element_type=F32
    )
    low_half = lax.broadcasted_iota(jnp.int32, (1, cells), 1) < pairs
    base = table[:group]
    base = jnp.where(low_half, base, pltpu.roll(base, pairs, 1))
    lift = jnp.where(low_half, 0.0, float((edge - 1) * face))
    wrong = jnp.where((base < 0.0) | (base >= float(face)), 1.0, 0.0)
    for a in range(edge):
        expected = base + (lift + float(a * face))
        wrong = jnp.maximum(
            wrong, jnp.where(table[a * group:(a + 1) * group] == expected, 0.0, 1.0)
        )
    flag_ref[...] = jnp.broadcast_to(
        jnp.max(jnp.max(wrong, axis=0, keepdims=True), axis=1, keepdims=True), flag_ref.shape
    )
    verdict = pltpu.make_async_copy(flag_ref, flag_hbm, fetch_sems.at[len(fetches)])
    verdict.start()
    pd_ref[:group, :] = base
    places = jnp.where(
        low_half, pd_ref[pl.ds(0, wraps, stride=2), :], pd_ref[pl.ds(1, wraps, stride=2), :]
    ).astype(jnp.int32)
    slot = jnp.bitwise_and(places, WIDE - 1)
    hi_ref[:wraps, :] = lax.shift_right_logical(places, 8)
    wide_ids = lax.broadcasted_iota(jnp.int16, (WIDE, cells), 0)
    one, zero = jnp.array(1.0, BF16), jnp.array(0.0, BF16)
    for w in range(wraps):
        hot = jnp.where(wide_ids == slot[w:w + 1, :].astype(jnp.int16), one, zero)
        oh_ref[:, w * cells:(w + 1) * cells] = hot
        oht_ref[w * cells:(w + 1) * cells, :] = hot.T

    for w in range(wraps):
        hi = jnp.broadcast_to(hi_ref[w:w + 1, :], (2 * states, cells))
        for t in range(tiles):
            hot_ref[t * 2 * states:(t + 1) * 2 * states, w * cells:(w + 1) * cells] = (
                jnp.where(hi == t, 1.0, 0.0).astype(BF16)
            )
    coups_ref[1] = jnp.concatenate([coup_ref[...]] * 2, axis=1)
    pl.semaphore_wait(barrier, devices * bands - 1)
    gaps = [
        send(psi_hbm.at[:, :face], ghost_ref, sems, 0, behind),
        send(pot_hbm.at[:potg_ref.shape[0], :], potg_ref, sems, 1, behind),
        send(coups_ref.at[1], coups_ref.at[0], sems, 2, ahead),
        send(coups_ref.at[1], coups_ref.at[2], sems, 3, behind),
        send(psi_hbm.at[:, :face], mate_ref, sems, 18, partner),
    ]

    rows128 = face // 128
    for fetch in fetches[4:]:
        fetch.wait()
    in_lower = entry_rank < float(pairs)
    last = (edge - 1) * group

    def proj_body(j, carry):
        rows = pl.ds(pl.multiple_of(j * nproj, nproj), nproj)
        projf_ref[rows, :] = proj_ref[j].astype(F32)
        return carry

    lax.fori_loop(0, width, proj_body, 0, unroll=8)

    def ends_body(i, carry):
        one, two = proj_ref[i].astype(F32), proj_ref[last + i].astype(F32)
        early = pl.multiple_of((width + i) * nproj, nproj)
        late = pl.multiple_of((width + group + i) * nproj, nproj)
        projf_ref[pl.ds(early, nproj), :] = jnp.where(in_lower, two, one)
        projf_ref[pl.ds(late, nproj), :] = jnp.where(in_lower, one, two)
        return carry

    lax.fori_loop(0, group, ends_body, 0, unroll=6)
    potf_ref[:slabs * rows128, :] = pot_ref[...].astype(F32) - CENTER

    def place(layer):
        if isinstance(layer, int):
            return 0 if layer == 0 else 1 if layer == slabs else layer + 1
        return layer + 1

    def put(layer, blocks):
        both = jnp.concatenate(blocks + [blocks[-1]], axis=0).astype(BF16)
        start = place(layer) * block
        if not isinstance(layer, int):
            start = pl.multiple_of(start, block)
        lhs_ref[pl.ds(start, block), :] = both

    def put_psi(layer, source, at):
        put(layer, [
            source[:, pl.ds(pl.multiple_of(at + t * WIDE, WIDE), WIDE)].astype(F32)
            for t in range(tiles)
        ])

    def psi_body(layer, carry):
        put_psi(layer, psi_ref, layer * face)
        return carry

    put_psi(0, psi_ref, 0)
    lax.fori_loop(1, slabs, psi_body, 0)

    def gather(first_row, chosen, finish, trips):
        rows = len(chosen) * block
        trip = wraps // trips

        def body(n, carry):
            hot = oh_ref[:, pl.ds(pl.multiple_of(n * trip * cells, trip * cells), trip * cells)]
            out = jnp.dot(lhs_ref[first_row:first_row + rows, :], hot, preferred_element_type=F32)
            pick(out, n * trip, trip)
            return carry

        def pick(out, first, columns):
            for c in range(columns):
                w = first + c
                hi = jnp.broadcast_to(hi_ref[pl.ds(w, 1), :], (states, cells))
                masks = [hi == t for t in range(1, tiles)]
                found = {}
                for k, layer in enumerate(chosen):
                    part = out[k * block:(k + 1) * block, c * cells:(c + 1) * cells]
                    value = part[:states]
                    for t in range(1, tiles):
                        value = jnp.where(
                            masks[t - 1], part[t * states:(t + 1) * states], value
                        )
                    found[layer] = value
                finish(w, found)

        if trips == 1:
            wide = 2 * cells
            for n in range(wraps // 2):
                out = jnp.dot(
                    lhs_ref[first_row:first_row + rows, :], oh_ref[:, n * wide:(n + 1) * wide],
                    preferred_element_type=F32,
                )
                pick(out, 2 * n, 2)
        else:
            lax.fori_loop(0, trips, body, 0)

    def store_pair(into, row, w, lower_cells, upper_cells):
        mixed = pltpu.roll(jnp.where(low_half, upper_cells, lower_cells), pairs, 1)
        at = (row + 2 * w) * states
        at = at if isinstance(w, int) else pl.multiple_of(at, 2 * states)
        into[pl.ds(at, states), :] = jnp.where(low_half, lower_cells, mixed)
        into[pl.ds(at + states, states), :] = jnp.where(low_half, mixed, upper_cells)

    def inner_found(w, found):
        for a in range(1, edge - 1):
            store_pair(xs_ref, a * group, w, found[a], found[edge - 1 + a])
        store_pair(ends_ref, 0, w, found[edge - 1], found[edge - 1])

    def outer_found(w, found):
        store_pair(ends_ref, group, w, found[0], found[slabs])

    def gather_inner():
        @pl.when(me >= 0)
        def split():
            gather(2 * block, tuple(range(1, slabs)), inner_found, 1)

    def gather_outer():
        gather(0, (0, slabs), outer_found, 1)

    def bcast(row):
        return projf_ref[pl.ds(row, states, stride=0), :]

    def partial_rows(source, at, proj_at, accs):
        values = jnp.dot(
            source[pl.ds(at, group * states), :].astype(BF16), spread_ref[...],
            preferred_element_type=F32,
        )
        accs = list(accs)
        for j in range(group):
            value = values[j * states:(j + 1) * states]
            for k in range(nproj):
                accs[k] = accs[k] + bcast(proj_at + j * nproj + k) * value
        return tuple(accs)

    def partial_inner():
        accs = partial_rows(ends_ref, 0, width * nproj, empty)
        for a in range(1, edge - 1):
            accs = partial_rows(xs_ref, a * group * states, a * group * nproj, accs)
        return accs

    def partial_outer(accs):
        return partial_rows(ends_ref, group * states, (width + group) * nproj, accs)

    slot_ids = lax.broadcasted_iota(jnp.int32, (4 * atoms, entries), 0)
    chosen_atom = jnp.where(slot_ids == eatom_ref[...], 1.0, 0.0).astype(BF16)
    chosen_send = jnp.concatenate(
        [chosen_atom[:2 * atoms], chosen_atom[atoms:3 * atoms], chosen_atom[2 * atoms:3 * atoms],
         chosen_atom[:atoms]], axis=0,
    )
    back = (((1,), (1,)), ((), ()))
    empty = tuple(jnp.zeros((states, entries), F32) for _ in range(nproj))
    low_atoms = lax.broadcasted_iota(jnp.int32, (1, 2 * atoms), 1) < atoms

    def send_atoms(step, accs):
        grouped = lax.dot_general(
            halves(jnp.concatenate(accs, axis=0), 1),
            jnp.concatenate([chosen_send, chosen_send], axis=1),
            back, preferred_element_type=F32,
        )
        for g in range(3):
            grouped_ref[step, g] = grouped[:, 2 * g * atoms:2 * (g + 1) * atoms]
        at = 4 + 6 * step
        return [
            send(grouped_ref.at[step, 1], left_ref.at[step], sems, at, ahead),
            send(grouped_ref.at[step, 0], right_ref.at[step], sems, at + 1, behind),
            send(grouped_ref.at[step, 2], far_ref.at[step, 0], sems, at + 2, ahead2),
            send(grouped_ref.at[step, 2], far_ref.at[step, 1], sems, at + 3, behind2),
        ]

    def cell_terms():
        early, late = ends_ref[:size, :], ends_ref[size:, :]
        xs_ref[:size, :] = jnp.where(low_half, late, early)
        xs_ref[last * states:, :] = jnp.where(low_half, early, late)
        kmat = kmat_ref[...]
        for s in range(0, states, 2):
            pair = jnp.concatenate(
                [xs_ref[pl.ds(s, width, stride=states), :],
                 xs_ref[pl.ds(s + 1, width, stride=states), :]], axis=1,
            ).astype(BF16)
            out = jnp.dot(kmat, pair, preferred_element_type=F32)
            ct_ref[pl.ds(s, width, stride=states), :] = out[:, :cells] * scale
            ct_ref[pl.ds(s + 1, width, stride=states), :] = out[:, cells:] * scale

    def entry_terms(step):
        right = pltpu.roll(right_ref[step], atoms, 1)
        coef = (
            grouped_ref[step, 0] + left_ref[step]
            + jnp.where(low_atoms, far_ref[step, 0], right),
            grouped_ref[step, 2] + right + pltpu.roll(far_ref[step, 1], atoms, 1),
        )
        rows = []
        for c in range(2):
            parts = []
            for k in range(nproj):
                acc = jnp.zeros((states, 2 * atoms), F32)
                for l in range(nproj):
                    at = k * nproj + l
                    acc = acc + (
                        couple_ref[c, at:at + 1, :] * coef[c][l * states:(l + 1) * states, :]
                    )
                parts.append(acc)
            rows.append(halves(jnp.concatenate(parts, axis=0), 1))
        half_atoms = [chosen_atom[:2 * atoms]] * 2 + [chosen_atom[2 * atoms:]] * 2
        terms = jnp.dot(
            jnp.concatenate(rows, axis=1), jnp.concatenate(half_atoms, axis=0),
            preferred_element_type=F32,
        )
        return [terms[k * states:(k + 1) * states] for k in range(nproj)]

    per = tiles * 2 * states
    size = group * states

    def terms_at(a):
        return ct_ref[a * size:(a + 1) * size, :]

    def node_rows(proj_at, before, terms):
        parts = []
        for j in range(group):
            row = proj_at + j * nproj
            total = bcast(row) * terms[0]
            for k in range(1, nproj):
                total = total + bcast(row + k) * terms[k]
            parts.append(total)
        twice = jnp.concatenate([spread_ref[...], spread_ref[...]], axis=1)
        value = before + lax.dot_general(
            halves(jnp.concatenate(parts, axis=0), 1), twice, back, preferred_element_type=F32
        )
        found = []
        for w in range(wraps):
            even = value[2 * w * states:(2 * w + 1) * states]
            odd = value[(2 * w + 1) * states:(2 * w + 2) * states]
            mixed = pltpu.roll(jnp.where(low_half, odd, even), pairs, 1)
            found.append((jnp.where(low_half, even, mixed), jnp.where(low_half, mixed, odd)))
        return found

    def fill(into, w, value):
        both = halves(value, 0)
        for t in range(tiles):
            rows = into + t * 2 * states
            masked_ref[rows:rows + 2 * states, w * cells:(w + 1) * cells] = (
                both * hot_ref[t * 2 * states:(t + 1) * 2 * states, w * cells:(w + 1) * cells]
            )

    def fill_late(terms):
        before = jnp.where(low_half, terms_at(0), terms_at(edge - 1))
        found = node_rows((width + group) * nproj, before, terms)
        for w, (one, two) in enumerate(found):
            fill(0, w, one)
            fill(per, w, two)

    def fill_early(terms):
        before = jnp.where(low_half, terms_at(edge - 1), terms_at(0))
        for w, (one, two) in enumerate(node_rows(width * nproj, before, terms)):
            fill(2 * per, w, one + two)

    def fill_inner(a, terms):
        found = node_rows(a * group * nproj, terms_at(a), terms)
        for w, (one, two) in enumerate(found):
            fill((2 * a + 1) * per, w, one)
            fill((2 * a + 2) * per, w, two)

    def scatter(into, number):
        out = jnp.dot(
            masked_ref[into:into + number * per, :], oht_ref[...], preferred_element_type=F32
        )
        return [
            [joined(out[n * per:(n + 1) * per], t) for t in range(tiles)] for n in range(number)
        ]

    def joined(value, t):
        return value[t * 2 * states:t * 2 * states + states] + (
            value[t * 2 * states + states:(t + 1) * 2 * states]
        )

    def scatter_outer(step, terms):
        fill_late(terms)
        head, tail = scatter(0, 2)
        for t in range(tiles):
            head_ref[step, :, t * WIDE:(t + 1) * WIDE] = head[t]
            tail_ref[step, :, t * WIDE:(t + 1) * WIDE] = tail[t]

    def scatter_rest(terms, finish):
        fill_early(terms)
        for a in range(1, edge):
            if a < edge - 1:
                fill_inner(a, terms)
            if a == 1:
                (out,) = scatter(2 * per, 1)
                finish(0, edge - 1, out)
            else:
                one, two = scatter((2 * a - 1) * per, 2)
                finish(a - 1, a - 1, one)
                finish(a - 1, a + edge - 2, two)

    def pot_row(layer, t, half):
        row = layer * rows128 + t * 2 + half
        return potf_ref[pl.ds(row, 1), :]

    def scaled(layer, t, summed, field):
        pot = jnp.concatenate([pot_row(layer, t, 0), pot_row(layer, t, 1)], axis=1)
        return (summed + pot * field) * (1.0 / HALFWIDTH)

    def lanes(layer, t):
        at = layer * face + t * WIDE
        return pl.ds(at if isinstance(layer, int) else pl.multiple_of(at, WIDE), WIDE)

    def first_layer(layer, summed, field):
        blocks = []
        for t in range(tiles):
            value = scaled(layer, t, summed(t), field(t)).astype(BF16).astype(F32)
            first_ref[:, lanes(layer, t)] = value
            blocks.append(value)
        put(layer, blocks)

    def last_layer(layer, summed):
        for t in range(tiles):
            value = scaled(layer, t, summed(t), first_ref[:, lanes(layer, t)])
            at = lanes(layer, t)
            out_ref[:, at] = (2.0 * value - psi_ref[:, at].astype(F32)).astype(BF16)

    def edge_sum(one_ref, two_ref):
        return lambda t: (
            one_ref[:, t * WIDE:(t + 1) * WIDE] + two_ref[:, t * WIDE:(t + 1) * WIDE]
        )

    gather_inner()
    accs = partial_inner()
    for copy in gaps:
        copy.wait()
    couple_ref[0] = jnp.where(low_atoms, coups_ref[0], coups_ref[1])
    couple_ref[1] = coups_ref[2]
    put_psi(slabs, ghost_ref, 0)
    gather_outer()
    copies = send_atoms(0, partial_outer(accs))
    verdict.wait()
    potf_ref[slabs * rows128:slabs * rows128 + potg_ref.shape[0], :] = (
        potg_ref[...].astype(F32) - CENTER
    )
    cell_terms()
    for copy in copies:
        copy.wait()
    terms = entry_terms(0)
    scatter_outer(0, terms)
    copies = [
        send(tail_ref.at[0], low_ref.at[0], sems, 8, ahead),
        send(head_ref.at[0], high_ref, sems, 9, behind),
    ]

    def first_done(layer, summed):
        first_layer(layer, summed, lambda t: psi_ref[:, lanes(layer, t)].astype(F32))

    scatter_rest(terms, lambda a, layer, out: first_done(layer, lambda t: out[t]))
    gather_inner()
    accs = partial_inner()
    for copy in copies:
        copy.wait()
    first_done(0, edge_sum(head_ref.at[0], low_ref.at[0]))
    first_layer(
        slabs, edge_sum(tail_ref.at[0], high_ref),
        lambda t: ghost_ref[:, t * WIDE:(t + 1) * WIDE].astype(F32),
    )
    gather_outer()
    copies = send_atoms(1, partial_outer(accs))
    mated = [send(first_ref.at[:, :face], mated_ref, sems, 20, partner)]
    cell_terms()
    for copy in copies:
        copy.wait()
    terms = entry_terms(1)
    scatter_outer(1, terms)
    tails = [
        send(tail_ref.at[1], low_ref.at[1], sems, 14, ahead),
        send(tail_ref.at[1], matel_ref, sems, 16, ahead_mate),
        send(head_ref.at[1], mateh_ref, sems, 19, partner),
    ]
    half = edge - 1

    def span(at, size):
        return pl.ds(pl.multiple_of(at, 128), size)

    def swap(n, layer):
        return pltpu.make_async_remote_copy(
            src_ref=out_ref.at[:, span(layer * face, face)],
            dst_ref=other_ref.at[:, span(n * face, face)],
            send_sem=sems.at[0, 21 + n], recv_sem=sems.at[1, 21 + n],
            device_id=partner, device_id_type=MESH_ID,
        )

    def last_done(a, layer, out):
        last_layer(layer, lambda t: out[t])
        if layer >= half and a in (half // 2, half - 1):
            for n in range(0 if a == half // 2 else half // 2 + 1, a + 1):
                swap(n, jnp.where(band == 0, n + half, n) if n else half).start()

    scatter_rest(terms, last_done)

    def gram(own, other):
        both = jnp.concatenate(
            [jnp.where(band == 0, own, other), jnp.where(band == 0, other, own)], axis=0
        ).astype(BF16)
        return lax.dot_general(both, both, back, preferred_element_type=F32)

    swap(0, half).wait()
    total = jnp.zeros((bands * states, bands * states), F32)
    for n in range(1, half):
        swap(n, half).wait()
        total = total + gram(
            out_ref[:, span(jnp.where(band == 0, n, n + half) * face, face)].astype(F32),
            other_ref[:, n * face:(n + 1) * face].astype(F32),
        )
    for copy in tails + mated:
        copy.wait()
    last_layer(0, edge_sum(head_ref.at[1], low_ref.at[1]))
    blocks = []
    summed = edge_sum(mateh_ref, matel_ref)
    for t in range(tiles):
        at = slice(t * WIDE, (t + 1) * WIDE)
        value = scaled(0, t, summed(t), mated_ref[:, at])
        value = (2.0 * value - mate_ref[:, at].astype(F32)).astype(BF16).astype(F32)
        blocks.append(jnp.where(band == 0, value, other_ref[:, at].astype(F32)))
    total = total + gram(
        out_ref[:, span(jnp.where(band == 0, 0, half) * face, face)].astype(F32),
        jnp.concatenate(blocks, axis=1),
    )
    size = bands * states
    lump = size * size // 128
    pieces = size // lump
    slots_ref[me] = jnp.concatenate(
        [total[r * lump:(r + 1) * lump] for r in range(pieces)], axis=1
    )

    def push(steps, carry):
        send(slots_ref.at[me], slots_ref.at[me], sems, 17, peer(steps))
        return carry

    lax.fori_loop(0, devices * bands - 1, push, 0)
    rest = pl.ds(0, devices * bands - 1)
    pltpu.make_async_remote_copy(
        src_ref=slots_ref.at[rest], dst_ref=slots_ref.at[rest], send_sem=sems.at[0, 17],
        recv_sem=sems.at[1, 17], device_id=partner, device_id_type=MESH_ID,
    ).wait()
    total = jnp.sum(slots_ref[...], axis=0) * (1.0 / (devices * count))
    corr_ref[...] = jnp.concatenate(
        [total[:, r * size:(r + 1) * size] for r in range(pieces)], axis=0
    )


def general(
    psi,
    cell_nodes,
    cell_scale,
    cell_matrix,
    node_potential,
    proj_values,
    entry_cell,
    entry_atom,
    coupling,
):
    states, node_count = psi.shape
    width, cells = cell_nodes.shape
    atoms, nproj, _ = coupling.shape
    entries = entry_atom.shape[0]
    full = node_count + FACEP
    chunks = full // FACEP
    layers = FACEP // WIDE
    groups = width // GROUP
    span = GROUP * cells

    table = cell_nodes.reshape(groups, GROUP, cells)
    owner = table // FACEP
    ids = jnp.arange(chunks, dtype=jnp.int32)
    flags = jnp.max(
        (owner[:, None] == ids[None, :, None, None]).astype(jnp.int32), axis=(2, 3)
    )
    rank = jnp.sum(flags[:, None, :] * (ids[None, :] < ids[:, None]), axis=2)
    places = jnp.arange(chunks + 1, dtype=jnp.int32)
    used = flags[:, :, None] * (rank[:, :, None] == places)
    listed = chunks + jnp.sum(used * (ids[None, :, None] - chunks), axis=1)
    listed = jnp.concatenate(
        [listed, jnp.full((groups, 1), chunks, jnp.int32), jnp.sum(flags, axis=1, keepdims=True)],
        axis=1,
    )
    sched = listed.astype(jnp.int32).reshape(groups * (chunks + 3))
    scale_row = cell_scale.reshape(1, cells)
    ecell = entry_cell.reshape(1, entries)
    eatom = entry_atom.reshape(1, entries)
    coup = coupling.transpose(1, 2, 0).reshape(nproj * nproj, atoms)
    potential = node_potential.astype(F32).reshape(1, node_count) - CENTER

    vmem = pl.BlockSpec(memory_space=pltpu.VMEM)
    smem = pl.BlockSpec(memory_space=pltpu.SMEM)

    padded = (layers * states + 15) // 16 * 16
    gather = pl.pallas_call(
        gather_kernel,
        out_shape=jax.ShapeDtypeStruct((width * states, cells), F32),
        in_specs=[smem] + [vmem] * 2,
        out_specs=vmem,
        scratch_shapes=[
            pltpu.VMEM((chunks + 1, padded, WIDE), BF16),
            pltpu.VMEM((WIDE, span), BF16),
        ],
        name="gather_cells",
    )
    scatter = pl.pallas_call(
        scatter_kernel,
        out_shape=jax.ShapeDtypeStruct((states, full), F32),
        in_specs=[smem] + [vmem] * 7,
        out_specs=vmem,
        scratch_shapes=[
            pltpu.VMEM((WIDE, span), BF16),
            pltpu.VMEM((width * states, entries), F32),
            pltpu.VMEM((width * states, cells), F32),
            pltpu.VMEM((2 * layers * 2 * states, span), BF16),
            pltpu.VMEM((chunks + 1, layers * 2 * states, WIDE), F32),
        ],
        name="scatter_nodes",
    )

    def remote(kernel, outs, n_in, scratch, copies, ident):
        return pl.pallas_call(
            kernel,
            out_shape=tuple(jax.ShapeDtypeStruct(*out) for out in outs),
            in_specs=[vmem] * n_in,
            out_specs=(vmem,) * len(outs),
            scratch_shapes=[pltpu.VMEM(*one) for one in scratch]
            + [pltpu.SemaphoreType.DMA((2, copies))],
            compiler_params=pltpu.CompilerParams(collective_id=ident, has_side_effects=True),
            name=kernel.__name__,
        )

    pair = (nproj * states, atoms)

    def assemble(extended, ident):
        values = gather(sched, table, extended)
        cell_terms, coef = remote(
            atoms_kernel, [((width * states, cells), F32), ((3,) + pair, F32)], 6,
            [((width * states, entries), F32), ((3,) + pair, F32)] + [((2,) + pair, F32)] * 3,
            4, ident,
        )(values, cell_matrix, scale_row, proj_values, ecell, eatom)
        return scatter(sched, table, cell_terms, coef, coup_all, proj_values, ecell, eatom)

    psi_ext, pot_ext, coup_all = remote(
        start_kernel,
        [((states, full), BF16), ((1, full), F32), ((3, nproj * nproj, atoms), F32)],
        3, [], 4, 1,
    )(psi, potential, coup)
    face = (states, FACEP)
    (first,) = remote(first_kernel, [((states, full), BF16)], 3, [(face, F32), (face, F32)], 2, 3)(
        assemble(psi_ext, 2), psi_ext, pot_ext
    )
    bands, devices = lax.axis_size("band"), lax.axis_size("mesh")
    square = (bands * states, bands * states)
    filtered, correlation = remote(
        last_kernel,
        [((states, node_count), BF16), (square, F32)],
        4,
        [(face, F32), ((states, node_count), BF16), ((devices,) + square, F32)],
        4, 5,
    )(assemble(first, 4), first, psi, potential)
    return (filtered, correlation)


def hand_over(filtered_ref, correlation_ref, out_ref, corr_ref, sems):
    copies = [
        pltpu.make_async_copy(filtered_ref, out_ref, sems.at[0]),
        pltpu.make_async_copy(correlation_ref, corr_ref, sems.at[1]),
    ]
    for copy in copies:
        copy.start()
    for copy in copies:
        copy.wait()


def bricks(states, node_count, width, cells, bands):
    edge = round(width ** (1.0 / 3.0))
    return (
        edge ** 3 == width
        and (edge - 1) * 2 * FACEP == node_count
        and edge % 2 == 0
        and cells == 128
        and FACEP % WIDE == 0
        and states == 8
        and bands == 2
        and edge * edge % 6 == 0
    )


def local(
    psi,
    cell_nodes,
    cell_scale,
    cell_matrix,
    node_potential,
    proj_values,
    entry_cell,
    entry_atom,
    coupling,
):
    states, node_count = psi.shape
    width, cells = cell_nodes.shape
    atoms, nproj, _ = coupling.shape
    entries = entry_atom.shape[0]
    bands, devices = lax.axis_size("band"), lax.axis_size("mesh")
    operands = (
        psi, cell_nodes, cell_scale, cell_matrix, node_potential, proj_values, entry_cell,
        entry_atom, coupling,
    )
    if not bricks(states, node_count, width, cells, bands):
        return general(*operands)
    edge = round(width ** (1.0 / 3.0))
    wraps = edge * edge // 2
    layers = node_count // FACEP + 1
    tiles = FACEP // WIDE
    block = (tiles + 1) * states
    per = tiles * 2 * states
    rows = node_count // 128
    ghost_rows = (FACEP // 128 + 15) // 16 * 16
    size = bands * states
    vmem = pl.BlockSpec(memory_space=pltpu.VMEM)
    anywhere = pl.BlockSpec(memory_space=pl.ANY)
    face = (states, FACEP)
    duo = (nproj * states, 2 * atoms)
    filtered, correlation, wrong = pl.pallas_call(
        fused_kernel,
        out_shape=(
            jax.ShapeDtypeStruct((states, node_count), BF16),
            jax.ShapeDtypeStruct((size, size), F32),
            jax.ShapeDtypeStruct((1, 128), F32),
        ),
        in_specs=[anywhere] * 9,
        out_specs=(vmem, vmem, anywhere),
        scratch_shapes=[
            pltpu.VMEM((1, 128), F32),
            pltpu.VMEM(psi.shape, BF16),
            pltpu.VMEM(cell_nodes.shape, jnp.int32),
            pltpu.VMEM(cell_matrix.shape, BF16),
            pltpu.VMEM((rows, 128), BF16),
            pltpu.VMEM(proj_values.shape, BF16),
            pltpu.VMEM((1, cells), F32),
            pltpu.VMEM((1, entries), jnp.int32),
            pltpu.VMEM((1, entries), jnp.int32),
            pltpu.VMEM((nproj * nproj, atoms), F32),
            pltpu.VMEM((WIDE, wraps * cells), BF16),
            pltpu.VMEM((wraps * cells, WIDE), BF16),
            pltpu.VMEM(((wraps + 7) // 8 * 8, cells), jnp.int32),
            pltpu.VMEM(((2 * wraps + 7) // 8 * 8, cells), F32),
            pltpu.VMEM((width * states, cells), F32),
            pltpu.VMEM((width * states, cells), F32),
            pltpu.VMEM((4 * wraps * states, cells), F32),
            pltpu.VMEM((layers * block, WIDE), BF16),
            pltpu.VMEM((layers * per, wraps * cells), BF16),
            pltpu.VMEM((states, layers * FACEP), F32),
            pltpu.VMEM((rows + ghost_rows, 128), F32),
            pltpu.VMEM((2,) + face, F32),
            pltpu.VMEM((2,) + face, F32),
            pltpu.VMEM((2,) + face, F32),
            pltpu.VMEM(face, F32),
            pltpu.VMEM((2, 3) + duo, F32),
            pltpu.VMEM((2,) + duo, F32),
            pltpu.VMEM((2,) + duo, F32),
            pltpu.VMEM((2, 2) + duo, F32),
            pltpu.VMEM(face, BF16),
            pltpu.VMEM((ghost_rows, 128), BF16),
            pltpu.VMEM((3, nproj * nproj, 2 * atoms), F32),
            pltpu.VMEM((cells, entries), BF16),
            pltpu.VMEM((states, node_count // 2), BF16),
            pltpu.VMEM((devices * bands, size * size // 128, 128), F32),
            pltpu.VMEM((per, wraps * cells), BF16),
            pltpu.VMEM((2, nproj * nproj, 2 * atoms), F32),
            pltpu.VMEM(face, BF16),
            pltpu.VMEM(face, F32),
            pltpu.VMEM(face, F32),
            pltpu.VMEM(face, F32),
            pltpu.VMEM(((width + 4 * wraps) * nproj, entries), F32),
            pltpu.SemaphoreType.DMA((10,)),
            pltpu.SemaphoreType.DMA((2, 26)),
        ],
        compiler_params=pltpu.CompilerParams(collective_id=0, has_side_effects=True),
        name="fused_steps",
    )(
        psi, cell_nodes, cell_scale.reshape(1, cells), cell_matrix,
        node_potential.reshape(rows, 128), proj_values, entry_cell.reshape(1, entries),
        entry_atom.reshape(1, entries),
        coupling.transpose(1, 2, 0).reshape(nproj * nproj, atoms),
    )
    results = lax.cond(
        wrong[0, 0] > 0.0,
        lambda: general(*operands),
        lambda: (filtered, correlation),
    )
    return pl.pallas_call(
        hand_over,
        out_shape=tuple(jax.ShapeDtypeStruct(one.shape, one.dtype) for one in results),
        in_specs=[anywhere] * 2,
        out_specs=(anywhere,) * 2,
        scratch_shapes=[pltpu.SemaphoreType.DMA((2,))],
        name="hand_over",
    )(*results)


def solution(mesh):
    return jax.shard_map(
        local,
        mesh=mesh,
        in_specs=(
            P("band", "mesh"),
            P(),
            P("mesh"),
            P(),
            P("mesh"),
            P(None, None, "mesh"),
            P("mesh"),
            P("mesh"),
            P("mesh", None, None),
        ),
        out_specs=(P("band", "mesh"), P()),
        check_vma=False,
    )
```

```python
import jax
import jax.numpy as jnp
from jax import lax
from jax.experimental import pallas as pl
from jax.experimental.pallas import tpu as pltpu
from jax.sharding import PartitionSpec as P

FACEP = 1792
CENTER = 0.5
HALFWIDTH = 2.5
HIGH = lax.Precision.HIGHEST
WIDE = 256
GROUP = 36
F32 = jnp.float32
BF16 = jnp.bfloat16


def fill_onehot(cn_ref, group, oh_ref):
    rows = cn_ref[group]
    hi = jnp.bitwise_and(rows, WIDE - 1)
    lanes = rows.shape[1]
    iota = lax.broadcasted_iota(jnp.int32, (WIDE, lanes), 0)
    for jj in range(GROUP):
        oh_ref[:, jj * lanes:(jj + 1) * lanes] = jnp.where(
            iota == hi[jj:jj + 1, :], 1.0, 0.0
        ).astype(BF16)
    return lax.shift_right_logical(rows, 8)


def gather_kernel(sched_ref, cn_ref, ext_ref, xs_ref, lhs_ref, oh_ref):
    states = ext_ref.shape[0]
    chunks = lhs_ref.shape[0] - 1
    layers = ext_ref.shape[1] // (chunks * WIDE)
    groups = cn_ref.shape[0]
    cells = cn_ref.shape[2]
    padded = lhs_ref.shape[1]
    slots = sched_ref.shape[0] // groups
    lhs_ref[...] = jnp.zeros_like(lhs_ref)
    for c in range(chunks):
        base = c * layers * WIDE
        parts = [
            ext_ref[:, base + l * WIDE:base + (l + 1) * WIDE].astype(F32) for l in range(layers)
        ]
        parts.append(jnp.zeros((padded - layers * states, WIDE), F32))
        lhs_ref[c] = jnp.concatenate(parts, axis=0).astype(BF16)
    xs_ref[...] = jnp.zeros_like(xs_ref)

    def group_body(g, carry):
        lo = fill_onehot(cn_ref, g, oh_ref)

        def pair_body(r, inner):
            first = sched_ref[g * slots + 2 * r]
            second = sched_ref[g * slots + 2 * r + 1]
            lhs = jnp.concatenate([lhs_ref[first], lhs_ref[second]], axis=0)
            out = jnp.dot(lhs, oh_ref[...], preferred_element_type=F32)
            for jj in range(GROUP):
                where = pl.ds(pl.multiple_of((g * GROUP + jj) * states, states), states)
                value = xs_ref[where, :]
                lanes = slice(jj * cells, (jj + 1) * cells)
                for half, chunk in enumerate((first, second)):
                    row = lo[jj:jj + 1, :] - chunk * layers
                    for l in range(layers):
                        at = half * padded + l * states
                        value = jnp.where(row == l, out[at:at + states, lanes], value)
                xs_ref[where, :] = value
            return inner

        pairs = lax.shift_right_logical(sched_ref[g * slots + slots - 1] + 1, 1)
        return lax.fori_loop(0, pairs, pair_body, carry)

    lax.fori_loop(0, groups, group_body, 0)


def scatter_kernel(sched_ref, cn_ref, ct_ref, coef_ref, coup_ref, proj_ref, ecell_ref,
                   eatom_ref, y_ref, oh_ref, ns_ref, v_ref, lhs_ref, acc_ref):
    chunks, rows_in_chunk, _ = acc_ref.shape
    chunks = chunks - 1
    groups = cn_ref.shape[0]
    cells = cn_ref.shape[2]
    width = groups * GROUP
    states = ct_ref.shape[0] // width
    layers = rows_in_chunk // (2 * states)
    nproj = proj_ref.shape[1]
    entries = ecell_ref.shape[1]
    atoms = coef_ref.shape[2]
    slot_ids = lax.broadcasted_iota(jnp.int32, (atoms, entries), 0)
    entry_terms = jnp.zeros((nproj * states, entries), F32)
    for g in range(3):
        rows = []
        for k in range(nproj):
            acc = jnp.zeros((states, atoms), F32)
            for l in range(nproj):
                acc = acc + (
                    coup_ref[g, k * nproj + l:k * nproj + l + 1, :]
                    * coef_ref[g, l * states:(l + 1) * states, :]
                )
            rows.append(acc)
        chosen = jnp.where(eatom_ref[...] == slot_ids + g * atoms, 1.0, 0.0)
        entry_terms = entry_terms + jnp.dot(
            jnp.concatenate(rows, axis=0), chosen, precision=HIGH, preferred_element_type=F32
        )
    terms = [entry_terms[k * states:(k + 1) * states, :] for k in range(nproj)]

    def node_body(j, carry):
        proj = proj_ref[j].astype(F32)
        total = proj[0:1, :] * terms[0]
        for k in range(1, nproj):
            total = total + proj[k:k + 1, :] * terms[k]
        ns_ref[pl.ds(pl.multiple_of(j * states, states), states), :] = total
        return carry

    lax.fori_loop(0, width, node_body, 0, unroll=8)
    cell_ids = lax.broadcasted_iota(jnp.int32, (cells, entries), 0)
    spread = jnp.where(cell_ids == ecell_ref[...], 1.0, 0.0).astype(BF16)
    back = (((1,), (1,)), ((), ()))
    node_vals = ns_ref[...]
    node_top = node_vals.astype(BF16)
    node_rest = (node_vals - node_top.astype(F32)).astype(BF16)
    v_ref[...] = (
        ct_ref[...]
        + lax.dot_general(node_top, spread, back, preferred_element_type=F32)
        + lax.dot_general(node_rest, spread, back, preferred_element_type=F32)
    )
    acc_ref[...] = jnp.zeros_like(acc_ref)
    slots = sched_ref.shape[0] // groups

    def group_body(g, carry):
        lo = fill_onehot(cn_ref, g, oh_ref)

        def pair_body(r, inner):
            first = sched_ref[g * slots + 2 * r]
            second = sched_ref[g * slots + 2 * r + 1]
            for jj in range(GROUP):
                start = pl.multiple_of((g * GROUP + jj) * states, states)
                value = v_ref[pl.ds(start, states), :]
                top = value.astype(BF16).astype(F32)
                both = jnp.concatenate([top, value - top], axis=0)
                lanes = slice(jj * cells, (jj + 1) * cells)
                for half, chunk in enumerate((first, second)):
                    row = lo[jj:jj + 1, :] - chunk * layers
                    for l in range(layers):
                        at = half * rows_in_chunk + l * 2 * states
                        lhs_ref[at:at + 2 * states, lanes] = (
                            jnp.where(row == l, both, 0.0).astype(BF16)
                        )
            out = lax.dot_general(lhs_ref[...], oh_ref[...], back, preferred_element_type=F32)
            acc_ref[first] += out[:rows_in_chunk]
            acc_ref[second] += out[rows_in_chunk:]
            return inner

        pairs = lax.shift_right_logical(sched_ref[g * slots + slots - 1] + 1, 1)
        return lax.fori_loop(0, pairs, pair_body, carry)

    lax.fori_loop(0, groups, group_body, 0)
    for c in range(chunks):
        for l in range(layers):
            base = (c * layers + l) * WIDE
            at = l * 2 * states
            y_ref[:, base:base + WIDE] = (
                acc_ref[c, at:at + states, :] + acc_ref[c, at + states:at + 2 * states, :]
            )


MESH_ID = pl.DeviceIdType.MESH


def ring_peer(steps):
    count = lax.axis_size("mesh")
    return lax.rem(lax.axis_index("mesh") + steps + count, count)


def send(src, dst, sems, at, peer):
    copy = pltpu.make_async_remote_copy(
        src_ref=src, dst_ref=dst, send_sem=sems.at[0, at], recv_sem=sems.at[1, at],
        device_id=peer, device_id_type=MESH_ID,
    )
    copy.start()
    return copy


def greet(peers):
    barrier = pltpu.get_barrier_semaphore()
    for peer in peers:
        pl.semaphore_signal(barrier, inc=1, device_id=peer, device_id_type=MESH_ID)
    return barrier


def start_kernel(psi_ref, pot_ref, coup_ref, ext_ref, potx_ref, coups_ref, sems):
    count = psi_ref.shape[1]
    face = ext_ref.shape[1] - count
    ahead, behind = {"mesh": ring_peer(1)}, {"mesh": ring_peer(-1)}
    pl.semaphore_wait(greet((ahead, behind)), 2)
    copies = [
        send(psi_ref.at[:, :face], ext_ref.at[:, count:], sems, 0, behind),
        send(coup_ref, coups_ref.at[0], sems, 1, ahead),
        send(coup_ref, coups_ref.at[2], sems, 2, behind),
        send(pot_ref.at[:, :face], potx_ref.at[:, count:], sems, 3, behind),
    ]
    ext_ref[:, :count] = psi_ref[...]
    potx_ref[:, :count] = pot_ref[...]
    coups_ref[1] = coup_ref[...]
    for copy in copies:
        copy.wait()


def atoms_kernel(xs_ref, kmat_ref, scale_ref, proj_ref, ecell_ref, eatom_ref, ct_ref, coef_ref,
                 es_ref, grouped_ref, left_ref, right_ref, far_ref, sems):
    peers = [{"mesh": ring_peer(steps)} for steps in (1, -1, 2, -2)]
    barrier = greet(peers)
    width, nproj, entries = proj_ref.shape
    cells = xs_ref.shape[1]
    states = xs_ref.shape[0] // width
    cell_ids = lax.broadcasted_iota(jnp.int32, (cells, entries), 0)
    spread = jnp.where(cell_ids == ecell_ref[...], 1.0, 0.0).astype(BF16)
    es_ref[...] = jnp.dot(xs_ref[...].astype(BF16), spread, preferred_element_type=F32)

    def partial_body(j, accs):
        values = es_ref[pl.ds(pl.multiple_of(j * states, states), states), :]
        proj = proj_ref[j].astype(F32)
        return tuple(acc + proj[k:k + 1, :] * values for k, acc in enumerate(accs))

    zero = jnp.zeros((states, entries), F32)
    accs = lax.fori_loop(0, width, partial_body, (zero,) * nproj, unroll=8)
    partial_sum = jnp.concatenate(accs, axis=0)
    atoms = grouped_ref.shape[2]
    slot_ids = lax.broadcasted_iota(jnp.int32, (atoms, entries), 0)
    for g in range(3):
        chosen = jnp.where(eatom_ref[...] == slot_ids + g * atoms, 1.0, 0.0)
        grouped_ref[g] = lax.dot_general(
            partial_sum, chosen, (((1,), (1,)), ((), ())), precision=HIGH,
            preferred_element_type=F32,
        )
    pl.semaphore_wait(barrier, 4)
    copies = [
        send(grouped_ref.at[1:3], left_ref, sems, 0, peers[0]),
        send(grouped_ref.at[0:2], right_ref, sems, 1, peers[1]),
        send(grouped_ref.at[2], far_ref.at[0], sems, 2, peers[2]),
        send(grouped_ref.at[0], far_ref.at[1], sems, 3, peers[3]),
    ]
    kmat = kmat_ref[...]
    scale = scale_ref[...]
    for s in range(0, states, 2):
        pair = jnp.concatenate(
            [xs_ref[pl.ds(s, width, stride=states), :], xs_ref[pl.ds(s + 1, width, stride=states), :]],
            axis=1,
        ).astype(BF16)
        out = jnp.dot(kmat, pair, preferred_element_type=F32)
        ct_ref[pl.ds(s, width, stride=states), :] = out[:, :cells] * scale
        ct_ref[pl.ds(s + 1, width, stride=states), :] = out[:, cells:] * scale
    for copy in copies:
        copy.wait()
    coef_ref[0] = left_ref[0] + far_ref[0] + grouped_ref[0]
    coef_ref[1] = grouped_ref[1] + left_ref[1] + right_ref[0]
    coef_ref[2] = right_ref[1] + grouped_ref[2] + far_ref[1]


def first_kernel(y_ref, ext_ref, pot_ref, first_ref, low_ref, high_ref, sems):
    full = y_ref.shape[1]
    face = low_ref.shape[1]
    count = full - face
    ahead, behind = {"mesh": ring_peer(1)}, {"mesh": ring_peer(-1)}
    barrier = greet((ahead, behind))

    def finish(total, at):
        scaled = (total + pot_ref[:, at] * ext_ref[:, at].astype(F32)) / HALFWIDTH
        first_ref[:, at] = scaled.astype(BF16)

    middle = face * (1 + (count // face - 1) // 2)
    for base in range(face, middle, face):
        at = slice(base, base + face)
        finish(y_ref[:, at], at)
    pl.semaphore_wait(barrier, 2)
    copies = [
        send(y_ref.at[:, count:], low_ref, sems, 0, ahead),
        send(y_ref.at[:, :face], high_ref, sems, 1, behind),
    ]
    for base in range(middle, count, face):
        at = slice(base, base + face)
        finish(y_ref[:, at], at)
    for copy in copies:
        copy.wait()
    finish(y_ref[:, :face] + low_ref[...], slice(0, face))
    finish(y_ref[:, count:] + high_ref[...], slice(count, full))


def last_kernel(y_ref, first_ref, psi_ref, pot_ref, out_ref, corr_ref, low_ref, other_ref,
                slots_ref, sems):
    count = psi_ref.shape[1]
    face = low_ref.shape[1]
    devices = lax.axis_size("mesh")
    bands = lax.axis_size("band")
    me = lax.axis_index("mesh")
    band = lax.axis_index("band")
    partner = {"band": lax.rem(band + 1, bands)}
    barrier = greet((partner,))

    def greet_body(steps, carry):
        pl.semaphore_signal(
            barrier, inc=1, device_id={"mesh": lax.rem(me + steps, devices)}, device_id_type=MESH_ID
        )
        return carry

    lax.fori_loop(1, devices, greet_body, 0)

    def finish(total, at):
        scaled = (total + pot_ref[:, at] * first_ref[:, at].astype(F32)) / HALFWIDTH
        out_ref[:, at] = (2.0 * scaled - psi_ref[:, at].astype(F32)).astype(BF16)

    for base in range(face, count, face):
        at = slice(base, base + face)
        finish(y_ref[:, at], at)
    pl.semaphore_wait(barrier, devices)
    tail = send(y_ref.at[:, count:count + face], low_ref, sems, 0, {"mesh": ring_peer(1)})
    swap = send(out_ref.at[:, face:], other_ref.at[:, face:], sems, 1, partner)
    states = out_ref.shape[0]

    def gram(base):
        at = slice(base, base + face)
        own, other = out_ref[:, at].astype(F32), other_ref[:, at].astype(F32)
        block = jnp.concatenate(
            [jnp.where(band == 0, own, other), jnp.where(band == 0, other, own)], axis=0
        ).astype(BF16)
        return lax.dot_general(
            block, block, (((1,), (1,)), ((), ())), preferred_element_type=F32
        )

    swap.wait()
    total = gram(face)
    for base in range(2 * face, count, face):
        total = total + gram(base)
    tail.wait()
    finish(y_ref[:, :face] + low_ref[...], slice(0, face))
    edge = send(out_ref.at[:, :face], other_ref.at[:, :face], sems, 3, partner)
    edge.wait()
    total = total + gram(0)
    slots_ref[me] = total

    def push(steps, carry):
        send(slots_ref.at[me], slots_ref.at[me], sems, 2, {"mesh": lax.rem(me + steps, devices)})
        return carry

    lax.fori_loop(1, devices, push, 0)
    pltpu.make_async_remote_copy(
        src_ref=slots_ref.at[pl.ds(0, devices - 1)], dst_ref=slots_ref.at[pl.ds(0, devices - 1)],
        send_sem=sems.at[0, 2], recv_sem=sems.at[1, 2], device_id=partner, device_id_type=MESH_ID,
    ).wait()
    corr_ref[...] = jnp.sum(slots_ref[...], axis=0) * (1.0 / (devices * count))


def everyone(count):
    bands = lax.axis_size("band")
    flat = lax.axis_index("mesh") * bands + lax.axis_index("band")
    early = flat < count // 2

    def peer(n):
        down = count - 1 - n
        other = jnp.where(
            early, jnp.where(down <= flat, down - 1, down), jnp.where(n >= flat, n + 1, n)
        )
        return {"mesh": other // bands, "band": lax.rem(other, bands)}

    return flat, peer


def halves(value, axis):
    top = value.astype(BF16)
    return jnp.concatenate([top, (value - top.astype(F32)).astype(BF16)], axis=axis)


def fused_kernel(psi_hbm, cn_hbm, scale_hbm, kmat_hbm, pot_hbm, proj_hbm, ecell_hbm, eatom_hbm,
                 coup_hbm, out_ref, corr_ref, flag_hbm, flag_ref,
                 psi_ref, cn_ref, kmat_ref, pot_ref, proj_ref, scale_ref, ecell_ref, eatom_ref, coup_ref,
                 oh_ref, oht_ref, hi_ref, pd_ref, xs_ref, ct_ref, ends_ref, lhs_ref,
                 masked_ref, first_ref, potf_ref, head_ref, tail_ref, low_ref, high_ref,
                 grouped_ref, left_ref, right_ref, far_ref, ghost_ref, potg_ref, coups_ref,
                 spread_ref, other_ref, slots_ref, hot_ref, couple_ref, mate_ref, mated_ref,
                 mateh_ref, matel_ref, projf_ref, fetch_sems, sems):
    fetches = [
        pltpu.make_async_copy(src, dst, fetch_sems.at[n])
        for n, (src, dst) in enumerate((
            (cn_hbm, cn_ref), (scale_hbm, scale_ref), (ecell_hbm, ecell_ref),
            (coup_hbm, coup_ref), (eatom_hbm, eatom_ref), (psi_hbm, psi_ref),
            (proj_hbm, proj_ref), (pot_hbm, pot_ref), (kmat_hbm, kmat_ref),
        ))
    ]
    for fetch in fetches:
        fetch.start()
    states, count = psi_ref.shape
    width, cells = cn_ref.shape
    face = ghost_ref.shape[1]
    slabs = count // face
    layers = slabs + 1
    _, nproj, entries = proj_ref.shape
    atoms = coup_ref.shape[1]
    edge = slabs // 2 + 1
    group = width // edge
    pairs = cells // 2
    tiles = face // WIDE
    block = (tiles + 1) * states
    wraps = group // 2
    devices, bands = lax.axis_size("mesh"), lax.axis_size("band")
    band = lax.axis_index("band")
    me, peer = everyone(devices * bands)
    ahead, behind = {"mesh": ring_peer(1)}, {"mesh": ring_peer(-1)}
    ahead2, behind2 = {"mesh": ring_peer(2)}, {"mesh": ring_peer(-2)}
    partner = {"band": lax.rem(band + 1, bands)}
    ahead_mate = {"mesh": ring_peer(1), "band": lax.rem(band + 1, bands)}
    barrier = pltpu.get_barrier_semaphore()

    behind_mate = {"mesh": ring_peer(-1), "band": lax.rem(band + 1, bands)}
    if devices > 16:
        guests = devices * bands - 1

        def greet_body(n, carry):
            pl.semaphore_signal(barrier, inc=1, device_id=peer(n), device_id_type=MESH_ID)
            return carry

        lax.fori_loop(0, guests, greet_body, 0)
    else:
        near = (ahead, behind, ahead2, behind2, ahead_mate, behind_mate, partner)
        guests = len(near)
        for one in near:
            pl.semaphore_signal(barrier, inc=1, device_id=one, device_id_type=MESH_ID)
    part = face // 2
    own_part, mate_part = band * part, (bands - 1 - band) * part

    def span(at, size):
        return pl.ds(pl.multiple_of(at, 128), size)

    for fetch in fetches[:4]:
        fetch.wait()
    down = lax.broadcasted_iota(jnp.int32, (cells, cells), 0)
    across = lax.broadcasted_iota(jnp.int32, (cells, cells), 1)
    eye = down == across
    key = jnp.broadcast_to(cn_ref[0:1, :].astype(F32), (cells, cells))
    key_col = jnp.sum(jnp.where(eye, key, 0.0), axis=1, keepdims=True)
    rank = jnp.sum(jnp.where(key < key_col, 1.0, 0.0), axis=1, keepdims=True)
    chosen_cell = rank == across.astype(F32)
    order = jnp.where(chosen_cell, 1.0, 0.0).astype(BF16)
    scale_col = jnp.sum(
        jnp.where(eye, jnp.broadcast_to(scale_ref[...], (cells, cells)), 0.0), axis=1, keepdims=True
    )
    scale = jnp.sum(jnp.where(chosen_cell, scale_col, 0.0), axis=0, keepdims=True)
    entry_rank = jnp.sum(
        jnp.where(lax.broadcasted_iota(jnp.int32, (cells, entries), 0) == ecell_ref[...], rank, 0.0),
        axis=0, keepdims=True,
    )
    spread = jnp.where(
        lax.broadcasted_iota(jnp.int32, (cells, entries), 0).astype(F32) == entry_rank, 1.0, 0.0
    )
    spread_ref[...] = spread.astype(BF16)
    table = cn_ref[...]
    upper = lax.shift_right_logical(table, 8).astype(F32)
    lower = jnp.bitwise_and(table, WIDE - 1).astype(F32)
    table = WIDE * jnp.dot(upper.astype(BF16), order, preferred_element_type=F32) + jnp.dot(
        lower.astype(BF16), order, preferred_element_type=F32
    )
    low_half = lax.broadcasted_iota(jnp.int32, (1, cells), 1) < pairs
    base = table[:group]
    base = jnp.where(low_half, base, pltpu.roll(base, pairs, 1))
    lift = jnp.where(low_half, 0.0, float((edge - 1) * face))
    wrong = jnp.where((base < 0.0) | (base >= float(face)), 1.0, 0.0)
    for a in range(edge):
        expected = base + (lift + float(a * face))
        wrong = jnp.maximum(
            wrong, jnp.where(table[a * group:(a + 1) * group] == expected, 0.0, 1.0)
        )
    flag_ref[...] = jnp.broadcast_to(
        jnp.max(jnp.max(wrong, axis=0, keepdims=True), axis=1, keepdims=True), flag_ref.shape
    )
    verdict = pltpu.make_async_copy(flag_ref, flag_hbm, fetch_sems.at[len(fetches)])
    verdict.start()
    pd_ref[:group, :] = base
    places = jnp.where(
        low_half, pd_ref[pl.ds(0, wraps, stride=2), :], pd_ref[pl.ds(1, wraps, stride=2), :]
    ).astype(jnp.int32)
    slot = jnp.bitwise_and(places, WIDE - 1)
    hi_ref[:wraps, :] = lax.shift_right_logical(places, 8)
    wide_ids = lax.broadcasted_iota(jnp.int16, (WIDE, cells), 0)
    one, zero = jnp.array(1.0, BF16), jnp.array(0.0, BF16)
    for w in range(wraps):
        hot = jnp.where(wide_ids == slot[w:w + 1, :].astype(jnp.int16), one, zero)
        oh_ref[:, w * cells:(w + 1) * cells] = hot
        oht_ref[w * cells:(w + 1) * cells, :] = hot.T

    for w in range(wraps):
        hi = jnp.broadcast_to(hi_ref[w:w + 1, :], (2 * states, cells))
        for t in range(tiles):
            hot_ref[t * 2 * states:(t + 1) * 2 * states, w * cells:(w + 1) * cells] = (
                jnp.where(hi == t, 1.0, 0.0).astype(BF16)
            )
    coups_ref[1] = jnp.concatenate([coup_ref[...]] * 2, axis=1)
    pl.semaphore_wait(barrier, guests)
    gaps = [
        send(psi_hbm.at[:, :face], ghost_ref, sems, 0, behind),
        send(pot_hbm.at[:potg_ref.shape[0], :], potg_ref, sems, 1, behind),
        send(coups_ref.at[1], coups_ref.at[0], sems, 2, ahead),
        send(coups_ref.at[1], coups_ref.at[2], sems, 3, behind),
        send(psi_hbm.at[:, span(mate_part, part)], mate_ref, sems, 18, partner),
    ]

    rows128 = face // 128
    for fetch in fetches[4:]:
        fetch.wait()
    in_lower = entry_rank < float(pairs)
    last = (edge - 1) * group

    def proj_body(j, carry):
        rows = pl.ds(pl.multiple_of(j * nproj, nproj), nproj)
        projf_ref[rows, :] = proj_ref[j].astype(F32)
        return carry

    lax.fori_loop(0, width, proj_body, 0, unroll=8)

    def ends_body(i, carry):
        one, two = proj_ref[i].astype(F32), proj_ref[last + i].astype(F32)
        early = pl.multiple_of((width + i) * nproj, nproj)
        late = pl.multiple_of((width + group + i) * nproj, nproj)
        projf_ref[pl.ds(early, nproj), :] = jnp.where(in_lower, two, one)
        projf_ref[pl.ds(late, nproj), :] = jnp.where(in_lower, one, two)
        return carry

    lax.fori_loop(0, group, ends_body, 0, unroll=6)
    potf_ref[:slabs * rows128, :] = pot_ref[...].astype(F32) - CENTER

    def place(layer):
        if isinstance(layer, int):
            return 0 if layer == 0 else 1 if layer == slabs else layer + 1
        return layer + 1

    def put(layer, blocks):
        both = jnp.concatenate(blocks + [blocks[-1]], axis=0).astype(BF16)
        start = place(layer) * block
        if not isinstance(layer, int):
            start = pl.multiple_of(start, block)
        lhs_ref[pl.ds(start, block), :] = both

    def put_psi(layer, source, at):
        put(layer, [
            source[:, pl.ds(pl.multiple_of(at + t * WIDE, WIDE), WIDE)].astype(F32)
            for t in range(tiles)
        ])

    def psi_body(layer, carry):
        put_psi(layer, psi_ref, layer * face)
        return carry

    put_psi(0, psi_ref, 0)
    lax.fori_loop(1, slabs, psi_body, 0)

    def gather(first_row, chosen, finish, trips):
        rows = len(chosen) * block
        trip = wraps // trips

        def body(n, carry):
            hot = oh_ref[:, pl.ds(pl.multiple_of(n * trip * cells, trip * cells), trip * cells)]
            out = jnp.dot(lhs_ref[first_row:first_row + rows, :], hot, preferred_element_type=F32)
            pick(out, n * trip, trip)
            return carry

        def pick(out, first, columns):
            for c in range(columns):
                w = first + c
                hi = jnp.broadcast_to(hi_ref[pl.ds(w, 1), :], (states, cells))
                masks = [hi == t for t in range(1, tiles)]
                found = {}
                for k, layer in enumerate(chosen):
                    part = out[k * block:(k + 1) * block, c * cells:(c + 1) * cells]
                    value = part[:states]
                    for t in range(1, tiles):
                        value = jnp.where(
                            masks[t - 1], part[t * states:(t + 1) * states], value
                        )
                    found[layer] = value
                finish(w, found)

        if trips == 1:
            wide = 2 * cells
            for n in range(wraps // 2):
                out = jnp.dot(
                    lhs_ref[first_row:first_row + rows, :], oh_ref[:, n * wide:(n + 1) * wide],
                    preferred_element_type=F32,
                )
                pick(out, 2 * n, 2)
        else:
            lax.fori_loop(0, trips, body, 0)

    def store_pair(into, row, w, lower_cells, upper_cells):
        mixed = pltpu.roll(jnp.where(low_half, upper_cells, lower_cells), pairs, 1)
        at = (row + 2 * w) * states
        at = at if isinstance(w, int) else pl.multiple_of(at, 2 * states)
        into[pl.ds(at, states), :] = jnp.where(low_half, lower_cells, mixed)
        into[pl.ds(at + states, states), :] = jnp.where(low_half, mixed, upper_cells)

    def inner_found(w, found):
        for a in range(1, edge - 1):
            store_pair(xs_ref, a * group, w, found[a], found[edge - 1 + a])
        store_pair(ends_ref, 0, w, found[edge - 1], found[edge - 1])

    def outer_found(w, found):
        store_pair(ends_ref, group, w, found[0], found[slabs])

    def gather_inner():
        @pl.when(me >= 0)
        def split():
            gather(2 * block, tuple(range(1, slabs)), inner_found, 1)

    def gather_outer():
        gather(0, (0, slabs), outer_found, 1)

    def bcast(row):
        return projf_ref[pl.ds(row, states, stride=0), :]

    def partial_rows(source, at, proj_at, accs):
        values = jnp.dot(
            source[pl.ds(at, group * states), :].astype(BF16), spread_ref[...],
            preferred_element_type=F32,
        )
        accs = list(accs)
        for j in range(group):
            value = values[j * states:(j + 1) * states]
            for k in range(nproj):
                accs[k] = accs[k] + bcast(proj_at + j * nproj + k) * value
        return tuple(accs)

    def partial_inner():
        accs = partial_rows(ends_ref, 0, width * nproj, empty)
        for a in range(1, edge - 1):
            accs = partial_rows(xs_ref, a * group * states, a * group * nproj, accs)
        return accs

    def partial_outer(accs):
        return partial_rows(ends_ref, group * states, (width + group) * nproj, accs)

    slot_ids = lax.broadcasted_iota(jnp.int32, (4 * atoms, entries), 0)
    chosen_atom = jnp.where(slot_ids == eatom_ref[...], 1.0, 0.0).astype(BF16)
    chosen_send = jnp.concatenate(
        [chosen_atom[:2 * atoms], chosen_atom[atoms:3 * atoms], chosen_atom[2 * atoms:3 * atoms],
         chosen_atom[:atoms]], axis=0,
    )
    back = (((1,), (1,)), ((), ()))
    empty = tuple(jnp.zeros((states, entries), F32) for _ in range(nproj))
    low_atoms = lax.broadcasted_iota(jnp.int32, (1, 2 * atoms), 1) < atoms

    def send_atoms(step, accs):
        grouped = lax.dot_general(
            halves(jnp.concatenate(accs, axis=0), 1),
            jnp.concatenate([chosen_send, chosen_send], axis=1),
            back, preferred_element_type=F32,
        )
        for g in range(3):
            grouped_ref[step, g] = grouped[:, 2 * g * atoms:2 * (g + 1) * atoms]
        at = 4 + 6 * step
        return [
            send(grouped_ref.at[step, 1], left_ref.at[step], sems, at, ahead),
            send(grouped_ref.at[step, 0], right_ref.at[step], sems, at + 1, behind),
            send(grouped_ref.at[step, 2], far_ref.at[step, 0], sems, at + 2, ahead2),
            send(grouped_ref.at[step, 2], far_ref.at[step, 1], sems, at + 3, behind2),
        ]

    def cell_terms():
        early, late = ends_ref[:size, :], ends_ref[size:, :]
        xs_ref[:size, :] = jnp.where(low_half, late, early)
        xs_ref[last * states:, :] = jnp.where(low_half, early, late)
        kmat = kmat_ref[...]
        for s in range(0, states, 2):
            pair = jnp.concatenate(
                [xs_ref[pl.ds(s, width, stride=states), :],
                 xs_ref[pl.ds(s + 1, width, stride=states), :]], axis=1,
            ).astype(BF16)
            out = jnp.dot(kmat, pair, preferred_element_type=F32)
            ct_ref[pl.ds(s, width, stride=states), :] = out[:, :cells] * scale
            ct_ref[pl.ds(s + 1, width, stride=states), :] = out[:, cells:] * scale

    def entry_terms(step):
        right = pltpu.roll(right_ref[step], atoms, 1)
        coef = (
            grouped_ref[step, 0] + left_ref[step]
            + jnp.where(low_atoms, far_ref[step, 0], right),
            grouped_ref[step, 2] + right + pltpu.roll(far_ref[step, 1], atoms, 1),
        )
        rows = []
        for c in range(2):
            parts = []
            for k in range(nproj):
                acc = jnp.zeros((states, 2 * atoms), F32)
                for l in range(nproj):
                    at = k * nproj + l
                    acc = acc + (
                        couple_ref[c, at:at + 1, :] * coef[c][l * states:(l + 1) * states, :]
                    )
                parts.append(acc)
            rows.append(halves(jnp.concatenate(parts, axis=0), 1))
        half_atoms = [chosen_atom[:2 * atoms]] * 2 + [chosen_atom[2 * atoms:]] * 2
        terms = jnp.dot(
            jnp.concatenate(rows, axis=1), jnp.concatenate(half_atoms, axis=0),
            preferred_element_type=F32,
        )
        return [terms[k * states:(k + 1) * states] for k in range(nproj)]

    per = tiles * 2 * states
    size = group * states

    def terms_at(a):
        return ct_ref[a * size:(a + 1) * size, :]

    def node_rows(proj_at, before, terms):
        parts = []
        for j in range(group):
            row = proj_at + j * nproj
            total = bcast(row) * terms[0]
            for k in range(1, nproj):
                total = total + bcast(row + k) * terms[k]
            parts.append(total)
        twice = jnp.concatenate([spread_ref[...], spread_ref[...]], axis=1)
        value = before + lax.dot_general(
            halves(jnp.concatenate(parts, axis=0), 1), twice, back, preferred_element_type=F32
        )
        found = []
        for w in range(wraps):
            even = value[2 * w * states:(2 * w + 1) * states]
            odd = value[(2 * w + 1) * states:(2 * w + 2) * states]
            mixed = pltpu.roll(jnp.where(low_half, odd, even), pairs, 1)
            found.append((jnp.where(low_half, even, mixed), jnp.where(low_half, mixed, odd)))
        return found

    def fill(into, w, value):
        both = halves(value, 0)
        for t in range(tiles):
            rows = into + t * 2 * states
            masked_ref[rows:rows + 2 * states, w * cells:(w + 1) * cells] = (
                both * hot_ref[t * 2 * states:(t + 1) * 2 * states, w * cells:(w + 1) * cells]
            )

    def fill_late(terms):
        before = jnp.where(low_half, terms_at(0), terms_at(edge - 1))
        found = node_rows((width + group) * nproj, before, terms)
        for w, (one, two) in enumerate(found):
            fill(0, w, one)
            fill(per, w, two)

    def fill_early(terms):
        before = jnp.where(low_half, terms_at(edge - 1), terms_at(0))
        for w, (one, two) in enumerate(node_rows(width * nproj, before, terms)):
            fill(2 * per, w, one + two)

    def fill_inner(a, terms):
        found = node_rows(a * group * nproj, terms_at(a), terms)
        for w, (one, two) in enumerate(found):
            fill((2 * a + 1) * per, w, one)
            fill((2 * a + 2) * per, w, two)

    def scatter(into, number):
        out = jnp.dot(
            masked_ref[into:into + number * per, :], oht_ref[...], preferred_element_type=F32
        )
        return [
            [joined(out[n * per:(n + 1) * per], t) for t in range(tiles)] for n in range(number)
        ]

    def joined(value, t):
        return value[t * 2 * states:t * 2 * states + states] + (
            value[t * 2 * states + states:(t + 1) * 2 * states]
        )

    def scatter_outer(step, terms):
        fill_late(terms)
        head, tail = scatter(0, 2)
        for t in range(tiles):
            head_ref[step, :, t * WIDE:(t + 1) * WIDE] = head[t]
            tail_ref[step, :, t * WIDE:(t + 1) * WIDE] = tail[t]

    def scatter_rest(terms, finish):
        fill_early(terms)
        for a in range(1, edge):
            if a < edge - 1:
                fill_inner(a, terms)
            if a == 1:
                (out,) = scatter(2 * per, 1)
                finish(0, edge - 1, out)
            else:
                one, two = scatter((2 * a - 1) * per, 2)
                finish(a - 1, a - 1, one)
                finish(a - 1, a + edge - 2, two)

    def pot_row(layer, t, half):
        row = layer * rows128 + t * 2 + half
        return potf_ref[pl.ds(row, 1), :]

    def scaled(layer, t, summed, field):
        pot = jnp.concatenate([pot_row(layer, t, 0), pot_row(layer, t, 1)], axis=1)
        return (summed + pot * field) * (1.0 / HALFWIDTH)

    def lanes(layer, t):
        at = layer * face + t * WIDE
        return pl.ds(at if isinstance(layer, int) else pl.multiple_of(at, WIDE), WIDE)

    def first_layer(layer, summed, field):
        blocks = []
        for t in range(tiles):
            value = scaled(layer, t, summed(t), field(t)).astype(BF16).astype(F32)
            first_ref[:, lanes(layer, t)] = value
            blocks.append(value)
        put(layer, blocks)

    def last_layer(layer, summed):
        for t in range(tiles):
            value = scaled(layer, t, summed(t), first_ref[:, lanes(layer, t)])
            at = lanes(layer, t)
            out_ref[:, at] = (2.0 * value - psi_ref[:, at].astype(F32)).astype(BF16)

    def edge_sum(one_ref, two_ref):
        return lambda t: (
            one_ref[:, t * WIDE:(t + 1) * WIDE] + two_ref[:, t * WIDE:(t + 1) * WIDE]
        )

    gather_inner()
    accs = partial_inner()
    for copy in gaps:
        copy.wait()
    couple_ref[0] = jnp.where(low_atoms, coups_ref[0], coups_ref[1])
    couple_ref[1] = coups_ref[2]
    put_psi(slabs, ghost_ref, 0)
    gather_outer()
    copies = send_atoms(0, partial_outer(accs))
    verdict.wait()
    potf_ref[slabs * rows128:slabs * rows128 + potg_ref.shape[0], :] = (
        potg_ref[...].astype(F32) - CENTER
    )
    cell_terms()
    for copy in copies:
        copy.wait()
    terms = entry_terms(0)
    scatter_outer(0, terms)
    copies = [
        send(tail_ref.at[0], low_ref.at[0], sems, 8, ahead),
        send(head_ref.at[0], high_ref, sems, 9, behind),
    ]

    def first_done(layer, summed):
        first_layer(layer, summed, lambda t: psi_ref[:, lanes(layer, t)].astype(F32))

    scatter_rest(terms, lambda a, layer, out: first_done(layer, lambda t: out[t]))
    gather_inner()
    accs = partial_inner()
    for copy in copies:
        copy.wait()
    first_done(0, edge_sum(head_ref.at[0], low_ref.at[0]))
    first_layer(
        slabs, edge_sum(tail_ref.at[0], high_ref),
        lambda t: ghost_ref[:, t * WIDE:(t + 1) * WIDE].astype(F32),
    )
    gather_outer()
    copies = send_atoms(1, partial_outer(accs))
    mated = [send(first_ref.at[:, span(mate_part, part)], mated_ref, sems, 20, partner)]
    cell_terms()
    for copy in copies:
        copy.wait()
    terms = entry_terms(1)
    scatter_outer(1, terms)
    tails = [
        send(tail_ref.at[1], low_ref.at[1], sems, 14, ahead),
        send(tail_ref.at[1, :, span(mate_part, part)], matel_ref, sems, 16, ahead_mate),
        send(head_ref.at[1, :, span(mate_part, part)], mateh_ref, sems, 19, partner),
    ]
    half = edge - 1

    def swap(n):
        if n == 0:
            at, size = half * face + mate_part, part
        else:
            at, size = jnp.where(band == 0, n + half, n) * face, face
        return pltpu.make_async_remote_copy(
            src_ref=out_ref.at[:, span(at, size)],
            dst_ref=other_ref.at[:, span(n * face, size)],
            send_sem=sems.at[0, 21 + n], recv_sem=sems.at[1, 21 + n],
            device_id=partner, device_id_type=MESH_ID,
        )

    def last_done(a, layer, out):
        last_layer(layer, lambda t: out[t])
        if layer >= half and a in (half // 2, half - 1):
            for n in range(0 if a == half // 2 else half // 2 + 1, a + 1):
                swap(n).start()

    scatter_rest(terms, last_done)

    def gram(own, other):
        both = jnp.concatenate(
            [jnp.where(band == 0, own, other), jnp.where(band == 0, other, own)], axis=0
        ).astype(BF16)
        return lax.dot_general(both, both, back, preferred_element_type=F32)

    swap(0).wait()
    total = gram(
        out_ref[:, span(half * face + own_part, part)].astype(F32), other_ref[:, :part].astype(F32)
    )
    for n in range(1, half):
        swap(n).wait()
        total = total + gram(
            out_ref[:, span(jnp.where(band == 0, n, n + half) * face, face)].astype(F32),
            other_ref[:, n * face:(n + 1) * face].astype(F32),
        )
    for copy in tails + mated:
        copy.wait()
    last_layer(0, edge_sum(head_ref.at[1], low_ref.at[1]))
    blocks = []
    for t in range(part // 128):
        at = slice(t * 128, (t + 1) * 128)
        pot = potf_ref[pl.ds(band * (part // 128) + t, 1), :]
        value = (mateh_ref[:, at] + matel_ref[:, at] + pot * mated_ref[:, at]) * (1.0 / HALFWIDTH)
        blocks.append((2.0 * value - mate_ref[:, at].astype(F32)).astype(BF16).astype(F32))
    total = total + gram(
        out_ref[:, span(own_part, part)].astype(F32), jnp.concatenate(blocks, axis=1)
    )
    size = bands * states
    lump = size * size // 128
    pieces = size // lump
    slots_ref[me] = jnp.concatenate(
        [total[r * lump:(r + 1) * lump] for r in range(pieces)], axis=1
    )

    def push(steps, carry):
        send(slots_ref.at[me], slots_ref.at[me], sems, 17, peer(steps))
        return carry

    lax.fori_loop(0, devices * bands - 1, push, 0)
    rest = pl.ds(0, devices * bands - 1)
    pltpu.make_async_remote_copy(
        src_ref=slots_ref.at[rest], dst_ref=slots_ref.at[rest], send_sem=sems.at[0, 17],
        recv_sem=sems.at[1, 17], device_id=partner, device_id_type=MESH_ID,
    ).wait()
    total = jnp.sum(slots_ref[...], axis=0) * (1.0 / (devices * count))
    corr_ref[...] = jnp.concatenate(
        [total[:, r * size:(r + 1) * size] for r in range(pieces)], axis=0
    )


def general(
    psi,
    cell_nodes,
    cell_scale,
    cell_matrix,
    node_potential,
    proj_values,
    entry_cell,
    entry_atom,
    coupling,
):
    states, node_count = psi.shape
    width, cells = cell_nodes.shape
    atoms, nproj, _ = coupling.shape
    entries = entry_atom.shape[0]
    full = node_count + FACEP
    chunks = full // FACEP
    layers = FACEP // WIDE
    groups = width // GROUP
    span = GROUP * cells

    table = cell_nodes.reshape(groups, GROUP, cells)
    owner = table // FACEP
    ids = jnp.arange(chunks, dtype=jnp.int32)
    flags = jnp.max(
        (owner[:, None] == ids[None, :, None, None]).astype(jnp.int32), axis=(2, 3)
    )
    rank = jnp.sum(flags[:, None, :] * (ids[None, :] < ids[:, None]), axis=2)
    places = jnp.arange(chunks + 1, dtype=jnp.int32)
    used = flags[:, :, None] * (rank[:, :, None] == places)
    listed = chunks + jnp.sum(used * (ids[None, :, None] - chunks), axis=1)
    listed = jnp.concatenate(
        [listed, jnp.full((groups, 1), chunks, jnp.int32), jnp.sum(flags, axis=1, keepdims=True)],
        axis=1,
    )
    sched = listed.astype(jnp.int32).reshape(groups * (chunks + 3))
    scale_row = cell_scale.reshape(1, cells)
    ecell = entry_cell.reshape(1, entries)
    eatom = entry_atom.reshape(1, entries)
    coup = coupling.transpose(1, 2, 0).reshape(nproj * nproj, atoms)
    potential = node_potential.astype(F32).reshape(1, node_count) - CENTER

    vmem = pl.BlockSpec(memory_space=pltpu.VMEM)
    smem = pl.BlockSpec(memory_space=pltpu.SMEM)

    padded = (layers * states + 15) // 16 * 16
    gather = pl.pallas_call(
        gather_kernel,
        out_shape=jax.ShapeDtypeStruct((width * states, cells), F32),
        in_specs=[smem] + [vmem] * 2,
        out_specs=vmem,
        scratch_shapes=[
            pltpu.VMEM((chunks + 1, padded, WIDE), BF16),
            pltpu.VMEM((WIDE, span), BF16),
        ],
        name="gather_cells",
    )
    scatter = pl.pallas_call(
        scatter_kernel,
        out_shape=jax.ShapeDtypeStruct((states, full), F32),
        in_specs=[smem] + [vmem] * 7,
        out_specs=vmem,
        scratch_shapes=[
            pltpu.VMEM((WIDE, span), BF16),
            pltpu.VMEM((width * states, entries), F32),
            pltpu.VMEM((width * states, cells), F32),
            pltpu.VMEM((2 * layers * 2 * states, span), BF16),
            pltpu.VMEM((chunks + 1, layers * 2 * states, WIDE), F32),
        ],
        name="scatter_nodes",
    )

    def remote(kernel, outs, n_in, scratch, copies, ident):
        return pl.pallas_call(
            kernel,
            out_shape=tuple(jax.ShapeDtypeStruct(*out) for out in outs),
            in_specs=[vmem] * n_in,
            out_specs=(vmem,) * len(outs),
            scratch_shapes=[pltpu.VMEM(*one) for one in scratch]
            + [pltpu.SemaphoreType.DMA((2, copies))],
            compiler_params=pltpu.CompilerParams(collective_id=ident, has_side_effects=True),
            name=kernel.__name__,
        )

    pair = (nproj * states, atoms)

    def assemble(extended, ident):
        values = gather(sched, table, extended)
        cell_terms, coef = remote(
            atoms_kernel, [((width * states, cells), F32), ((3,) + pair, F32)], 6,
            [((width * states, entries), F32), ((3,) + pair, F32)] + [((2,) + pair, F32)] * 3,
            4, ident,
        )(values, cell_matrix, scale_row, proj_values, ecell, eatom)
        return scatter(sched, table, cell_terms, coef, coup_all, proj_values, ecell, eatom)

    psi_ext, pot_ext, coup_all = remote(
        start_kernel,
        [((states, full), BF16), ((1, full), F32), ((3, nproj * nproj, atoms), F32)],
        3, [], 4, 1,
    )(psi, potential, coup)
    face = (states, FACEP)
    (first,) = remote(first_kernel, [((states, full), BF16)], 3, [(face, F32), (face, F32)], 2, 3)(
        assemble(psi_ext, 2), psi_ext, pot_ext
    )
    bands, devices = lax.axis_size("band"), lax.axis_size("mesh")
    square = (bands * states, bands * states)
    filtered, correlation = remote(
        last_kernel,
        [((states, node_count), BF16), (square, F32)],
        4,
        [(face, F32), ((states, node_count), BF16), ((devices,) + square, F32)],
        4, 5,
    )(assemble(first, 4), first, psi, potential)
    return (filtered, correlation)


def hand_over(filtered_ref, correlation_ref, out_ref, corr_ref, sems):
    copies = [
        pltpu.make_async_copy(filtered_ref, out_ref, sems.at[0]),
        pltpu.make_async_copy(correlation_ref, corr_ref, sems.at[1]),
    ]
    for copy in copies:
        copy.start()
    for copy in copies:
        copy.wait()


def bricks(states, node_count, width, cells, bands):
    edge = round(width ** (1.0 / 3.0))
    return (
        edge ** 3 == width
        and (edge - 1) * 2 * FACEP == node_count
        and edge % 2 == 0
        and cells == 128
        and FACEP % WIDE == 0
        and FACEP % 256 == 0
        and states == 8
        and bands == 2
        and edge * edge % 6 == 0
    )


def local(
    psi,
    cell_nodes,
    cell_scale,
    cell_matrix,
    node_potential,
    proj_values,
    entry_cell,
    entry_atom,
    coupling,
):
    states, node_count = psi.shape
    width, cells = cell_nodes.shape
    atoms, nproj, _ = coupling.shape
    entries = entry_atom.shape[0]
    bands, devices = lax.axis_size("band"), lax.axis_size("mesh")
    operands = (
        psi, cell_nodes, cell_scale, cell_matrix, node_potential, proj_values, entry_cell,
        entry_atom, coupling,
    )
    if not bricks(states, node_count, width, cells, bands):
        return general(*operands)
    edge = round(width ** (1.0 / 3.0))
    wraps = edge * edge // 2
    layers = node_count // FACEP + 1
    tiles = FACEP // WIDE
    block = (tiles + 1) * states
    per = tiles * 2 * states
    rows = node_count // 128
    ghost_rows = (FACEP // 128 + 15) // 16 * 16
    size = bands * states
    vmem = pl.BlockSpec(memory_space=pltpu.VMEM)
    anywhere = pl.BlockSpec(memory_space=pl.ANY)
    face = (states, FACEP)
    duo = (nproj * states, 2 * atoms)
    filtered, correlation, wrong = pl.pallas_call(
        fused_kernel,
        out_shape=(
            jax.ShapeDtypeStruct((states, node_count), BF16),
            jax.ShapeDtypeStruct((size, size), F32),
            jax.ShapeDtypeStruct((1, 128), F32),
        ),
        in_specs=[anywhere] * 9,
        out_specs=(vmem, vmem, anywhere),
        scratch_shapes=[
            pltpu.VMEM((1, 128), F32),
            pltpu.VMEM(psi.shape, BF16),
            pltpu.VMEM(cell_nodes.shape, jnp.int32),
            pltpu.VMEM(cell_matrix.shape, BF16),
            pltpu.VMEM((rows, 128), BF16),
            pltpu.VMEM(proj_values.shape, BF16),
            pltpu.VMEM((1, cells), F32),
            pltpu.VMEM((1, entries), jnp.int32),
            pltpu.VMEM((1, entries), jnp.int32),
            pltpu.VMEM((nproj * nproj, atoms), F32),
            pltpu.VMEM((WIDE, wraps * cells), BF16),
            pltpu.VMEM((wraps * cells, WIDE), BF16),
            pltpu.VMEM(((wraps + 7) // 8 * 8, cells), jnp.int32),
            pltpu.VMEM(((2 * wraps + 7) // 8 * 8, cells), F32),
            pltpu.VMEM((width * states, cells), F32),
            pltpu.VMEM((width * states, cells), F32),
            pltpu.VMEM((4 * wraps * states, cells), F32),
            pltpu.VMEM((layers * block, WIDE), BF16),
            pltpu.VMEM((layers * per, wraps * cells), BF16),
            pltpu.VMEM((states, layers * FACEP), F32),
            pltpu.VMEM((rows + ghost_rows, 128), F32),
            pltpu.VMEM((2,) + face, F32),
            pltpu.VMEM((2,) + face, F32),
            pltpu.VMEM((2,) + face, F32),
            pltpu.VMEM(face, F32),
            pltpu.VMEM((2, 3) + duo, F32),
            pltpu.VMEM((2,) + duo, F32),
            pltpu.VMEM((2,) + duo, F32),
            pltpu.VMEM((2, 2) + duo, F32),
            pltpu.VMEM(face, BF16),
            pltpu.VMEM((ghost_rows, 128), BF16),
            pltpu.VMEM((3, nproj * nproj, 2 * atoms), F32),
            pltpu.VMEM((cells, entries), BF16),
            pltpu.VMEM((states, node_count // 2), BF16),
            pltpu.VMEM((devices * bands, size * size // 128, 128), F32),
            pltpu.VMEM((per, wraps * cells), BF16),
            pltpu.VMEM((2, nproj * nproj, 2 * atoms), F32),
            pltpu.VMEM((states, FACEP // 2), BF16),
            pltpu.VMEM((states, FACEP // 2), F32),
            pltpu.VMEM((states, FACEP // 2), F32),
            pltpu.VMEM((states, FACEP // 2), F32),
            pltpu.VMEM(((width + 4 * wraps) * nproj, entries), F32),
            pltpu.SemaphoreType.DMA((10,)),
            pltpu.SemaphoreType.DMA((2, 26)),
        ],
        compiler_params=pltpu.CompilerParams(collective_id=0, has_side_effects=True),
        name="fused_steps",
    )(
        psi, cell_nodes, cell_scale.reshape(1, cells), cell_matrix,
        node_potential.reshape(rows, 128), proj_values, entry_cell.reshape(1, entries),
        entry_atom.reshape(1, entries),
        coupling.transpose(1, 2, 0).reshape(nproj * nproj, atoms),
    )
    results = lax.cond(
        wrong[0, 0] > 0.0,
        lambda: general(*operands),
        lambda: (filtered, correlation),
    )
    return pl.pallas_call(
        hand_over,
        out_shape=tuple(jax.ShapeDtypeStruct(one.shape, one.dtype) for one in results),
        in_specs=[anywhere] * 2,
        out_specs=(anywhere,) * 2,
        scratch_shapes=[pltpu.SemaphoreType.DMA((2,))],
        name="hand_over",
    )(*results)


def solution(mesh):
    return jax.shard_map(
        local,
        mesh=mesh,
        in_specs=(
            P("band", "mesh"),
            P(),
            P("mesh"),
            P(),
            P("mesh"),
            P(None, None, "mesh"),
            P("mesh"),
            P("mesh"),
            P("mesh", None, None),
        ),
        out_specs=(P("band", "mesh"), P()),
        check_vma=False,
    )
```

```python
import jax
import jax.numpy as jnp
from jax import lax
from jax.experimental import pallas as pl
from jax.experimental.pallas import tpu as pltpu
from jax.sharding import PartitionSpec as P

FACEP = 1792
CENTER = 0.5
HALFWIDTH = 2.5
HIGH = lax.Precision.HIGHEST
WIDE = 256
GROUP = 36
F32 = jnp.float32
BF16 = jnp.bfloat16


def fill_onehot(cn_ref, group, oh_ref):
    rows = cn_ref[group]
    hi = jnp.bitwise_and(rows, WIDE - 1)
    lanes = rows.shape[1]
    iota = lax.broadcasted_iota(jnp.int32, (WIDE, lanes), 0)
    for jj in range(GROUP):
        oh_ref[:, jj * lanes:(jj + 1) * lanes] = jnp.where(
            iota == hi[jj:jj + 1, :], 1.0, 0.0
        ).astype(BF16)
    return lax.shift_right_logical(rows, 8)


def gather_kernel(sched_ref, cn_ref, ext_ref, xs_ref, lhs_ref, oh_ref):
    states = ext_ref.shape[0]
    chunks = lhs_ref.shape[0] - 1
    layers = ext_ref.shape[1] // (chunks * WIDE)
    groups = cn_ref.shape[0]
    cells = cn_ref.shape[2]
    padded = lhs_ref.shape[1]
    slots = sched_ref.shape[0] // groups
    lhs_ref[...] = jnp.zeros_like(lhs_ref)
    for c in range(chunks):
        base = c * layers * WIDE
        parts = [
            ext_ref[:, base + l * WIDE:base + (l + 1) * WIDE].astype(F32) for l in range(layers)
        ]
        parts.append(jnp.zeros((padded - layers * states, WIDE), F32))
        lhs_ref[c] = jnp.concatenate(parts, axis=0).astype(BF16)
    xs_ref[...] = jnp.zeros_like(xs_ref)

    def group_body(g, carry):
        lo = fill_onehot(cn_ref, g, oh_ref)

        def pair_body(r, inner):
            first = sched_ref[g * slots + 2 * r]
            second = sched_ref[g * slots + 2 * r + 1]
            lhs = jnp.concatenate([lhs_ref[first], lhs_ref[second]], axis=0)
            out = jnp.dot(lhs, oh_ref[...], preferred_element_type=F32)
            for jj in range(GROUP):
                where = pl.ds(pl.multiple_of((g * GROUP + jj) * states, states), states)
                value = xs_ref[where, :]
                lanes = slice(jj * cells, (jj + 1) * cells)
                for half, chunk in enumerate((first, second)):
                    row = lo[jj:jj + 1, :] - chunk * layers
                    for l in range(layers):
                        at = half * padded + l * states
                        value = jnp.where(row == l, out[at:at + states, lanes], value)
                xs_ref[where, :] = value
            return inner

        pairs = lax.shift_right_logical(sched_ref[g * slots + slots - 1] + 1, 1)
        return lax.fori_loop(0, pairs, pair_body, carry)

    lax.fori_loop(0, groups, group_body, 0)


def scatter_kernel(sched_ref, cn_ref, ct_ref, coef_ref, coup_ref, proj_ref, ecell_ref,
                   eatom_ref, y_ref, oh_ref, ns_ref, v_ref, lhs_ref, acc_ref):
    chunks, rows_in_chunk, _ = acc_ref.shape
    chunks = chunks - 1
    groups = cn_ref.shape[0]
    cells = cn_ref.shape[2]
    width = groups * GROUP
    states = ct_ref.shape[0] // width
    layers = rows_in_chunk // (2 * states)
    nproj = proj_ref.shape[1]
    entries = ecell_ref.shape[1]
    atoms = coef_ref.shape[2]
    slot_ids = lax.broadcasted_iota(jnp.int32, (atoms, entries), 0)
    entry_terms = jnp.zeros((nproj * states, entries), F32)
    for g in range(3):
        rows = []
        for k in range(nproj):
            acc = jnp.zeros((states, atoms), F32)
            for l in range(nproj):
                acc = acc + (
                    coup_ref[g, k * nproj + l:k * nproj + l + 1, :]
                    * coef_ref[g, l * states:(l + 1) * states, :]
                )
            rows.append(acc)
        chosen = jnp.where(eatom_ref[...] == slot_ids + g * atoms, 1.0, 0.0)
        entry_terms = entry_terms + jnp.dot(
            jnp.concatenate(rows, axis=0), chosen, precision=HIGH, preferred_element_type=F32
        )
    terms = [entry_terms[k * states:(k + 1) * states, :] for k in range(nproj)]

    def node_body(j, carry):
        proj = proj_ref[j].astype(F32)
        total = proj[0:1, :] * terms[0]
        for k in range(1, nproj):
            total = total + proj[k:k + 1, :] * terms[k]
        ns_ref[pl.ds(pl.multiple_of(j * states, states), states), :] = total
        return carry

    lax.fori_loop(0, width, node_body, 0, unroll=8)
    cell_ids = lax.broadcasted_iota(jnp.int32, (cells, entries), 0)
    spread = jnp.where(cell_ids == ecell_ref[...], 1.0, 0.0).astype(BF16)
    back = (((1,), (1,)), ((), ()))
    node_vals = ns_ref[...]
    node_top = node_vals.astype(BF16)
    node_rest = (node_vals - node_top.astype(F32)).astype(BF16)
    v_ref[...] = (
        ct_ref[...]
        + lax.dot_general(node_top, spread, back, preferred_element_type=F32)
        + lax.dot_general(node_rest, spread, back, preferred_element_type=F32)
    )
    acc_ref[...] = jnp.zeros_like(acc_ref)
    slots = sched_ref.shape[0] // groups

    def group_body(g, carry):
        lo = fill_onehot(cn_ref, g, oh_ref)

        def pair_body(r, inner):
            first = sched_ref[g * slots + 2 * r]
            second = sched_ref[g * slots + 2 * r + 1]
            for jj in range(GROUP):
                start = pl.multiple_of((g * GROUP + jj) * states, states)
                value = v_ref[pl.ds(start, states), :]
                top = value.astype(BF16).astype(F32)
                both = jnp.concatenate([top, value - top], axis=0)
                lanes = slice(jj * cells, (jj + 1) * cells)
                for half, chunk in enumerate((first, second)):
                    row = lo[jj:jj + 1, :] - chunk * layers
                    for l in range(layers):
                        at = half * rows_in_chunk + l * 2 * states
                        lhs_ref[at:at + 2 * states, lanes] = (
                            jnp.where(row == l, both, 0.0).astype(BF16)
                        )
            out = lax.dot_general(lhs_ref[...], oh_ref[...], back, preferred_element_type=F32)
            acc_ref[first] += out[:rows_in_chunk]
            acc_ref[second] += out[rows_in_chunk:]
            return inner

        pairs = lax.shift_right_logical(sched_ref[g * slots + slots - 1] + 1, 1)
        return lax.fori_loop(0, pairs, pair_body, carry)

    lax.fori_loop(0, groups, group_body, 0)
    for c in range(chunks):
        for l in range(layers):
            base = (c * layers + l) * WIDE
            at = l * 2 * states
            y_ref[:, base:base + WIDE] = (
                acc_ref[c, at:at + states, :] + acc_ref[c, at + states:at + 2 * states, :]
            )


MESH_ID = pl.DeviceIdType.MESH


def ring_peer(steps):
    count = lax.axis_size("mesh")
    return lax.rem(lax.axis_index("mesh") + steps + count, count)


def send(src, dst, sems, at, peer):
    copy = pltpu.make_async_remote_copy(
        src_ref=src, dst_ref=dst, send_sem=sems.at[0, at], recv_sem=sems.at[1, at],
        device_id=peer, device_id_type=MESH_ID,
    )
    copy.start()
    return copy


def greet(peers):
    barrier = pltpu.get_barrier_semaphore()
    for peer in peers:
        pl.semaphore_signal(barrier, inc=1, device_id=peer, device_id_type=MESH_ID)
    return barrier


def start_kernel(psi_ref, pot_ref, coup_ref, ext_ref, potx_ref, coups_ref, sems):
    count = psi_ref.shape[1]
    face = ext_ref.shape[1] - count
    ahead, behind = {"mesh": ring_peer(1)}, {"mesh": ring_peer(-1)}
    pl.semaphore_wait(greet((ahead, behind)), 2)
    copies = [
        send(psi_ref.at[:, :face], ext_ref.at[:, count:], sems, 0, behind),
        send(coup_ref, coups_ref.at[0], sems, 1, ahead),
        send(coup_ref, coups_ref.at[2], sems, 2, behind),
        send(pot_ref.at[:, :face], potx_ref.at[:, count:], sems, 3, behind),
    ]
    ext_ref[:, :count] = psi_ref[...]
    potx_ref[:, :count] = pot_ref[...]
    coups_ref[1] = coup_ref[...]
    for copy in copies:
        copy.wait()


def atoms_kernel(xs_ref, kmat_ref, scale_ref, proj_ref, ecell_ref, eatom_ref, ct_ref, coef_ref,
                 es_ref, grouped_ref, left_ref, right_ref, far_ref, sems):
    peers = [{"mesh": ring_peer(steps)} for steps in (1, -1, 2, -2)]
    barrier = greet(peers)
    width, nproj, entries = proj_ref.shape
    cells = xs_ref.shape[1]
    states = xs_ref.shape[0] // width
    cell_ids = lax.broadcasted_iota(jnp.int32, (cells, entries), 0)
    spread = jnp.where(cell_ids == ecell_ref[...], 1.0, 0.0).astype(BF16)
    es_ref[...] = jnp.dot(xs_ref[...].astype(BF16), spread, preferred_element_type=F32)

    def partial_body(j, accs):
        values = es_ref[pl.ds(pl.multiple_of(j * states, states), states), :]
        proj = proj_ref[j].astype(F32)
        return tuple(acc + proj[k:k + 1, :] * values for k, acc in enumerate(accs))

    zero = jnp.zeros((states, entries), F32)
    accs = lax.fori_loop(0, width, partial_body, (zero,) * nproj, unroll=8)
    partial_sum = jnp.concatenate(accs, axis=0)
    atoms = grouped_ref.shape[2]
    slot_ids = lax.broadcasted_iota(jnp.int32, (atoms, entries), 0)
    for g in range(3):
        chosen = jnp.where(eatom_ref[...] == slot_ids + g * atoms, 1.0, 0.0)
        grouped_ref[g] = lax.dot_general(
            partial_sum, chosen, (((1,), (1,)), ((), ())), precision=HIGH,
            preferred_element_type=F32,
        )
    pl.semaphore_wait(barrier, 4)
    copies = [
        send(grouped_ref.at[1:3], left_ref, sems, 0, peers[0]),
        send(grouped_ref.at[0:2], right_ref, sems, 1, peers[1]),
        send(grouped_ref.at[2], far_ref.at[0], sems, 2, peers[2]),
        send(grouped_ref.at[0], far_ref.at[1], sems, 3, peers[3]),
    ]
    kmat = kmat_ref[...]
    scale = scale_ref[...]
    for s in range(0, states, 2):
        pair = jnp.concatenate(
            [xs_ref[pl.ds(s, width, stride=states), :], xs_ref[pl.ds(s + 1, width, stride=states), :]],
            axis=1,
        ).astype(BF16)
        out = jnp.dot(kmat, pair, preferred_element_type=F32)
        ct_ref[pl.ds(s, width, stride=states), :] = out[:, :cells] * scale
        ct_ref[pl.ds(s + 1, width, stride=states), :] = out[:, cells:] * scale
    for copy in copies:
        copy.wait()
    coef_ref[0] = left_ref[0] + far_ref[0] + grouped_ref[0]
    coef_ref[1] = grouped_ref[1] + left_ref[1] + right_ref[0]
    coef_ref[2] = right_ref[1] + grouped_ref[2] + far_ref[1]


def first_kernel(y_ref, ext_ref, pot_ref, first_ref, low_ref, high_ref, sems):
    full = y_ref.shape[1]
    face = low_ref.shape[1]
    count = full - face
    ahead, behind = {"mesh": ring_peer(1)}, {"mesh": ring_peer(-1)}
    barrier = greet((ahead, behind))

    def finish(total, at):
        scaled = (total + pot_ref[:, at] * ext_ref[:, at].astype(F32)) / HALFWIDTH
        first_ref[:, at] = scaled.astype(BF16)

    middle = face * (1 + (count // face - 1) // 2)
    for base in range(face, middle, face):
        at = slice(base, base + face)
        finish(y_ref[:, at], at)
    pl.semaphore_wait(barrier, 2)
    copies = [
        send(y_ref.at[:, count:], low_ref, sems, 0, ahead),
        send(y_ref.at[:, :face], high_ref, sems, 1, behind),
    ]
    for base in range(middle, count, face):
        at = slice(base, base + face)
        finish(y_ref[:, at], at)
    for copy in copies:
        copy.wait()
    finish(y_ref[:, :face] + low_ref[...], slice(0, face))
    finish(y_ref[:, count:] + high_ref[...], slice(count, full))


def last_kernel(y_ref, first_ref, psi_ref, pot_ref, out_ref, corr_ref, low_ref, other_ref,
                slots_ref, sems):
    count = psi_ref.shape[1]
    face = low_ref.shape[1]
    devices = lax.axis_size("mesh")
    bands = lax.axis_size("band")
    me = lax.axis_index("mesh")
    band = lax.axis_index("band")
    partner = {"band": lax.rem(band + 1, bands)}
    barrier = greet((partner,))

    def greet_body(steps, carry):
        pl.semaphore_signal(
            barrier, inc=1, device_id={"mesh": lax.rem(me + steps, devices)}, device_id_type=MESH_ID
        )
        return carry

    lax.fori_loop(1, devices, greet_body, 0)

    def finish(total, at):
        scaled = (total + pot_ref[:, at] * first_ref[:, at].astype(F32)) / HALFWIDTH
        out_ref[:, at] = (2.0 * scaled - psi_ref[:, at].astype(F32)).astype(BF16)

    for base in range(face, count, face):
        at = slice(base, base + face)
        finish(y_ref[:, at], at)
    pl.semaphore_wait(barrier, devices)
    tail = send(y_ref.at[:, count:count + face], low_ref, sems, 0, {"mesh": ring_peer(1)})
    swap = send(out_ref.at[:, face:], other_ref.at[:, face:], sems, 1, partner)
    states = out_ref.shape[0]

    def gram(base):
        at = slice(base, base + face)
        own, other = out_ref[:, at].astype(F32), other_ref[:, at].astype(F32)
        block = jnp.concatenate(
            [jnp.where(band == 0, own, other), jnp.where(band == 0, other, own)], axis=0
        ).astype(BF16)
        return lax.dot_general(
            block, block, (((1,), (1,)), ((), ())), preferred_element_type=F32
        )

    swap.wait()
    total = gram(face)
    for base in range(2 * face, count, face):
        total = total + gram(base)
    tail.wait()
    finish(y_ref[:, :face] + low_ref[...], slice(0, face))
    edge = send(out_ref.at[:, :face], other_ref.at[:, :face], sems, 3, partner)
    edge.wait()
    total = total + gram(0)
    slots_ref[me] = total

    def push(steps, carry):
        send(slots_ref.at[me], slots_ref.at[me], sems, 2, {"mesh": lax.rem(me + steps, devices)})
        return carry

    lax.fori_loop(1, devices, push, 0)
    pltpu.make_async_remote_copy(
        src_ref=slots_ref.at[pl.ds(0, devices - 1)], dst_ref=slots_ref.at[pl.ds(0, devices - 1)],
        send_sem=sems.at[0, 2], recv_sem=sems.at[1, 2], device_id=partner, device_id_type=MESH_ID,
    ).wait()
    corr_ref[...] = jnp.sum(slots_ref[...], axis=0) * (1.0 / (devices * count))


def everyone(count):
    bands = lax.axis_size("band")
    flat = lax.axis_index("mesh") * bands + lax.axis_index("band")
    early = flat < count // 2

    def peer(n):
        down = count - 1 - n
        other = jnp.where(
            early, jnp.where(down <= flat, down - 1, down), jnp.where(n >= flat, n + 1, n)
        )
        return {"mesh": other // bands, "band": lax.rem(other, bands)}

    return flat, peer


def halves(value, axis):
    top = value.astype(BF16)
    return jnp.concatenate([top, (value - top.astype(F32)).astype(BF16)], axis=axis)


def fused_kernel(psi_hbm, cn_hbm, scale_hbm, kmat_hbm, pot_hbm, proj_hbm, ecell_hbm, eatom_hbm,
                 coup_hbm, out_ref, corr_ref, flag_hbm, flag_ref,
                 psi_ref, cn_ref, kmat_ref, pot_ref, proj_ref, scale_ref, ecell_ref, eatom_ref, coup_ref,
                 oh_ref, oht_ref, hi_ref, pd_ref, xs_ref, ct_ref, ends_ref, lhs_ref,
                 masked_ref, first_ref, potf_ref, head_ref, tail_ref, low_ref, high_ref,
                 grouped_ref, left_ref, right_ref, far_ref, ghost_ref, potg_ref, coups_ref,
                 spread_ref, other_ref, slots_ref, hot_ref, couple_ref, mate_ref, mated_ref,
                 mateh_ref, matel_ref, projf_ref, fetch_sems, sems):
    fetches = [
        pltpu.make_async_copy(src, dst, fetch_sems.at[n])
        for n, (src, dst) in enumerate((
            (cn_hbm, cn_ref), (scale_hbm, scale_ref), (ecell_hbm, ecell_ref),
            (coup_hbm, coup_ref), (eatom_hbm, eatom_ref), (psi_hbm, psi_ref),
            (proj_hbm, proj_ref), (pot_hbm, pot_ref), (kmat_hbm, kmat_ref),
        ))
    ]
    for fetch in fetches:
        fetch.start()
    states, count = psi_ref.shape
    width, cells = cn_ref.shape
    face = ghost_ref.shape[1]
    slabs = count // face
    layers = slabs + 1
    _, nproj, entries = proj_ref.shape
    atoms = coup_ref.shape[1]
    edge = slabs // 2 + 1
    group = width // edge
    pairs = cells // 2
    tiles = face // WIDE
    block = (tiles + 1) * states
    wraps = group // 2
    devices, bands = lax.axis_size("mesh"), lax.axis_size("band")
    band = lax.axis_index("band")
    me, peer = everyone(devices * bands)
    ahead, behind = {"mesh": ring_peer(1)}, {"mesh": ring_peer(-1)}
    ahead2, behind2 = {"mesh": ring_peer(2)}, {"mesh": ring_peer(-2)}
    partner = {"band": lax.rem(band + 1, bands)}
    ahead_mate = {"mesh": ring_peer(1), "band": lax.rem(band + 1, bands)}
    barrier = pltpu.get_barrier_semaphore()

    behind_mate = {"mesh": ring_peer(-1), "band": lax.rem(band + 1, bands)}
    if devices > 16:
        guests = devices * bands - 1

        def greet_body(n, carry):
            pl.semaphore_signal(barrier, inc=1, device_id=peer(n), device_id_type=MESH_ID)
            return carry

        lax.fori_loop(0, guests, greet_body, 0)
    else:
        near = (ahead, behind, ahead2, behind2, ahead_mate, behind_mate, partner)
        guests = len(near)
        for one in near:
            pl.semaphore_signal(barrier, inc=1, device_id=one, device_id_type=MESH_ID)
    part = face // 2
    own_part, mate_part = band * part, (bands - 1 - band) * part

    def span(at, size):
        return pl.ds(pl.multiple_of(at, 128), size)

    for fetch in fetches[:4]:
        fetch.wait()
    down = lax.broadcasted_iota(jnp.int32, (cells, cells), 0)
    across = lax.broadcasted_iota(jnp.int32, (cells, cells), 1)
    eye = down == across
    key = jnp.broadcast_to(cn_ref[0:1, :].astype(F32), (cells, cells))
    key_col = jnp.sum(jnp.where(eye, key, 0.0), axis=1, keepdims=True)
    rank = jnp.sum(jnp.where(key < key_col, 1.0, 0.0), axis=1, keepdims=True)
    chosen_cell = rank == across.astype(F32)
    order = jnp.where(chosen_cell, 1.0, 0.0).astype(BF16)
    scale_col = jnp.sum(
        jnp.where(eye, jnp.broadcast_to(scale_ref[...], (cells, cells)), 0.0), axis=1, keepdims=True
    )
    scale = jnp.sum(jnp.where(chosen_cell, scale_col, 0.0), axis=0, keepdims=True)
    entry_rank = jnp.sum(
        jnp.where(lax.broadcasted_iota(jnp.int32, (cells, entries), 0) == ecell_ref[...], rank, 0.0),
        axis=0, keepdims=True,
    )
    spread = jnp.where(
        lax.broadcasted_iota(jnp.int32, (cells, entries), 0).astype(F32) == entry_rank, 1.0, 0.0
    )
    spread_ref[...] = spread.astype(BF16)
    table = cn_ref[...]
    upper = lax.shift_right_logical(table, 8).astype(F32)
    lower = jnp.bitwise_and(table, WIDE - 1).astype(F32)
    table = WIDE * jnp.dot(upper.astype(BF16), order, preferred_element_type=F32) + jnp.dot(
        lower.astype(BF16), order, preferred_element_type=F32
    )
    low_half = lax.broadcasted_iota(jnp.int32, (1, cells), 1) < pairs
    base = table[:group]
    base = jnp.where(low_half, base, pltpu.roll(base, pairs, 1))
    lift = jnp.where(low_half, 0.0, float((edge - 1) * face))
    wrong = jnp.where((base < 0.0) | (base >= float(face)), 1.0, 0.0)
    for a in range(edge):
        expected = base + (lift + float(a * face))
        wrong = jnp.maximum(
            wrong, jnp.where(table[a * group:(a + 1) * group] == expected, 0.0, 1.0)
        )
    flag_ref[...] = jnp.broadcast_to(
        jnp.max(jnp.max(wrong, axis=0, keepdims=True), axis=1, keepdims=True), flag_ref.shape
    )
    verdict = pltpu.make_async_copy(flag_ref, flag_hbm, fetch_sems.at[len(fetches)])
    verdict.start()
    pd_ref[:group, :] = base
    places = jnp.where(
        low_half, pd_ref[pl.ds(0, wraps, stride=2), :], pd_ref[pl.ds(1, wraps, stride=2), :]
    ).astype(jnp.int32)
    slot = jnp.bitwise_and(places, WIDE - 1)
    hi_ref[:wraps, :] = lax.shift_right_logical(places, 8)
    wide_ids = lax.broadcasted_iota(jnp.int16, (WIDE, cells), 0)
    one, zero = jnp.array(1.0, BF16), jnp.array(0.0, BF16)
    for w in range(wraps):
        hot = jnp.where(wide_ids == slot[w:w + 1, :].astype(jnp.int16), one, zero)
        oh_ref[:, w * cells:(w + 1) * cells] = hot
        oht_ref[w * cells:(w + 1) * cells, :] = hot.T

    for w in range(wraps):
        hi = jnp.broadcast_to(hi_ref[w:w + 1, :], (2 * states, cells))
        for t in range(tiles):
            hot_ref[t * 2 * states:(t + 1) * 2 * states, w * cells:(w + 1) * cells] = (
                jnp.where(hi == t, 1.0, 0.0).astype(BF16)
            )
    coups_ref[1] = jnp.concatenate([coup_ref[...]] * 2, axis=1)
    pl.semaphore_wait(barrier, guests)
    gaps = [
        send(psi_hbm.at[:, :face], ghost_ref, sems, 0, behind),
        send(pot_hbm.at[:potg_ref.shape[0], :], potg_ref, sems, 1, behind),
        send(coups_ref.at[1], coups_ref.at[0], sems, 2, ahead),
        send(coups_ref.at[1], coups_ref.at[2], sems, 3, behind),
        send(psi_hbm.at[:, span(mate_part, part)], mate_ref, sems, 18, partner),
    ]

    rows128 = face // 128
    for fetch in fetches[4:]:
        fetch.wait()
    in_lower = entry_rank < float(pairs)
    last = (edge - 1) * group

    def proj_body(j, carry):
        rows = pl.ds(pl.multiple_of(j * nproj, nproj), nproj)
        projf_ref[rows, :] = proj_ref[j].astype(F32)
        return carry

    lax.fori_loop(0, width, proj_body, 0, unroll=8)

    def ends_body(i, carry):
        one, two = proj_ref[i].astype(F32), proj_ref[last + i].astype(F32)
        early = pl.multiple_of((width + i) * nproj, nproj)
        late = pl.multiple_of((width + group + i) * nproj, nproj)
        projf_ref[pl.ds(early, nproj), :] = jnp.where(in_lower, two, one)
        projf_ref[pl.ds(late, nproj), :] = jnp.where(in_lower, one, two)
        return carry

    lax.fori_loop(0, group, ends_body, 0, unroll=6)
    potf_ref[:slabs * rows128, :] = pot_ref[...].astype(F32) - CENTER

    def place(layer):
        if isinstance(layer, int):
            return 0 if layer == 0 else 1 if layer == slabs else layer + 1
        return layer + 1

    def put(layer, blocks):
        both = jnp.concatenate(blocks + [blocks[-1]], axis=0).astype(BF16)
        start = place(layer) * block
        if not isinstance(layer, int):
            start = pl.multiple_of(start, block)
        lhs_ref[pl.ds(start, block), :] = both

    def put_psi(layer, source, at):
        put(layer, [
            source[:, pl.ds(pl.multiple_of(at + t * WIDE, WIDE), WIDE)].astype(F32)
            for t in range(tiles)
        ])

    def psi_body(layer, carry):
        put_psi(layer, psi_ref, layer * face)
        return carry

    put_psi(0, psi_ref, 0)
    lax.fori_loop(1, slabs, psi_body, 0)

    def gather(first_row, chosen, finish, trips):
        rows = len(chosen) * block
        trip = wraps // trips

        def body(n, carry):
            hot = oh_ref[:, pl.ds(pl.multiple_of(n * trip * cells, trip * cells), trip * cells)]
            out = jnp.dot(lhs_ref[first_row:first_row + rows, :], hot, preferred_element_type=F32)
            pick(out, n * trip, trip)
            return carry

        def pick(out, first, columns):
            for c in range(columns):
                w = first + c
                hi = jnp.broadcast_to(hi_ref[pl.ds(w, 1), :], (states, cells))
                masks = [hi == t for t in range(1, tiles)]
                found = {}
                for k, layer in enumerate(chosen):
                    part = out[k * block:(k + 1) * block, c * cells:(c + 1) * cells]
                    value = part[:states]
                    for t in range(1, tiles):
                        value = jnp.where(
                            masks[t - 1], part[t * states:(t + 1) * states], value
                        )
                    found[layer] = value
                finish(w, found)

        if trips == 1:
            wide = 2 * cells
            for n in range(wraps // 2):
                out = jnp.dot(
                    lhs_ref[first_row:first_row + rows, :], oh_ref[:, n * wide:(n + 1) * wide],
                    preferred_element_type=F32,
                )
                pick(out, 2 * n, 2)
        else:
            lax.fori_loop(0, trips, body, 0)

    def store_pair(into, row, w, lower_cells, upper_cells):
        mixed = pltpu.roll(jnp.where(low_half, upper_cells, lower_cells), pairs, 1)
        at = (row + 2 * w) * states
        at = at if isinstance(w, int) else pl.multiple_of(at, 2 * states)
        into[pl.ds(at, states), :] = jnp.where(low_half, lower_cells, mixed)
        into[pl.ds(at + states, states), :] = jnp.where(low_half, mixed, upper_cells)

    def inner_found(w, found):
        for a in range(1, edge - 1):
            store_pair(xs_ref, a * group, w, found[a], found[edge - 1 + a])
        store_pair(ends_ref, 0, w, found[edge - 1], found[edge - 1])

    def outer_found(w, found):
        store_pair(ends_ref, group, w, found[0], found[slabs])

    def gather_inner():
        @pl.when(me >= 0)
        def split():
            gather(2 * block, tuple(range(1, slabs)), inner_found, 1)

    def gather_outer():
        gather(0, (0, slabs), outer_found, 1)

    def bcast(row):
        return projf_ref[pl.ds(row, states, stride=0), :]

    def partial_rows(source, at, proj_at, accs):
        values = jnp.dot(
            source[pl.ds(at, group * states), :].astype(BF16), spread_ref[...],
            preferred_element_type=F32,
        )
        accs = list(accs)
        for j in range(group):
            value = values[j * states:(j + 1) * states]
            for k in range(nproj):
                accs[k] = accs[k] + bcast(proj_at + j * nproj + k) * value
        return tuple(accs)

    def partial_inner():
        accs = partial_rows(ends_ref, 0, width * nproj, empty)
        for a in range(1, edge - 1):
            accs = partial_rows(xs_ref, a * group * states, a * group * nproj, accs)
        return accs

    def partial_outer(accs):
        return partial_rows(ends_ref, group * states, (width + group) * nproj, accs)

    slot_ids = lax.broadcasted_iota(jnp.int32, (4 * atoms, entries), 0)
    chosen_atom = jnp.where(slot_ids == eatom_ref[...], 1.0, 0.0).astype(BF16)
    chosen_send = jnp.concatenate(
        [chosen_atom[:2 * atoms], chosen_atom[atoms:3 * atoms], chosen_atom[2 * atoms:3 * atoms],
         chosen_atom[:atoms]], axis=0,
    )
    back = (((1,), (1,)), ((), ()))
    empty = tuple(jnp.zeros((states, entries), F32) for _ in range(nproj))
    low_atoms = lax.broadcasted_iota(jnp.int32, (1, 2 * atoms), 1) < atoms

    def send_atoms(step, accs):
        grouped = lax.dot_general(
            halves(jnp.concatenate(accs, axis=0), 1),
            jnp.concatenate([chosen_send, chosen_send], axis=1),
            back, preferred_element_type=F32,
        )
        for g in range(3):
            grouped_ref[step, g] = grouped[:, 2 * g * atoms:2 * (g + 1) * atoms]
        at = 4 + 6 * step
        return [
            send(grouped_ref.at[step, 1], left_ref.at[step], sems, at, ahead),
            send(grouped_ref.at[step, 0], right_ref.at[step], sems, at + 1, behind),
            send(grouped_ref.at[step, 2], far_ref.at[step, 0], sems, at + 2, ahead2),
            send(grouped_ref.at[step, 2], far_ref.at[step, 1], sems, at + 3, behind2),
        ]

    def cell_terms():
        early, late = ends_ref[:size, :], ends_ref[size:, :]
        xs_ref[:size, :] = jnp.where(low_half, late, early)
        xs_ref[last * states:, :] = jnp.where(low_half, early, late)
        kmat = kmat_ref[...]
        for s in range(0, states, 2):
            pair = jnp.concatenate(
                [xs_ref[pl.ds(s, width, stride=states), :],
                 xs_ref[pl.ds(s + 1, width, stride=states), :]], axis=1,
            ).astype(BF16)
            out = jnp.dot(kmat, pair, preferred_element_type=F32)
            ct_ref[pl.ds(s, width, stride=states), :] = out[:, :cells] * scale
            ct_ref[pl.ds(s + 1, width, stride=states), :] = out[:, cells:] * scale

    def entry_terms(step):
        right = pltpu.roll(right_ref[step], atoms, 1)
        coef = (
            grouped_ref[step, 0] + left_ref[step]
            + jnp.where(low_atoms, far_ref[step, 0], right),
            grouped_ref[step, 2] + right + pltpu.roll(far_ref[step, 1], atoms, 1),
        )
        rows = []
        for c in range(2):
            parts = []
            for k in range(nproj):
                acc = jnp.zeros((states, 2 * atoms), F32)
                for l in range(nproj):
                    at = k * nproj + l
                    acc = acc + (
                        couple_ref[c, at:at + 1, :] * coef[c][l * states:(l + 1) * states, :]
                    )
                parts.append(acc)
            rows.append(halves(jnp.concatenate(parts, axis=0), 1))
        half_atoms = [chosen_atom[:2 * atoms]] * 2 + [chosen_atom[2 * atoms:]] * 2
        terms = jnp.dot(
            jnp.concatenate(rows, axis=1), jnp.concatenate(half_atoms, axis=0),
            preferred_element_type=F32,
        )
        return [terms[k * states:(k + 1) * states] for k in range(nproj)]

    per = tiles * 2 * states
    size = group * states

    def terms_at(a):
        return ct_ref[a * size:(a + 1) * size, :]

    def node_rows(proj_at, before, terms):
        parts = []
        for j in range(group):
            row = proj_at + j * nproj
            total = bcast(row) * terms[0]
            for k in range(1, nproj):
                total = total + bcast(row + k) * terms[k]
            parts.append(total)
        twice = jnp.concatenate([spread_ref[...], spread_ref[...]], axis=1)
        value = before + lax.dot_general(
            halves(jnp.concatenate(parts, axis=0), 1), twice, back, preferred_element_type=F32
        )
        found = []
        for w in range(wraps):
            even = value[2 * w * states:(2 * w + 1) * states]
            odd = value[(2 * w + 1) * states:(2 * w + 2) * states]
            mixed = pltpu.roll(jnp.where(low_half, odd, even), pairs, 1)
            found.append((jnp.where(low_half, even, mixed), jnp.where(low_half, mixed, odd)))
        return found

    def fill(into, w, value):
        both = halves(value, 0)
        for t in range(tiles):
            rows = into + t * 2 * states
            masked_ref[rows:rows + 2 * states, w * cells:(w + 1) * cells] = (
                both * hot_ref[t * 2 * states:(t + 1) * 2 * states, w * cells:(w + 1) * cells]
            )

    def fill_late(terms):
        before = jnp.where(low_half, terms_at(0), terms_at(edge - 1))
        found = node_rows((width + group) * nproj, before, terms)
        for w, (one, two) in enumerate(found):
            fill(0, w, one)
            fill(per, w, two)

    def fill_early(terms):
        before = jnp.where(low_half, terms_at(edge - 1), terms_at(0))
        for w, (one, two) in enumerate(node_rows(width * nproj, before, terms)):
            fill(2 * per, w, one + two)

    def fill_inner(a, terms, one_at, two_at):
        found = node_rows(a * group * nproj, terms_at(a), terms)
        for w, (one, two) in enumerate(found):
            fill(one_at * per, w, one)
            fill(two_at * per, w, two)

    def scatter(into, number):
        into = into if isinstance(into, int) else pl.multiple_of(into, per)
        out = jnp.dot(
            masked_ref[pl.ds(into, number * per), :], oht_ref[...], preferred_element_type=F32
        )
        return [
            [joined(out[n * per:(n + 1) * per], t) for t in range(tiles)] for n in range(number)
        ]

    def joined(value, t):
        return value[t * 2 * states:t * 2 * states + states] + (
            value[t * 2 * states + states:(t + 1) * 2 * states]
        )

    def scatter_outer(step, terms):
        fill_late(terms)
        head, tail = scatter(0, 2)
        for t in range(tiles):
            head_ref[step, :, t * WIDE:(t + 1) * WIDE] = head[t]
            tail_ref[step, :, t * WIDE:(t + 1) * WIDE] = tail[t]

    def scatter_rest(terms, finish):
        fill_early(terms)
        for a in range(1, edge):
            if a < edge - 1:
                fill_inner(a, terms, 2 * a + 1, 2 * a + 2)
            if a == 1:
                (out,) = scatter(2 * per, 1)
                finish(0, edge - 1, out)
            else:
                one, two = scatter((2 * a - 1) * per, 2)
                finish(a - 1, a - 1, one)
                finish(a - 1, a + edge - 2, two)

    def pot_row(layer, t, half):
        row = layer * rows128 + t * 2 + half
        return potf_ref[pl.ds(row, 1), :]

    def scaled(layer, t, summed, field):
        pot = jnp.concatenate([pot_row(layer, t, 0), pot_row(layer, t, 1)], axis=1)
        return (summed + pot * field) * (1.0 / HALFWIDTH)

    def lanes(layer, t):
        at = layer * face + t * WIDE
        return pl.ds(at if isinstance(layer, int) else pl.multiple_of(at, WIDE), WIDE)

    def first_layer(layer, summed, field):
        blocks = []
        for t in range(tiles):
            value = scaled(layer, t, summed(t), field(t)).astype(BF16).astype(F32)
            first_ref[:, lanes(layer, t)] = value
            blocks.append(value)
        put(layer, blocks)

    def last_layer(layer, summed):
        for t in range(tiles):
            value = scaled(layer, t, summed(t), first_ref[:, lanes(layer, t)])
            at = lanes(layer, t)
            out_ref[:, at] = (2.0 * value - psi_ref[:, at].astype(F32)).astype(BF16)

    def edge_sum(one_ref, two_ref):
        return lambda t: (
            one_ref[:, t * WIDE:(t + 1) * WIDE] + two_ref[:, t * WIDE:(t + 1) * WIDE]
        )

    gather_inner()
    accs = partial_inner()
    for copy in gaps:
        copy.wait()
    couple_ref[0] = jnp.where(low_atoms, coups_ref[0], coups_ref[1])
    couple_ref[1] = coups_ref[2]
    put_psi(slabs, ghost_ref, 0)
    gather_outer()
    copies = send_atoms(0, partial_outer(accs))
    verdict.wait()
    potf_ref[slabs * rows128:slabs * rows128 + potg_ref.shape[0], :] = (
        potg_ref[...].astype(F32) - CENTER
    )
    cell_terms()
    for copy in copies:
        copy.wait()
    terms = entry_terms(0)
    scatter_outer(0, terms)
    copies = [
        send(tail_ref.at[0], low_ref.at[0], sems, 8, ahead),
        send(head_ref.at[0], high_ref, sems, 9, behind),
    ]

    def first_done(layer, summed):
        first_layer(layer, summed, lambda t: psi_ref[:, lanes(layer, t)].astype(F32))

    scatter_rest(terms, lambda a, layer, out: first_done(layer, lambda t: out[t]))
    gather_inner()
    accs = partial_inner()
    for copy in copies:
        copy.wait()
    first_done(0, edge_sum(head_ref.at[0], low_ref.at[0]))
    first_layer(
        slabs, edge_sum(tail_ref.at[0], high_ref),
        lambda t: ghost_ref[:, t * WIDE:(t + 1) * WIDE].astype(F32),
    )
    gather_outer()
    copies = send_atoms(1, partial_outer(accs))
    mated = [send(first_ref.at[:, span(mate_part, part)], mated_ref, sems, 20, partner)]
    cell_terms()
    for copy in copies:
        copy.wait()
    terms = entry_terms(1)
    scatter_outer(1, terms)
    tails = [
        send(tail_ref.at[1], low_ref.at[1], sems, 14, ahead),
        send(tail_ref.at[1, :, span(mate_part, part)], matel_ref, sems, 16, ahead_mate),
        send(head_ref.at[1, :, span(mate_part, part)], mateh_ref, sems, 19, partner),
    ]
    half = edge - 1

    def swap(n):
        if n == 0:
            at, size = half * face + mate_part, part
        else:
            at, size = jnp.where(band == 0, n + half, n) * face, face
        return pltpu.make_async_remote_copy(
            src_ref=out_ref.at[:, span(at, size)],
            dst_ref=other_ref.at[:, span(n * face, size)],
            send_sem=sems.at[0, 21 + n], recv_sem=sems.at[1, 21 + n],
            device_id=partner, device_id_type=MESH_ID,
        )

    def sent(a):
        return jnp.where(band == 0, a + half, a)

    def kept(a):
        return jnp.where(band == 0, a, a + half)

    def finish(first, number, rows, layer_of):
        found = scatter(rows * per, number)
        for n in range(number):
            last_layer(layer_of(first + n), lambda t: found[n][t])

    upper, lower = edge + 1, 3
    sent_rows = jnp.where(band == 0, upper, lower)
    kept_rows = jnp.where(band == 0, lower, upper)
    early_half = (half - 1) // 2
    fill_early(terms)
    for a in range(1, half):
        fill_inner(a, terms, lower + a - 1, upper + a - 1)
        if a == early_half:
            finish(0, 1, 2, lambda a: half)
            finish(1, early_half, sent_rows, sent)
    for n in range(early_half + 1):
        swap(n).start()
    finish(early_half + 1, half - 1 - early_half, sent_rows + early_half, sent)
    for n in range(early_half + 1, half):
        swap(n).start()
    finish(1, half - 1, kept_rows, kept)

    def gram(own, other):
        both = jnp.concatenate(
            [jnp.where(band == 0, own, other), jnp.where(band == 0, other, own)], axis=0
        ).astype(BF16)
        return lax.dot_general(both, both, back, preferred_element_type=F32)

    swap(0).wait()
    total = gram(
        out_ref[:, span(half * face + own_part, part)].astype(F32), other_ref[:, :part].astype(F32)
    )
    for n in range(1, half):
        swap(n).wait()
        total = total + gram(
            out_ref[:, span(jnp.where(band == 0, n, n + half) * face, face)].astype(F32),
            other_ref[:, n * face:(n + 1) * face].astype(F32),
        )
    for copy in tails + mated:
        copy.wait()
    last_layer(0, edge_sum(head_ref.at[1], low_ref.at[1]))
    blocks = []
    for t in range(part // 128):
        at = slice(t * 128, (t + 1) * 128)
        pot = potf_ref[pl.ds(band * (part // 128) + t, 1), :]
        value = (mateh_ref[:, at] + matel_ref[:, at] + pot * mated_ref[:, at]) * (1.0 / HALFWIDTH)
        blocks.append((2.0 * value - mate_ref[:, at].astype(F32)).astype(BF16).astype(F32))
    total = total + gram(
        out_ref[:, span(own_part, part)].astype(F32), jnp.concatenate(blocks, axis=1)
    )
    size = bands * states
    lump = size * size // 128
    pieces = size // lump
    slots_ref[me] = jnp.concatenate(
        [total[r * lump:(r + 1) * lump] for r in range(pieces)], axis=1
    )

    def push(steps, carry):
        send(slots_ref.at[me], slots_ref.at[me], sems, 17, peer(steps))
        return carry

    lax.fori_loop(0, devices * bands - 1, push, 0)
    rest = pl.ds(0, devices * bands - 1)
    pltpu.make_async_remote_copy(
        src_ref=slots_ref.at[rest], dst_ref=slots_ref.at[rest], send_sem=sems.at[0, 17],
        recv_sem=sems.at[1, 17], device_id=partner, device_id_type=MESH_ID,
    ).wait()
    total = jnp.sum(slots_ref[...], axis=0) * (1.0 / (devices * count))
    corr_ref[...] = jnp.concatenate(
        [total[:, r * size:(r + 1) * size] for r in range(pieces)], axis=0
    )


def general(
    psi,
    cell_nodes,
    cell_scale,
    cell_matrix,
    node_potential,
    proj_values,
    entry_cell,
    entry_atom,
    coupling,
):
    states, node_count = psi.shape
    width, cells = cell_nodes.shape
    atoms, nproj, _ = coupling.shape
    entries = entry_atom.shape[0]
    full = node_count + FACEP
    chunks = full // FACEP
    layers = FACEP // WIDE
    groups = width // GROUP
    span = GROUP * cells

    table = cell_nodes.reshape(groups, GROUP, cells)
    owner = table // FACEP
    ids = jnp.arange(chunks, dtype=jnp.int32)
    flags = jnp.max(
        (owner[:, None] == ids[None, :, None, None]).astype(jnp.int32), axis=(2, 3)
    )
    rank = jnp.sum(flags[:, None, :] * (ids[None, :] < ids[:, None]), axis=2)
    places = jnp.arange(chunks + 1, dtype=jnp.int32)
    used = flags[:, :, None] * (rank[:, :, None] == places)
    listed = chunks + jnp.sum(used * (ids[None, :, None] - chunks), axis=1)
    listed = jnp.concatenate(
        [listed, jnp.full((groups, 1), chunks, jnp.int32), jnp.sum(flags, axis=1, keepdims=True)],
        axis=1,
    )
    sched = listed.astype(jnp.int32).reshape(groups * (chunks + 3))
    scale_row = cell_scale.reshape(1, cells)
    ecell = entry_cell.reshape(1, entries)
    eatom = entry_atom.reshape(1, entries)
    coup = coupling.transpose(1, 2, 0).reshape(nproj * nproj, atoms)
    potential = node_potential.astype(F32).reshape(1, node_count) - CENTER

    vmem = pl.BlockSpec(memory_space=pltpu.VMEM)
    smem = pl.BlockSpec(memory_space=pltpu.SMEM)

    padded = (layers * states + 15) // 16 * 16
    gather = pl.pallas_call(
        gather_kernel,
        out_shape=jax.ShapeDtypeStruct((width * states, cells), F32),
        in_specs=[smem] + [vmem] * 2,
        out_specs=vmem,
        scratch_shapes=[
            pltpu.VMEM((chunks + 1, padded, WIDE), BF16),
            pltpu.VMEM((WIDE, span), BF16),
        ],
        name="gather_cells",
    )
    scatter = pl.pallas_call(
        scatter_kernel,
        out_shape=jax.ShapeDtypeStruct((states, full), F32),
        in_specs=[smem] + [vmem] * 7,
        out_specs=vmem,
        scratch_shapes=[
            pltpu.VMEM((WIDE, span), BF16),
            pltpu.VMEM((width * states, entries), F32),
            pltpu.VMEM((width * states, cells), F32),
            pltpu.VMEM((2 * layers * 2 * states, span), BF16),
            pltpu.VMEM((chunks + 1, layers * 2 * states, WIDE), F32),
        ],
        name="scatter_nodes",
    )

    def remote(kernel, outs, n_in, scratch, copies, ident):
        return pl.pallas_call(
            kernel,
            out_shape=tuple(jax.ShapeDtypeStruct(*out) for out in outs),
            in_specs=[vmem] * n_in,
            out_specs=(vmem,) * len(outs),
            scratch_shapes=[pltpu.VMEM(*one) for one in scratch]
            + [pltpu.SemaphoreType.DMA((2, copies))],
            compiler_params=pltpu.CompilerParams(collective_id=ident, has_side_effects=True),
            name=kernel.__name__,
        )

    pair = (nproj * states, atoms)

    def assemble(extended, ident):
        values = gather(sched, table, extended)
        cell_terms, coef = remote(
            atoms_kernel, [((width * states, cells), F32), ((3,) + pair, F32)], 6,
            [((width * states, entries), F32), ((3,) + pair, F32)] + [((2,) + pair, F32)] * 3,
            4, ident,
        )(values, cell_matrix, scale_row, proj_values, ecell, eatom)
        return scatter(sched, table, cell_terms, coef, coup_all, proj_values, ecell, eatom)

    psi_ext, pot_ext, coup_all = remote(
        start_kernel,
        [((states, full), BF16), ((1, full), F32), ((3, nproj * nproj, atoms), F32)],
        3, [], 4, 1,
    )(psi, potential, coup)
    face = (states, FACEP)
    (first,) = remote(first_kernel, [((states, full), BF16)], 3, [(face, F32), (face, F32)], 2, 3)(
        assemble(psi_ext, 2), psi_ext, pot_ext
    )
    bands, devices = lax.axis_size("band"), lax.axis_size("mesh")
    square = (bands * states, bands * states)
    filtered, correlation = remote(
        last_kernel,
        [((states, node_count), BF16), (square, F32)],
        4,
        [(face, F32), ((states, node_count), BF16), ((devices,) + square, F32)],
        4, 5,
    )(assemble(first, 4), first, psi, potential)
    return (filtered, correlation)


def hand_over(filtered_ref, correlation_ref, out_ref, corr_ref, sems):
    copies = [
        pltpu.make_async_copy(filtered_ref, out_ref, sems.at[0]),
        pltpu.make_async_copy(correlation_ref, corr_ref, sems.at[1]),
    ]
    for copy in copies:
        copy.start()
    for copy in copies:
        copy.wait()


def bricks(states, node_count, width, cells, bands):
    edge = round(width ** (1.0 / 3.0))
    return (
        edge ** 3 == width
        and (edge - 1) * 2 * FACEP == node_count
        and edge % 2 == 0
        and cells == 128
        and FACEP % WIDE == 0
        and FACEP % 256 == 0
        and states == 8
        and bands == 2
        and edge * edge % 6 == 0
    )


def local(
    psi,
    cell_nodes,
    cell_scale,
    cell_matrix,
    node_potential,
    proj_values,
    entry_cell,
    entry_atom,
    coupling,
):
    states, node_count = psi.shape
    width, cells = cell_nodes.shape
    atoms, nproj, _ = coupling.shape
    entries = entry_atom.shape[0]
    bands, devices = lax.axis_size("band"), lax.axis_size("mesh")
    operands = (
        psi, cell_nodes, cell_scale, cell_matrix, node_potential, proj_values, entry_cell,
        entry_atom, coupling,
    )
    if not bricks(states, node_count, width, cells, bands):
        return general(*operands)
    edge = round(width ** (1.0 / 3.0))
    wraps = edge * edge // 2
    layers = node_count // FACEP + 1
    tiles = FACEP // WIDE
    block = (tiles + 1) * states
    per = tiles * 2 * states
    rows = node_count // 128
    ghost_rows = (FACEP // 128 + 15) // 16 * 16
    size = bands * states
    vmem = pl.BlockSpec(memory_space=pltpu.VMEM)
    anywhere = pl.BlockSpec(memory_space=pl.ANY)
    face = (states, FACEP)
    duo = (nproj * states, 2 * atoms)
    filtered, correlation, wrong = pl.pallas_call(
        fused_kernel,
        out_shape=(
            jax.ShapeDtypeStruct((states, node_count), BF16),
            jax.ShapeDtypeStruct((size, size), F32),
            jax.ShapeDtypeStruct((1, 128), F32),
        ),
        in_specs=[anywhere] * 9,
        out_specs=(vmem, vmem, anywhere),
        scratch_shapes=[
            pltpu.VMEM((1, 128), F32),
            pltpu.VMEM(psi.shape, BF16),
            pltpu.VMEM(cell_nodes.shape, jnp.int32),
            pltpu.VMEM(cell_matrix.shape, BF16),
            pltpu.VMEM((rows, 128), BF16),
            pltpu.VMEM(proj_values.shape, BF16),
            pltpu.VMEM((1, cells), F32),
            pltpu.VMEM((1, entries), jnp.int32),
            pltpu.VMEM((1, entries), jnp.int32),
            pltpu.VMEM((nproj * nproj, atoms), F32),
            pltpu.VMEM((WIDE, wraps * cells), BF16),
            pltpu.VMEM((wraps * cells, WIDE), BF16),
            pltpu.VMEM(((wraps + 7) // 8 * 8, cells), jnp.int32),
            pltpu.VMEM(((2 * wraps + 7) // 8 * 8, cells), F32),
            pltpu.VMEM((width * states, cells), F32),
            pltpu.VMEM((width * states, cells), F32),
            pltpu.VMEM((4 * wraps * states, cells), F32),
            pltpu.VMEM((layers * block, WIDE), BF16),
            pltpu.VMEM((layers * per, wraps * cells), BF16),
            pltpu.VMEM((states, layers * FACEP), F32),
            pltpu.VMEM((rows + ghost_rows, 128), F32),
            pltpu.VMEM((2,) + face, F32),
            pltpu.VMEM((2,) + face, F32),
            pltpu.VMEM((2,) + face, F32),
            pltpu.VMEM(face, F32),
            pltpu.VMEM((2, 3) + duo, F32),
            pltpu.VMEM((2,) + duo, F32),
            pltpu.VMEM((2,) + duo, F32),
            pltpu.VMEM((2, 2) + duo, F32),
            pltpu.VMEM(face, BF16),
            pltpu.VMEM((ghost_rows, 128), BF16),
            pltpu.VMEM((3, nproj * nproj, 2 * atoms), F32),
            pltpu.VMEM((cells, entries), BF16),
            pltpu.VMEM((states, node_count // 2), BF16),
            pltpu.VMEM((devices * bands, size * size // 128, 128), F32),
            pltpu.VMEM((per, wraps * cells), BF16),
            pltpu.VMEM((2, nproj * nproj, 2 * atoms), F32),
            pltpu.VMEM((states, FACEP // 2), BF16),
            pltpu.VMEM((states, FACEP // 2), F32),
            pltpu.VMEM((states, FACEP // 2), F32),
            pltpu.VMEM((states, FACEP // 2), F32),
            pltpu.VMEM(((width + 4 * wraps) * nproj, entries), F32),
            pltpu.SemaphoreType.DMA((10,)),
            pltpu.SemaphoreType.DMA((2, 26)),
        ],
        compiler_params=pltpu.CompilerParams(collective_id=0, has_side_effects=True),
        name="fused_steps",
    )(
        psi, cell_nodes, cell_scale.reshape(1, cells), cell_matrix,
        node_potential.reshape(rows, 128), proj_values, entry_cell.reshape(1, entries),
        entry_atom.reshape(1, entries),
        coupling.transpose(1, 2, 0).reshape(nproj * nproj, atoms),
    )
    results = lax.cond(
        wrong[0, 0] > 0.0,
        lambda: general(*operands),
        lambda: (filtered, correlation),
    )
    return pl.pallas_call(
        hand_over,
        out_shape=tuple(jax.ShapeDtypeStruct(one.shape, one.dtype) for one in results),
        in_specs=[anywhere] * 2,
        out_specs=(anywhere,) * 2,
        scratch_shapes=[pltpu.SemaphoreType.DMA((2,))],
        name="hand_over",
    )(*results)


def solution(mesh):
    return jax.shard_map(
        local,
        mesh=mesh,
        in_specs=(
            P("band", "mesh"),
            P(),
            P("mesh"),
            P(),
            P("mesh"),
            P(None, None, "mesh"),
            P("mesh"),
            P("mesh"),
            P("mesh", None, None),
        ),
        out_specs=(P("band", "mesh"), P()),
        check_vma=False,
    )
```
